32 devices in a mesh: seq: 8 (over z, y), slide: 4 (over x, core).
Axes of the slice: x: 2, y: 2, z: 4, core: 2. Of those that a mesh axis runs over, the one named last changes fastest.
Arguments:
- tiles: bfloat16 [40960, 768], P(('seq', 'slide')), may hold values from -6 to 6
- dest_table: int32 [40960], P(('seq', 'slide')), may hold values from -1 to 16383, as said below
- owner_row: int32 [4, 4096], P('slide', 'seq'), may hold values from 0 to 40959, as said below
- w_qkv: bfloat16 [768, 2304], replicated, may hold values from -6 to 6, as said below
- w_out: bfloat16 [768, 768], replicated, may hold values from -0.21875 to 0.21875
- gain_attn: float32 [768], replicated, may hold values from 0.1 to 1.9
- gain_out: float32 [768], replicated, may hold values from 0.1 to 1.9
Outputs:
- predicted: bfloat16 [40960, 768], P(('seq', 'slide'))
The draws below stay inside these ranges and needn't reach their ends.
Inputs may be any that keep to these rules, and one draw needn't show every extreme that they name: `dest_table`: for each tile row its student position g * 4096 + p, or -1 for a masked row; every position is named by exactly one row. The rows of one device that go to one student device (the positions of group g with the same p // 512) number 0 or exactly 32, and each student device receives rows from exactly half of all devices. `owner_row`: the tile row held at each student position: the inverse of dest_table. `w_qkv`: heads side by side in each projection.
All inputs are finite; a program needn't handle non-finite values.
Results may differ from the reference program's by a relative error of at most 0.0045.
Values may be sent and summed in bfloat16 or wider, within the bound.
No kernel may reach another device: no remote copies, remote signals or barrier semaphores. Data moves between devices by JAX's collectives and lax.ppermute only.
A program may use at most 128 MiB of HBM per device.

```python
import jax
import jax.numpy as jnp
from jax import lax

D = 768
HEADS = 12
HDIM = 64
SEG = 2048
TOK_DEV = 1280
VIS_DEV = 512
CAP = 32
VLEN = 4096
GROUPS = 4
ROWS = 40960
N_SEQ = 8
N_SLIDE = 4


def route_tables(key):
    devices = N_SEQ * N_SLIDE
    half = devices // 2
    base_key = jax.random.fold_in(key, 7)
    heat_key, noise_key, order_key = jax.random.split(base_key, 3)
    heat = jax.random.randint(heat_key, (devices,), 0, 4)
    noise = jax.random.randint(noise_key, (devices, devices), 0, 65536)
    scores = (noise + heat[None, :] * 40000) * devices + jnp.arange(devices, dtype=jnp.int32)[None, :]
    _, chosen = lax.top_k(scores, half)
    picked = jnp.zeros((devices, devices), jnp.int32).at[jnp.arange(devices)[:, None], chosen].set(1)
    blocks = jnp.cumsum(picked, axis=1) - 1
    targets = jnp.arange(devices, dtype=jnp.int32)
    group = targets % N_SLIDE
    seq_part = targets // N_SLIDE
    inside = blocks.T[:, :, None] * CAP + jnp.arange(CAP, dtype=jnp.int32)[None, None, :]
    flat = group[None, :, None] * VLEN + seq_part[None, :, None] * VIS_DEV + inside
    entries = jnp.where(picked.T[:, :, None] == 1, flat, -1).reshape(devices, devices * CAP)
    order_keys = jax.random.split(order_key, devices)
    orders = jax.vmap(lambda single: jax.random.permutation(single, TOK_DEV))(order_keys)
    table = jnp.full((devices, TOK_DEV), -1, jnp.int32)
    table = table.at[jnp.arange(devices)[:, None], orders[:, :devices * CAP]].set(entries.astype(jnp.int32))
    return table.reshape(devices * TOK_DEV)


def draw_dest_table(key, part):
    return route_tables(key)


def draw_owner_row(key, part):
    table = route_tables(key)
    rows = jnp.arange(table.shape[0], dtype=jnp.int32)
    place = jnp.where(table >= 0, table, GROUPS * VLEN)
    owners = jnp.zeros((GROUPS * VLEN,), jnp.int32).at[place].set(rows, mode='drop')
    return owners.reshape(GROUPS, VLEN)


def draw_w_qkv(key, part):
    base = jnp.clip(jax.random.normal(key, (D, 3 * D), jnp.float32), -6.0, 6.0) * D ** (-0.5)
    return base.astype(jnp.bfloat16)


def block_levels(stream_key, extent, cuts, least, top_value):
    def one(position, blocks):
        heights = jax.random.uniform(jax.random.fold_in(jax.random.fold_in(stream_key, 6), position), (blocks,), jnp.float32, least / len(cuts), top_value / len(cuts))
        return jnp.repeat(jnp.exp(heights), extent[position] // blocks).reshape((-1,) + (1,) * (len(extent) - position - 1))

    level = one(*cuts[0])
    for cut in cuts[1:]:
        level = level * one(*cut)
    return level


def scatter_about(own_key, dims, width, limit, cuts=(), kind=jnp.bfloat16):
    array = jax.random.normal(own_key, dims, jnp.float32) * width
    if len(cuts) > 0:
        array = block_levels(own_key, dims, cuts, -0.22, 0.18) * array
    return jnp.clip(array, min=-limit, max=limit).astype(kind)


def setup_inputs(seed: int = 0) -> dict:
    key_of = jax.random.split(jax.random.key(seed), 8)
    tiles = scatter_about(key_of[0], (ROWS, D), 1.0, 6.0, ((0, 32),))
    dest_table = draw_dest_table(jax.random.fold_in(key_of[7], 71), 0)
    owner_row = draw_owner_row(jax.random.fold_in(key_of[7], 71), 0)
    w_qkv = draw_w_qkv(jax.random.fold_in(key_of[7], 71), 0)
    w_out = scatter_about(key_of[4], (D, D), D ** -0.5, 0.21875)
    gain_attn = jnp.clip(1.0 + 0.18 * jax.random.normal(key_of[5], (D,), jnp.float32), 0.1, 1.9)
    gain_out = jnp.clip(1.0 + 0.18 * jax.random.normal(key_of[6], (D,), jnp.float32), 0.1, 1.9)
    return dict(tiles=tiles, dest_table=dest_table, owner_row=owner_row, w_qkv=w_qkv, w_out=w_out, gain_attn=gain_attn, gain_out=gain_out)


EPS = 1e-05

def layer_norm(inputs, gain):
    average = lax.optimization_barrier(jnp.mean(inputs, axis=-1, keepdims=True))
    centred = inputs - average
    spread = lax.optimization_barrier(jnp.mean(centred * centred, axis=-1, keepdims=True))
    return centred * lax.rsqrt(spread + EPS) * gain

def attend(triple):
    queries, keys, values = triple
    scores = jnp.einsum('qd,kd->qk', queries.astype(jnp.float32), keys.astype(jnp.float32))
    peak = lax.optimization_barrier(jnp.max(scores, axis=-1, keepdims=True))
    weights = jnp.exp(scores - peak)
    total = lax.optimization_barrier(jnp.sum(weights, axis=-1, keepdims=True))
    rounded = lax.optimization_barrier(weights.astype(jnp.bfloat16))
    mixed = jnp.einsum('qk,kd->qd', rounded.astype(jnp.float32), values.astype(jnp.float32))
    return (mixed / total, peak[:, 0] + jnp.log(total[:, 0]))

def branch(queries, keys, values, span, stride):
    length = queries.shape[0]

    def arrange(block):
        shaped = block.reshape(length // span, span // stride, stride, HEADS, HDIM)
        return shaped.transpose(0, 2, 3, 1, 4).reshape(-1, span // stride, HDIM)
    mixed, log_total = lax.map(attend, (arrange(queries), arrange(keys), arrange(values)))
    mixed = mixed.reshape(length // span, stride, HEADS, span // stride, HDIM)
    mixed = mixed.transpose(0, 3, 1, 2, 4).reshape(length, HEADS, HDIM)
    log_total = log_total.reshape(length // span, stride, HEADS, span // stride)
    log_total = log_total.transpose(0, 3, 1, 2).reshape(length, HEADS)
    return (mixed, log_total)

def encode(rows, w_qkv, w_out, gain_attn, gain_out):
    length = rows.shape[0]
    normed = layer_norm(rows.astype(jnp.float32), gain_attn).astype(jnp.bfloat16)
    projected = jnp.dot(normed, w_qkv, preferred_element_type=jnp.float32)
    queries = (projected[:, :D] * HDIM ** (-0.5)).astype(jnp.bfloat16).reshape(length, HEADS, HDIM)
    keys = projected[:, D:2 * D].astype(jnp.bfloat16).reshape(length, HEADS, HDIM)
    values = projected[:, 2 * D:].astype(jnp.bfloat16).reshape(length, HEADS, HDIM)
    outputs = []
    totals = []
    for stride in (1, 2, 4):
        mixed, log_total = branch(queries, keys, values, SEG, stride)
        outputs.append(mixed)
        totals.append(log_total)
    far_mixed, far_total = branch(queries, keys, values, length, 8)
    far_rounded = lax.optimization_barrier(far_mixed.astype(jnp.bfloat16))
    outputs.append(far_rounded.astype(jnp.float32))
    totals.append(far_total)
    stacked = jnp.stack(outputs)
    stacked_totals = jnp.stack(totals)
    top = lax.optimization_barrier(jnp.max(stacked_totals, axis=0))
    scale = jnp.exp(stacked_totals - top)
    combined = lax.optimization_barrier(jnp.sum(scale[..., None] * stacked, axis=0)) / lax.optimization_barrier(jnp.sum(scale, axis=0))[..., None]
    attended = combined.reshape(length, D).astype(jnp.bfloat16)
    hidden = rows.astype(jnp.float32) + jnp.dot(attended, w_out, preferred_element_type=jnp.float32)
    return layer_norm(hidden, gain_out).astype(jnp.bfloat16)

def reference(tiles, dest_table, owner_row, w_qkv, w_out, gain_attn, gain_out):
    student_rows = tiles[owner_row]
    predictions = lax.map(lambda rows: encode(rows, w_qkv, w_out, gain_attn, gain_out), student_rows)
    flat = predictions.reshape(-1, D)
    valid = dest_table >= 0
    safe = jnp.where(valid, dest_table, 0).astype(jnp.int32)
    picked = flat[safe]
    return jnp.where(valid[:, None], picked, jnp.zeros_like(picked))
```

```python
import functools
import math

import jax
import jax.numpy as jnp
from jax import lax
from jax.experimental import pallas as pl
from jax.experimental.pallas import tpu as pltpu
from jax.sharding import Mesh
from jax.sharding import PartitionSpec as P

HEADS = 12
HDIM = 64
SEG = 2048
CLASSES = 8
EPS = 1e-05
VMEM = 60 << 20


def layer_norm(inputs, gain):
    average = jnp.mean(inputs, axis=-1, keepdims=True)
    centred = inputs - average
    spread = jnp.mean(centred * centred, axis=-1, keepdims=True)
    return centred * lax.rsqrt(spread + EPS) * gain


def one_hot(left, right):
    return jnp.where(left == right, 1.0, 0.0).astype(jnp.bfloat16)


def dot(left, right):
    return jnp.dot(left, right, preferred_element_type=jnp.float32)


def units_of(member, members):
    owned = HEADS * CLASSES // members
    units = [divmod(member * owned + i, CLASSES) for i in range(owned)]
    return units + units[-1:] * (owned % 2)


def heads_of(member, members):
    first = units_of(member, members)[0][0]
    return first, min(first + 1, HEADS - 1)


def pack_kernel(visible, capacity, dest_ref, tiles_ref, out_ref, slot_ref):
    slots, _ = out_ref.shape
    count = dest_ref.shape[1]
    devices = slots // capacity
    target = jnp.right_shift(dest_ref[...], visible.bit_length() - 1)
    lanes = 128
    before = one_hot_lt(lanes)
    offset = jnp.zeros((devices, 1), jnp.float32)
    pieces = []
    for start in range(0, count, lanes):
        here = target[:, start : start + lanes]
        device = lax.broadcasted_iota(jnp.int32, (devices, lanes), 0)
        chosen = jnp.where(device == here, 1.0, 0.0)
        rank = dot(chosen.astype(jnp.bfloat16), before) + offset
        placed = jnp.sum(chosen * rank, axis=0, keepdims=True).astype(jnp.int32)
        pieces.append(jnp.where(here >= 0, here * capacity + placed, -1))
        offset = offset + jnp.sum(chosen, axis=1, keepdims=True)
    slot = jnp.concatenate(pieces, axis=1)
    slot_ref[...] = slot
    step = math.gcd(slots, 256)
    for start in range(0, slots, step):
        wanted = lax.broadcasted_iota(jnp.int32, (step, count), 0) + start
        rows = dot(one_hot(wanted, slot), tiles_ref[...])
        out_ref[start : start + step, :] = rows.astype(jnp.bfloat16)


def one_hot_lt(size):
    row = lax.broadcasted_iota(jnp.int32, (size, size), 0)
    column = lax.broadcasted_iota(jnp.int32, (size, size), 1)
    return jnp.where(row < column, 1.0, 0.0).astype(jnp.bfloat16)


def project_kernel(members, slot_ref, arrived_ref, gain_ref, wq_ref, wkv_ref, rows_ref, send_ref, q_ref, kv_ref):
    visible, width = rows_ref.shape
    slots = arrived_ref.shape[0]
    part = visible // CLASSES
    chosen = one_hot(lax.broadcasted_iota(jnp.int32, (visible, slots), 1), slot_ref[...])
    rows = dot(chosen, arrived_ref[...])
    rows_ref[...] = rows.astype(jnp.bfloat16)
    normed = layer_norm(rows, gain_ref[...]).astype(jnp.bfloat16)
    q_ref[...] = (dot(normed, wq_ref[...]) * HDIM ** (-0.5)).astype(jnp.bfloat16)
    kv_ref[...] = dot(normed, wkv_ref[...]).astype(jnp.bfloat16)
    low = lax.broadcasted_iota(jnp.int32, (part, 2 * HDIM), 1) < HDIM
    for member in range(members):
        for place, head in enumerate(heads_of(member, members)):
            send_ref[member, place * visible : (place + 1) * visible, :] = kv_ref[
                :, head * 2 * HDIM : (head + 1) * 2 * HDIM
            ]
        units = units_of(member, members)
        for i in range(0, len(units), 2):
            pair = [
                q_ref[cls * part : (cls + 1) * part, head * 2 * HDIM : (head + 1) * 2 * HDIM]
                for head, cls in units[i : i + 2]
            ]
            at = 2 * visible + i // 2 * part
            send_ref[member, at : at + part, :] = jnp.where(low, pair[0], pair[1])


def attend_kernel(visible, place_ref, class_ref, block_ref, out_ref):
    members = block_ref.shape[0]
    part = visible // CLASSES
    group = SEG // visible
    segments = members // group
    step = pl.program_id(0)
    rows = group * part
    low = lax.broadcasted_iota(jnp.int32, (rows, 2 * HDIM), 1) < HDIM
    counts = [1 + (t % 2 == 0) + (t % 4 == 0) + (t % 8 == 0) for t in range(CLASSES)]

    def keys_of(segment, place, cls):
        at = pl.multiple_of(place * visible + cls * part, part)
        return jnp.concatenate(
            [block_ref[segment * group + i, pl.ds(at, part), :] for i in range(group)], axis=0
        )

    for segment in range(segments):
        halves = []
        for half in range(2):
            place = place_ref[2 * step + half]
            cls = class_ref[2 * step + half]
            at = pl.multiple_of(2 * visible + step * part, part)
            query = jnp.concatenate(
                [block_ref[segment * group + i, pl.ds(at, part), :] for i in range(group)], axis=0
            )
            if half == 1:
                query = jnp.concatenate([query[:, HDIM:], query[:, :HDIM]], axis=1)
            query = jnp.where(low, query, jnp.zeros_like(query))
            keys = [(keys_of(segment, place, jnp.bitwise_and(cls + t, CLASSES - 1)), counts[t]) for t in range(CLASSES)]
            keys += [(keys_of(other, place, cls), 1) for other in range(segments) if other != segment]
            scores = [
                lax.dot_general(query, key, (((1,), (1,)), ((), ())), preferred_element_type=jnp.float32)
                for key, _ in keys
            ]
            peak = jnp.max(functools.reduce(jnp.maximum, scores), axis=-1, keepdims=True)
            mixed = jnp.zeros((rows, 2 * HDIM), jnp.float32)
            for score, (key, count) in zip(scores, keys):
                weights = jnp.exp(score - (peak - math.log(count))).astype(jnp.bfloat16)
                mixed += dot(weights, jnp.where(low, jnp.ones_like(key), key))
            turned = jnp.concatenate([mixed[:, HDIM:], mixed[:, :HDIM]], axis=1)
            halves.append(turned / mixed if half == 0 else mixed / turned)
        both = jnp.where(low, halves[0], halves[1]).astype(jnp.bfloat16)
        for i in range(group):
            out_ref[segment * group + i, :, :] = both[i * part : (i + 1) * part, :]


def finish_kernel(slot_ref, mixed_ref, rows_ref, gain_ref, w_ref, out_ref, attended_ref):
    visible, _ = rows_ref.shape
    members = mixed_ref.shape[0]
    part = visible // CLASSES
    slots = out_ref.shape[0]
    where = {}
    for member in range(members):
        owned = HEADS * CLASSES // members
        for i, unit in enumerate(units_of(member, members)[:owned]):
            where[unit] = (member, i)
    for head in range(0, HEADS, 2):
        for cls in range(CLASSES):
            pair = []
            for one in (head, head + 1):
                member, i = where[(one, cls)]
                tile = mixed_ref[member, i // 2 * part : (i // 2 + 1) * part, :]
                pair.append(tile[:, i % 2 * HDIM : (i % 2 + 1) * HDIM])
            attended_ref[cls * part : (cls + 1) * part, head * HDIM : (head + 2) * HDIM] = (
                jnp.concatenate(pair, axis=1)
            )
    hidden = rows_ref[...].astype(jnp.float32) + dot(attended_ref[...], w_ref[...])
    answer = layer_norm(hidden, gain_ref[...]).astype(jnp.bfloat16)
    step = math.gcd(slots, 256)
    for start in range(0, slots, step):
        wanted = lax.broadcasted_iota(jnp.int32, (step, visible), 0) + start
        out_ref[start : start + step, :] = dot(one_hot(wanted, slot_ref[...]), answer).astype(
            jnp.bfloat16
        )


def unpack_kernel(slot_ref, back_ref, out_ref):
    count, _ = out_ref.shape
    slots = back_ref.shape[0]
    step = math.gcd(count, 256)
    for start in range(0, count, step):
        here = lax.broadcasted_iota(jnp.int32, (step, slots), 1)
        chosen = one_hot(slot_ref[start : start + step, :], here)
        out_ref[start : start + step, :] = dot(chosen, back_ref[...]).astype(jnp.bfloat16)


def call(kernel, outs, name, scratch=()):
    return pl.pallas_call(
        kernel,
        out_shape=outs,
        scratch_shapes=list(scratch),
        compiler_params=pltpu.CompilerParams(vmem_limit_bytes=VMEM),
        name=name,
    )


def on_device(tiles, dest_table, owner_row, w_qkv, w_out, gain_attn, gain_out):
    groups = lax.axis_size("group")
    axes = ("group", "high", "low")
    inside = ("high", "low")
    members = lax.axis_size(inside)
    devices = groups * members
    count, width = tiles.shape
    visible = owner_row.shape[1]
    capacity = 2 * visible // devices
    slots = devices * capacity
    part = visible // CLASSES
    owned = HEADS * CLASSES // members
    pairs = (owned + 1) // 2
    bf16 = jnp.bfloat16

    moves = [(s * groups + g, g * members + s) for g in range(groups) for s in range(members)]
    owners = lax.ppermute(owner_row.reshape(visible // 128, 128), axes, moves).reshape(visible)
    owners = owners.reshape(part, CLASSES).T.reshape(visible)

    outgoing, send_slot = call(
        functools.partial(pack_kernel, visible, capacity),
        (jax.ShapeDtypeStruct((slots, width), bf16), jax.ShapeDtypeStruct((1, count), jnp.int32)),
        "pack",
    )(dest_table.reshape(1, count), tiles)
    arrived = lax.all_to_all(
        outgoing.reshape(devices, capacity, width), axes, split_axis=0, concat_axis=0, tiled=True
    ).reshape(slots, width)

    source = owners // count
    same = source[:, None] == source[None, :]
    earlier = owners[None, :] < owners[:, None]
    placed = jnp.sum((same & earlier).astype(jnp.int32), axis=1)
    slot = source * capacity + placed

    heads = w_qkv.reshape(width, 3, HEADS, HDIM)
    wq = jnp.stack([heads[:, 0], heads[:, 0]], axis=2).reshape(width, 2 * width)
    wkv = jnp.stack([heads[:, 1], heads[:, 2]], axis=2).reshape(width, 2 * width)

    rows, send = call(
        functools.partial(project_kernel, members),
        (
            jax.ShapeDtypeStruct((visible, width), bf16),
            jax.ShapeDtypeStruct((members, 2 * visible + pairs * part, 2 * HDIM), bf16),
        ),
        "project",
        [pltpu.VMEM((visible, 2 * width), bf16), pltpu.VMEM((visible, 2 * width), bf16)],
    )(slot[:, None], arrived, gain_attn[None, :], wq, wkv)
    blocks = lax.all_to_all(send, inside, split_axis=0, concat_axis=0, tiled=True)

    first = lax.axis_index(inside) * owned
    units = jnp.minimum(first + jnp.arange(2 * pairs), HEADS * CLASSES - 1).astype(jnp.int32)
    mixed = pl.pallas_call(
        functools.partial(attend_kernel, visible),
        out_shape=jax.ShapeDtypeStruct((members, pairs * part, 2 * HDIM), bf16),
        grid_spec=pltpu.PrefetchScalarGridSpec(
            num_scalar_prefetch=2,
            grid=(pairs,),
            in_specs=[pl.BlockSpec(blocks.shape, lambda i, *_: (0, 0, 0), pipeline_mode=pl.Buffered(1))],
            out_specs=pl.BlockSpec((members, part, 2 * HDIM), lambda i, *_: (0, i, 0)),
        ),
        compiler_params=pltpu.CompilerParams(vmem_limit_bytes=VMEM),
        name="attend",
    )(jnp.minimum(units // CLASSES - first // CLASSES, 1), units % CLASSES, blocks)
    mixed = lax.all_to_all(mixed, inside, split_axis=0, concat_axis=0, tiled=True)

    answers = call(
        finish_kernel,
        jax.ShapeDtypeStruct((slots, width), bf16),
        "finish",
        [pltpu.VMEM((visible, width), bf16)],
    )(slot[None, :], mixed, rows, gain_out[None, :], w_out)
    back = lax.all_to_all(
        answers.reshape(devices, capacity, width), axes, split_axis=0, concat_axis=0, tiled=True
    ).reshape(slots, width)
    return call(unpack_kernel, jax.ShapeDtypeStruct((count, width), bf16), "unpack")(
        send_slot.reshape(count, 1), back
    )


def solution(mesh):
    n_seq, n_slide = mesh.shape["seq"], mesh.shape["slide"]
    split = Mesh(
        mesh.devices.reshape(n_slide, n_seq // n_slide, n_slide), ("group", "high", "low")
    )
    every = ("group", "high", "low")
    in_specs = (P(every, None), P(every), P("low", ("group", "high")), P(), P(), P(), P())
    return jax.shard_map(
        on_device, mesh=split, in_specs=in_specs, out_specs=P(every, None), check_vma=False
    )
```

```python
import functools
import math

import jax
import jax.numpy as jnp
from jax import lax
from jax.experimental import pallas as pl
from jax.experimental.pallas import tpu as pltpu
from jax.sharding import Mesh
from jax.sharding import PartitionSpec as P

HEADS = 12
HDIM = 64
SEG = 2048
CLASSES = 8
EPS = 1e-05
VMEM = 24 << 20


def layer_norm(inputs, gain):
    average = jnp.mean(inputs, axis=-1, keepdims=True)
    centred = inputs - average
    spread = jnp.mean(centred * centred, axis=-1, keepdims=True)
    return centred * lax.rsqrt(spread + EPS) * gain


def one_hot(left, right):
    return jnp.where(left == right, 1.0, 0.0).astype(jnp.bfloat16)


def dot(left, right):
    return jnp.dot(left, right, preferred_element_type=jnp.float32)


def parts_of(members):
    full = HEADS // members
    every = [(0, cls) for cls in range(CLASSES)]
    parts = [
        (i * members, (i + 1) * members, [([i * members + member], every) for member in range(members)])
        for i in range(full)
    ]
    first = full * members
    owned = (HEADS - first) * CLASSES // members
    if owned:
        dealt = []
        for member in range(members):
            units = [divmod(first * CLASSES + member * owned + i, CLASSES) for i in range(owned)]
            dealt.append((sorted({head for head, _ in units}), units))
        width = max(len(heads) for heads, _ in dealt)
        part = []
        for heads, units in dealt:
            units = [(heads.index(head), cls) for head, cls in units]
            part.append((heads + heads[-1:] * (width - len(heads)), units + units[-1:] * (owned % 2)))
        parts.append((first, HEADS, part))
    return parts


def swap(tile):
    return jnp.concatenate([tile[:, HDIM:], tile[:, :HDIM]], axis=1)


def dot_nt(left, right):
    return lax.dot_general(left, right, (((1,), (1,)), ((), ())), preferred_element_type=jnp.float32)


def pack_kernel(visible, capacity, dest_ref, tiles_hbm, out_ref, slot_ref, tiles_ref, sem):
    fetch = pltpu.make_async_copy(tiles_hbm, tiles_ref, sem)
    fetch.start()
    slots, _ = out_ref.shape
    count = dest_ref.shape[1]
    devices = slots // capacity
    target = jnp.right_shift(dest_ref[...], visible.bit_length() - 1)
    lanes = 128
    before = one_hot_lt(lanes)
    offset = jnp.zeros((devices, 1), jnp.float32)
    pieces = []
    for start in range(0, count, lanes):
        here = target[:, start : start + lanes]
        device = lax.broadcasted_iota(jnp.int32, (devices, lanes), 0)
        chosen = jnp.where(device == here, 1.0, 0.0)
        rank = dot(chosen.astype(jnp.bfloat16), before) + offset
        placed = jnp.sum(chosen * rank, axis=0, keepdims=True).astype(jnp.int32)
        pieces.append(jnp.where(here >= 0, here * capacity + placed, -1))
        offset = offset + jnp.sum(chosen, axis=1, keepdims=True)
    slot = jnp.concatenate(pieces, axis=1)
    slot_ref[...] = slot
    fetch.wait()
    step = math.gcd(slots, 256)
    for start in range(0, slots, step):
        wanted = lax.broadcasted_iota(jnp.int32, (step, count), 0) + start
        rows = dot(one_hot(wanted, slot), tiles_ref[...])
        out_ref[start : start + step, :] = rows.astype(jnp.bfloat16)


def one_hot_lt(size):
    row = lax.broadcasted_iota(jnp.int32, (size, size), 0)
    column = lax.broadcasted_iota(jnp.int32, (size, size), 1)
    return jnp.where(row < column, 1.0, 0.0).astype(jnp.bfloat16)


def gather_rows(slot_ref, arrived_ref, gain_ref, rows_ref, normed_ref):
    visible, slots = rows_ref.shape[0], arrived_ref.shape[0]
    chosen = one_hot(lax.broadcasted_iota(jnp.int32, (visible, slots), 1), slot_ref[...])
    rows = dot(chosen, arrived_ref[...])
    rows_ref[...] = rows.astype(jnp.bfloat16)
    normed_ref[...] = layer_norm(rows, gain_ref[...]).astype(jnp.bfloat16)


def project_part(part, normed_ref, w_ref, wvt_ref, send_ref, q_ref, k_ref, vt_ref):
    first, last, members = part
    visible, width = normed_ref.shape
    rows, middle = visible // CLASSES, visible // 2
    low, high = first * HDIM, last * HDIM
    normed = normed_ref[...]
    q_ref[...] = (dot(normed, w_ref[:, low:high]) * HDIM ** (-0.5)).astype(jnp.bfloat16)
    k_ref[...] = dot(normed, w_ref[:, width + low : width + high]).astype(jnp.bfloat16)
    vt_ref[...] = dot_nt(wvt_ref[low:high, :], normed).astype(jnp.bfloat16)
    wide = 2 * HDIM

    def place_pair(left, left_odd, right, right_odd):
        left = swap(left) if left_odd else left
        right = right if right_odd else swap(right)
        lanes = lax.broadcasted_iota(jnp.int32, left.shape, 1)
        return jnp.where(lanes < HDIM, left, right)

    for head in range(first, last):
        at, odd = (head - first) // 2 * wide, head % 2
        keys = place_pair(k_ref[:middle, at : at + wide], odd, k_ref[middle:, at : at + wide], odd)
        values = vt_ref[(head - first) * HDIM : (head - first + 1) * HDIM, :]
        for member, (heads, _) in enumerate(members):
            for place in [place for place, one in enumerate(heads) if one == head]:
                base = place * visible
                send_ref[member, base : base + middle, :] = keys
                for i in range(visible // wide):
                    top = base + middle + i * HDIM
                    send_ref[member, top : top + HDIM, :] = values[:, i * wide : (i + 1) * wide]
    for member, (heads, units) in enumerate(members):
        for i in range(0, len(units), 2):
            tiles = []
            for place, cls in units[i : i + 2]:
                at = (heads[place] - first) // 2 * wide
                tiles += [q_ref[cls * rows : (cls + 1) * rows, at : at + wide], heads[place] % 2]
            top = len(heads) * visible + i // 2 * rows
            send_ref[member, top : top + rows, :] = place_pair(*tiles)


def first_kernel(part, slot_ref, arrived_ref, gain_ref, w_ref, wvt_ref, rows_ref, normed_ref, send_ref, *scratch):
    gather_rows(slot_ref, arrived_ref, gain_ref, rows_ref, normed_ref)
    project_part(part, normed_ref, w_ref, wvt_ref, send_ref, *scratch)


def attend_kernel(visible, heads, place_ref, class_ref, block_ref, out_ref):
    members = block_ref.shape[0]
    rows, middle = visible // CLASSES, visible // 2
    group = SEG // visible
    segments = members // group
    wide = 2 * HDIM
    step = pl.program_id(0)
    top = pl.multiple_of(heads * visible + step * rows, rows)
    low = lax.broadcasted_iota(jnp.int32, (group * rows, wide), 1) < HDIM

    for segment in range(segments):
        queries = jnp.concatenate(
            [block_ref[segment * group + i, pl.ds(top, rows), :] for i in range(group)], axis=0
        )
        turned = swap(queries)
        none = jnp.zeros_like(queries)
        halves = []
        for half in range(2):
            cls = class_ref[2 * step + half]
            base = pl.multiple_of(place_ref[2 * step + half] * visible, visible)
            offsets = []
            for other in range(CLASSES):
                apart = jnp.bitwise_and(other - cls, CLASSES - 1)
                offset = jnp.where(jnp.bitwise_and(apart, 1) == 0, math.log(2.0), 0.0)
                offset = jnp.where(apart == 4, math.log(3.0), offset)
                offsets.append(jnp.where(apart == 0, math.log(4.0), offset))
            left = jnp.where(low, turned if half else queries, none)
            right = jnp.where(low, none, queries if half else turned)
            far = jnp.where(cls >= CLASSES // 2, right, left)
            odd = jnp.bitwise_and(cls, 1) == 1

            blocks = []
            for i in range(group):
                member = segment * group + i
                keys = block_ref[member, pl.ds(base, middle), :]
                for side in range(2):
                    count = visible // wide // 2
                    values = [
                        block_ref[member, pl.ds(base + middle + (side * count + j) * HDIM, HDIM), :]
                        for j in range(count)
                    ]
                    score = dot_nt(keys, right if side else left)
                    blocks.append((score, offsets[side * 4 : side * 4 + 4], jnp.concatenate(values, axis=1)))
            for other in range(segments):
                if other == segment:
                    continue
                keys, values = [], []
                for i in range(group):
                    member = other * group + i
                    at = pl.multiple_of(base + jnp.bitwise_and(cls, CLASSES // 2 - 1) * rows, rows)
                    keys.append(block_ref[member, pl.ds(at, rows), :])
                    at = pl.multiple_of(base + middle + jnp.right_shift(cls, 1) * HDIM, HDIM)
                    tile = block_ref[member, pl.ds(at, HDIM), :]
                    values.append(jnp.where(odd, swap(tile), tile)[:, :HDIM])
                score = dot_nt(jnp.concatenate(keys, axis=0), far)
                blocks.append((score, [0.0] * 4, jnp.concatenate(values, axis=1)))

            peak = jnp.max(functools.reduce(jnp.maximum, [score for score, _, _ in blocks]), axis=0, keepdims=True)
            weights = [
                jnp.exp(score[i * rows : (i + 1) * rows] - (peak - offset)).astype(jnp.bfloat16)
                for score, shifts, _ in blocks
                for i, offset in enumerate(shifts)
            ]
            values = jnp.concatenate([value for _, _, value in blocks], axis=1)
            values = jnp.concatenate([values, jnp.ones((16, values.shape[1]), jnp.bfloat16)], axis=0)
            mixed = dot(values, jnp.concatenate(weights, axis=0))
            halves.append(mixed[:HDIM] / mixed[HDIM : HDIM + 1])
        both = jnp.concatenate(halves, axis=0).T.astype(jnp.bfloat16)
        for i in range(group):
            out_ref[segment * group + i, :, :] = both[i * rows : (i + 1) * rows, :]


def finish_kernel(parts, slot_ref, *refs):
    mixed_refs, (rows_ref, gain_ref, w_ref, out_ref, attended_ref) = refs[: len(parts)], refs[len(parts) :]
    visible, _ = rows_ref.shape
    part = visible // CLASSES
    slots = out_ref.shape[0]
    where = {}
    for mixed_ref, (_, _, members) in zip(mixed_refs, parts):
        for member, (heads, units) in enumerate(members):
            for i, (place, cls) in enumerate(units):
                where.setdefault((heads[place], cls), (mixed_ref, member, i))
    for head in range(0, HEADS, 2):
        for cls in range(CLASSES):
            pair = []
            for one in (head, head + 1):
                mixed_ref, member, i = where[(one, cls)]
                tile = mixed_ref[member, i // 2 * part : (i // 2 + 1) * part, :]
                pair.append(tile[:, i % 2 * HDIM : (i % 2 + 1) * HDIM])
            attended_ref[cls * part : (cls + 1) * part, head * HDIM : (head + 2) * HDIM] = (
                jnp.concatenate(pair, axis=1)
            )
    hidden = rows_ref[...].astype(jnp.float32) + dot(attended_ref[...], w_ref[...])
    answer = layer_norm(hidden, gain_ref[...]).astype(jnp.bfloat16)
    step = math.gcd(slots, 256)
    for start in range(0, slots, step):
        wanted = lax.broadcasted_iota(jnp.int32, (step, visible), 0) + start
        out_ref[start : start + step, :] = dot(one_hot(wanted, slot_ref[...]), answer).astype(
            jnp.bfloat16
        )


def unpack_kernel(slot_ref, back_ref, out_ref):
    count, _ = out_ref.shape
    slots = back_ref.shape[0]
    step = math.gcd(count, 256)
    for start in range(0, count, step):
        here = lax.broadcasted_iota(jnp.int32, (step, slots), 1)
        chosen = one_hot(slot_ref[start : start + step, :], here)
        out_ref[start : start + step, :] = dot(chosen, back_ref[...]).astype(jnp.bfloat16)


IN_VMEM = pl.BlockSpec(memory_space=pltpu.VMEM)
WHOLE = pl.BlockSpec()


def call(kernel, outs, out_specs, name, *operands, in_specs=None, scratch=()):
    return pl.pallas_call(
        kernel,
        out_shape=outs,
        in_specs=in_specs or [IN_VMEM] * len(operands),
        out_specs=out_specs,
        scratch_shapes=list(scratch),
        compiler_params=pltpu.CompilerParams(vmem_limit_bytes=VMEM),
        name=name,
    )(*operands)


def on_device(tiles, dest_table, owner_row, w_qkv, w_out, gain_attn, gain_out):
    groups = lax.axis_size("group")
    axes = ("group", "high", "low")
    inside = ("high", "low")
    members = lax.axis_size(inside)
    devices = groups * members
    count, width = tiles.shape
    visible = owner_row.shape[1]
    capacity = 2 * visible // devices
    slots = devices * capacity
    rows = visible // CLASSES
    parts = parts_of(members)
    bf16 = jnp.bfloat16

    moves = [(s * groups + g, g * members + s) for g in range(groups) for s in range(members)]
    owners = lax.ppermute(owner_row.reshape(visible // 128, 128), axes, moves).reshape(visible)
    owners = owners.reshape(rows, CLASSES).T.reshape(visible)

    outgoing, send_slot = call(
        functools.partial(pack_kernel, visible, capacity),
        (jax.ShapeDtypeStruct((slots, width), bf16), jax.ShapeDtypeStruct((1, count), jnp.int32)),
        (WHOLE, IN_VMEM),
        "pack",
        dest_table.reshape(1, count),
        tiles,
        in_specs=[IN_VMEM, pl.BlockSpec(memory_space=pl.ANY)],
        scratch=[pltpu.VMEM((count, width), bf16), pltpu.SemaphoreType.DMA],
    )
    arrived = lax.all_to_all(
        outgoing.reshape(devices, capacity, width), axes, split_axis=0, concat_axis=0, tiled=True
    ).reshape(slots, width)

    source = owners // count
    same = source[:, None] == source[None, :]
    earlier = owners[None, :] < owners[:, None]
    placed = jnp.sum((same & earlier).astype(jnp.int32), axis=1)
    slot = source * capacity + placed

    weights = (w_qkv, w_qkv[:, 2 * width :].T)
    blocks = []
    for i, part in enumerate(parts):
        first, last, dealt = part
        heads, units = len(dealt[0][0]), len(dealt[0][1])
        shape = jax.ShapeDtypeStruct((members, heads * visible + units // 2 * rows, 2 * HDIM), bf16)
        size = (last - first) * HDIM
        scratch = [pltpu.VMEM((visible, size), bf16)] * 2 + [pltpu.VMEM((size, visible), bf16)]
        if i == 0:
            student, normed, send = call(
                functools.partial(first_kernel, part),
                (jax.ShapeDtypeStruct((visible, width), bf16),) * 2 + (shape,),
                (WHOLE, IN_VMEM, WHOLE),
                "project_first",
                slot[:, None],
                arrived,
                gain_attn[None, :],
                *weights,
                scratch=scratch,
            )
        else:
            kernel = functools.partial(project_part, part)
            send = call(kernel, shape, WHOLE, "project_next", normed, *weights, scratch=scratch)
        if blocks:
            blocks[-1], send = lax.optimization_barrier((blocks[-1], send))
        blocks.append(lax.all_to_all(send, inside, split_axis=0, concat_axis=0, tiled=True))

    mixed = []
    for (_, _, part), block in zip(parts, blocks):
        heads, units = len(part[0][0]), len(part[0][1])
        table = jnp.array([list(zip(*units)) for _, units in part], jnp.int32)[lax.axis_index(inside)]
        result = pl.pallas_call(
            functools.partial(attend_kernel, visible, heads),
            out_shape=jax.ShapeDtypeStruct((members, units // 2 * rows, 2 * HDIM), bf16),
            grid_spec=pltpu.PrefetchScalarGridSpec(
                num_scalar_prefetch=2,
                grid=(units // 2,),
                in_specs=[IN_VMEM],
                out_specs=pl.BlockSpec((members, rows, 2 * HDIM), lambda i, *_: (0, i, 0)),
            ),
            compiler_params=pltpu.CompilerParams(vmem_limit_bytes=VMEM),
            name="attend",
        )(table[0], table[1], block)
        mixed.append(lax.all_to_all(result, inside, split_axis=0, concat_axis=0, tiled=True))

    answers = call(
        functools.partial(finish_kernel, parts),
        jax.ShapeDtypeStruct((slots, width), bf16),
        WHOLE,
        "finish",
        slot[None, :],
        *mixed,
        student,
        gain_out[None, :],
        w_out,
        scratch=[pltpu.VMEM((visible, width), bf16)],
    )
    back = lax.all_to_all(
        answers.reshape(devices, capacity, width), axes, split_axis=0, concat_axis=0, tiled=True
    ).reshape(slots, width)
    shape = jax.ShapeDtypeStruct((count, width), bf16)
    return call(unpack_kernel, shape, WHOLE, "unpack", send_slot.reshape(count, 1), back)


def solution(mesh):
    n_seq, n_slide = mesh.shape["seq"], mesh.shape["slide"]
    split = Mesh(
        mesh.devices.reshape(n_slide, n_seq // n_slide, n_slide), ("group", "high", "low")
    )
    every = ("group", "high", "low")
    in_specs = (P(every, None), P(every), P("low", ("group", "high")), P(), P(), P(), P())
    return jax.shard_map(
        on_device, mesh=split, in_specs=in_specs, out_specs=P(every, None), check_vma=False
    )
```

```python
import functools
import itertools
import math

import jax
import jax.numpy as jnp
from jax import lax
from jax.experimental import pallas as pl
from jax.experimental.pallas import tpu as pltpu
from jax.sharding import Mesh
from jax.sharding import PartitionSpec as P

HEADS = 12
HDIM = 64
SEG = 2048
CLASSES = 8
EPS = 1e-05
VMEM = 24 << 20


def layer_norm(inputs, gain):
    average = jnp.mean(inputs, axis=-1, keepdims=True)
    centred = inputs - average
    spread = jnp.mean(centred * centred, axis=-1, keepdims=True)
    return centred * lax.rsqrt(spread + EPS) * gain


def one_hot(left, right):
    return jnp.where(left == right, 1.0, 0.0).astype(jnp.bfloat16)


def dot(left, right):
    return jnp.dot(left, right, preferred_element_type=jnp.float32)


def parts_of(members):
    full = HEADS // members
    every = [(0, cls) for cls in range(CLASSES)]
    parts = [
        (i * members, (i + 1) * members, [([i * members + member], every) for member in range(members)])
        for i in range(full)
    ]
    first = full * members
    owned = (HEADS - first) * CLASSES // members
    if owned:
        dealt = []
        for member in range(members):
            units = [divmod(first * CLASSES + member * owned + i, CLASSES) for i in range(owned)]
            dealt.append((sorted({head for head, _ in units}), units))
        width = max(len(heads) for heads, _ in dealt)
        part = []
        for heads, units in dealt:
            units = [(heads.index(head), cls) for head, cls in units]
            part.append((heads + heads[-1:] * (width - len(heads)), units + units[-1:] * (owned % 2)))
        parts.append((first, HEADS, part))
    return parts


def swap(tile):
    return jnp.concatenate([tile[:, HDIM:], tile[:, :HDIM]], axis=1)


def dot_nt(left, right):
    return lax.dot_general(left, right, (((1,), (1,)), ((), ())), preferred_element_type=jnp.float32)


def pack_kernel(visible, capacity, dest_ref, tiles_hbm, out_hbm, slot_ref, tiles_ref, out_ref, sem, sems):
    fetch = pltpu.make_async_copy(tiles_hbm, tiles_ref, sem)
    fetch.start()
    slots, _ = out_ref.shape
    count = dest_ref.shape[1]
    devices = slots // capacity
    target = jnp.right_shift(dest_ref[...], visible.bit_length() - 1)
    lanes = 128
    before = one_hot_lt(lanes)
    offset = jnp.zeros((devices, 1), jnp.float32)
    pieces = []
    for start in range(0, count, lanes):
        here = target[:, start : start + lanes]
        device = lax.broadcasted_iota(jnp.int32, (devices, lanes), 0)
        chosen = jnp.where(device == here, 1.0, 0.0)
        rank = dot(chosen.astype(jnp.bfloat16), before) + offset
        placed = jnp.sum(chosen * rank, axis=0, keepdims=True).astype(jnp.int32)
        pieces.append(jnp.where(here >= 0, here * capacity + placed, -1))
        offset = offset + jnp.sum(chosen, axis=1, keepdims=True)
    slot = jnp.concatenate(pieces, axis=1)
    slot_ref[...] = slot
    fetch.wait()
    step = math.gcd(slots, 256)
    copies = []
    for start in range(0, slots, step):
        wanted = lax.broadcasted_iota(jnp.int32, (step, count), 0) + start
        rows = dot(one_hot(wanted, slot), tiles_ref[...])
        out_ref[start : start + step, :] = rows.astype(jnp.bfloat16)
        copies.append(write(out_ref, out_hbm, start, step, sems))
    for copy in copies:
        copy.wait()


def write(source, target, start, step, sems):
    at = pl.ds(start, step)
    copy = pltpu.make_async_copy(source.at[at], target.at[at], sems.at[start // step])
    copy.start()
    return copy


def one_hot_lt(size):
    row = lax.broadcasted_iota(jnp.int32, (size, size), 0)
    column = lax.broadcasted_iota(jnp.int32, (size, size), 1)
    return jnp.where(row < column, 1.0, 0.0).astype(jnp.bfloat16)


def project_part(part, normed, w_ref, wvt_ref, send_hbm, send_ref, q_ref, k_ref, vt_ref, sems):
    first, last, members = part
    visible, width = normed.shape
    rows, middle = visible // CLASSES, visible // 2
    low, high = 0, (last - first) * HDIM
    q_ref[...] = (dot(normed, w_ref[0]) * HDIM ** (-0.5)).astype(jnp.bfloat16)
    k_ref[...] = dot(normed, w_ref[1]).astype(jnp.bfloat16)
    vt_ref[...] = dot_nt(wvt_ref[...], normed).astype(jnp.bfloat16)
    wide = 2 * HDIM

    def place_pair(left, left_odd, right, right_odd):
        left = swap(left) if left_odd else left
        right = right if right_odd else swap(right)
        lanes = lax.broadcasted_iota(jnp.int32, left.shape, 1)
        return jnp.where(lanes < HDIM, left, right)

    for head in range(first, last):
        at, odd = (head - first) // 2 * wide, head % 2
        keys = place_pair(k_ref[:middle, at : at + wide], odd, k_ref[middle:, at : at + wide], odd)
        values = vt_ref[(head - first) * HDIM : (head - first + 1) * HDIM, :]
        for member, (heads, _) in enumerate(members):
            for place in [place for place, one in enumerate(heads) if one == head]:
                base = place * visible
                send_ref[member, base : base + middle, :] = keys
                for i in range(visible // wide):
                    top = base + middle + i * HDIM
                    send_ref[member, top : top + HDIM, :] = values[:, i * wide : (i + 1) * wide]
    copies = []
    for member, (heads, units) in enumerate(members):
        for i in range(0, len(units), 2):
            tiles = []
            for place, cls in units[i : i + 2]:
                at = (heads[place] - first) // 2 * wide
                tiles += [q_ref[cls * rows : (cls + 1) * rows, at : at + wide], heads[place] % 2]
            top = len(heads) * visible + i // 2 * rows
            send_ref[member, top : top + rows, :] = place_pair(*tiles)
        copies.append(write(send_ref, send_hbm, member, 1, sems))
    return copies


def fetch_weights(part, w_hbm, wvt_hbm, w_ref, wvt_ref, sems):
    width = w_hbm.shape[0]
    at, size = part[0] * HDIM, (part[1] - part[0]) * HDIM
    copies = [
        pltpu.make_async_copy(w_hbm.at[:, pl.ds(i * width + at, size)], w_ref.at[i], sems.at[i])
        for i in range(2)
    ]
    copies.append(pltpu.make_async_copy(wvt_hbm.at[pl.ds(at, size)], wvt_ref, sems.at[2]))
    for copy in copies:
        copy.start()
    return copies


def first_kernel(part, slot_ref, arrived_ref, gain_ref, w_hbm, wvt_hbm, rows_hbm, normed_hbm, send_hbm,
                 w_ref, wvt_ref, send_ref, q_ref, k_ref, vt_ref, sems, rows_ref, normed_ref, more):
    weights = fetch_weights(part, w_hbm, wvt_hbm, w_ref, wvt_ref, more)
    visible, slots = rows_ref.shape[0], arrived_ref.shape[0]
    chosen = one_hot(lax.broadcasted_iota(jnp.int32, (visible, slots), 1), slot_ref[...])
    rows = dot(chosen, arrived_ref[...])
    rows_ref[...] = rows.astype(jnp.bfloat16)
    normed = layer_norm(rows, gain_ref[...]).astype(jnp.bfloat16)
    normed_ref[...] = normed
    copies = [
        pltpu.make_async_copy(rows_ref, rows_hbm, more.at[3]),
        pltpu.make_async_copy(normed_ref, normed_hbm, more.at[4]),
    ]
    for copy in copies:
        copy.start()
    for copy in weights:
        copy.wait()
    copies += project_part(part, normed, w_ref, wvt_ref, send_hbm, send_ref, q_ref, k_ref, vt_ref, sems)
    for copy in copies:
        copy.wait()


def next_kernel(part, normed_ref, w_hbm, wvt_hbm, send_hbm, w_ref, wvt_ref, send_ref, q_ref, k_ref, vt_ref, sems, more):
    for copy in fetch_weights(part, w_hbm, wvt_hbm, w_ref, wvt_ref, more):
        copy.wait()
    for copy in project_part(part, normed_ref[...], w_ref, wvt_ref, send_hbm, send_ref, q_ref, k_ref, vt_ref, sems):
        copy.wait()


def attend_kernel(visible, heads, place_ref, class_ref, block_ref, out_ref, score_ref, peak_ref):
    members = block_ref.shape[0]
    rows, middle = visible // CLASSES, visible // 2
    group = SEG // visible
    segments = members // group
    wide = 2 * HDIM
    size = group * rows
    turns = out_ref.shape[1] // rows * segments
    low = lax.broadcasted_iota(jnp.int32, (size, wide), 1) < HDIM

    def tile_of(turn, half):
        step, segment = turn // segments, turn % segments
        cls = class_ref[2 * step + half]
        base = pl.multiple_of(place_ref[2 * step + half] * visible, visible)
        return step, segment, cls, base

    def member_of(segment, i, apart):
        return lax.rem(segment + apart, segments) * group + i

    def blocks_of(segment):
        near = [(member_of(segment, i, 0), side) for i in range(group) for side in range(2)]
        return near + [(apart, None) for apart in range(1, segments)]

    def score_steps(turn, half):
        step, segment, cls, base = tile_of(turn, half)
        top = pl.multiple_of(heads * visible + step * rows, rows)
        queries = jnp.concatenate(
            [block_ref[member_of(segment, i, 0), pl.ds(top, rows), :] for i in range(group)], axis=0
        )
        turned = swap(queries)
        none = jnp.zeros_like(queries)
        left = jnp.where(low, turned if half else queries, none)
        right = jnp.where(low, none, queries if half else turned)
        far = jnp.where(cls >= CLASSES // 2, right, left)
        peak = None
        for j, (member, side) in enumerate(blocks_of(segment)):
            if side is None:
                at = pl.multiple_of(base + jnp.bitwise_and(cls, CLASSES // 2 - 1) * rows, rows)
                keys = [block_ref[member_of(segment, i, member), pl.ds(at, rows), :] for i in range(group)]
                score = dot_nt(jnp.concatenate(keys, axis=0), far)
            else:
                score = dot_nt(block_ref[member, pl.ds(base, middle), :], right if side else left)
            score_ref[half, j * size : (j + 1) * size, :] = score
            highest = jnp.max(score.reshape(size // 8, 8, size), axis=0)
            peak = highest if peak is None else jnp.maximum(peak, highest)
            yield
        peak_ref[half] = jnp.broadcast_to(jnp.max(peak, axis=0, keepdims=True), peak.shape)
        yield

    def weight_steps(turn, half, results):
        step, segment, cls, base = tile_of(turn, half)
        peak = peak_ref[half]
        odd = jnp.bitwise_and(cls, 1) == 1
        mixed = jnp.zeros((HDIM + 16, size), jnp.float32)
        for j, (member, side) in enumerate(blocks_of(segment)):
            values = []
            if side is None:
                at = pl.multiple_of(base + middle + jnp.right_shift(cls, 1) * HDIM, HDIM)
                for i in range(group):
                    tile = block_ref[member_of(segment, i, member), pl.ds(at, HDIM), :]
                    values.append(jnp.where(odd, swap(tile), tile)[:, :HDIM])
                shifted = [peak] * group
            else:
                count = visible // wide // 2
                for i in range(count):
                    at = pl.multiple_of(base + middle + (side * count + i) * HDIM, HDIM)
                    values.append(block_ref[member, pl.ds(at, HDIM), :])
                shifted = []
                for other in range(side * 4, side * 4 + 4):
                    apart = jnp.bitwise_and(other - cls, CLASSES - 1)
                    offset = jnp.where(jnp.bitwise_and(apart, 1) == 0, math.log(2.0), 0.0)
                    offset = jnp.where(apart == 4, math.log(3.0), offset)
                    shifted.append(peak - jnp.where(apart == 0, math.log(4.0), offset))
            weights = []
            for i, one in enumerate(shifted):
                at = j * size + i * rows
                score = score_ref[half, at : at + rows, :].reshape(rows // 8, 8, size)
                weights.append(jnp.exp(score - one[None]).reshape(rows, size).astype(jnp.bfloat16))
            values = jnp.concatenate(values, axis=1)
            values = jnp.concatenate([values, jnp.ones((16, size), jnp.bfloat16)], axis=0)
            mixed += dot(values, jnp.concatenate(weights, axis=0))
            yield
        results.append(mixed[:HDIM] / mixed[HDIM : HDIM + 1])
        yield

    def run(*streams):
        for _ in itertools.zip_longest(*streams):
            pass

    def body(turn, carry):
        results = []
        run(weight_steps(turn, 0, results), score_steps(turn, 1))
        after = jnp.minimum(turn + 1, turns - 1)
        run(weight_steps(turn, 1, results), score_steps(after, 0))
        both = jnp.concatenate(results, axis=0).T.astype(jnp.bfloat16)
        step, segment = turn // segments, turn % segments
        for i in range(group):
            at = pl.multiple_of(step * rows, rows)
            out_ref[segment * group + i, pl.ds(at, rows), :] = both[i * rows : (i + 1) * rows, :]
        return carry

    run(score_steps(0, 0))
    lax.fori_loop(0, turns, body, 0)


def finish_kernel(parts, slot_ref, *refs):
    mixed_refs = refs[: len(parts)]
    rows_hbm, gain_ref, w_hbm, out_hbm, attended_ref, rows_ref, w_ref, out_ref, more, sems = refs[len(parts) :]
    fetches = [
        pltpu.make_async_copy(w_hbm, w_ref, more.at[0]),
        pltpu.make_async_copy(rows_hbm, rows_ref, more.at[1]),
    ]
    for copy in fetches:
        copy.start()
    visible, _ = rows_ref.shape
    part = visible // CLASSES
    slots = out_ref.shape[0]
    where = {}
    for mixed_ref, (_, _, members) in zip(mixed_refs, parts):
        for member, (heads, units) in enumerate(members):
            for i, (place, cls) in enumerate(units):
                where.setdefault((heads[place], cls), (mixed_ref, member, i))
    for head in range(0, HEADS, 2):
        for cls in range(CLASSES):
            pair = []
            for one in (head, head + 1):
                mixed_ref, member, i = where[(one, cls)]
                tile = mixed_ref[member, i // 2 * part : (i // 2 + 1) * part, :]
                pair.append(tile[:, i % 2 * HDIM : (i % 2 + 1) * HDIM])
            attended_ref[cls * part : (cls + 1) * part, head * HDIM : (head + 2) * HDIM] = (
                jnp.concatenate(pair, axis=1)
            )
    for copy in fetches:
        copy.wait()
    hidden = rows_ref[...].astype(jnp.float32) + dot(attended_ref[...], w_ref[...])
    answer = layer_norm(hidden, gain_ref[...]).astype(jnp.bfloat16)
    step = math.gcd(slots, 256)
    copies = []
    for start in range(0, slots, step):
        wanted = lax.broadcasted_iota(jnp.int32, (step, visible), 0) + start
        out_ref[start : start + step, :] = dot(one_hot(wanted, slot_ref[...]), answer).astype(
            jnp.bfloat16
        )
        copies.append(write(out_ref, out_hbm, start, step, sems))
    for copy in copies:
        copy.wait()


def unpack_kernel(slot_ref, back_ref, out_hbm, out_ref, sems):
    count = out_ref.shape[0]
    slots = back_ref.shape[0]
    step = math.gcd(count, 256)
    copies = []
    for start in range(0, count, step):
        here = lax.broadcasted_iota(jnp.int32, (step, slots), 1)
        chosen = one_hot(slot_ref[start : start + step, :], here)
        out_ref[start : start + step, :] = dot(chosen, back_ref[...]).astype(jnp.bfloat16)
        copies.append(write(out_ref, out_hbm, start, step, sems))
    for copy in copies:
        copy.wait()


IN_VMEM = pl.BlockSpec(memory_space=pltpu.VMEM)
IN_HBM = pl.BlockSpec(memory_space=pltpu.HBM)
COPIES = pltpu.SemaphoreType.DMA


def call(kernel, outs, out_specs, name, *operands, in_specs=None, scratch=()):
    in_specs = in_specs or [IN_VMEM] * len(operands)
    operands = [
        pltpu.with_memory_space_constraint(operand, pltpu.HBM) if spec is IN_HBM else operand
        for operand, spec in zip(operands, in_specs)
    ]
    outs = jax.tree.map(
        lambda out, spec: pltpu.HBM(out.shape, out.dtype) if spec is IN_HBM else out, outs, out_specs
    )
    return pl.pallas_call(
        kernel,
        out_shape=outs,
        in_specs=in_specs,
        out_specs=out_specs,
        scratch_shapes=list(scratch),
        compiler_params=pltpu.CompilerParams(vmem_limit_bytes=VMEM),
        name=name,
    )(*operands)


def on_device(tiles, dest_table, owner_row, w_qkv, w_out, gain_attn, gain_out):
    groups = lax.axis_size("group")
    axes = ("group", "high", "low")
    inside = ("high", "low")
    members = lax.axis_size(inside)
    devices = groups * members
    count, width = tiles.shape
    visible = owner_row.shape[1]
    capacity = 2 * visible // devices
    slots = devices * capacity
    rows = visible // CLASSES
    parts = parts_of(members)
    bf16 = jnp.bfloat16

    moves = [(s * groups + g, g * members + s) for g in range(groups) for s in range(members)]
    owners = lax.ppermute(owner_row.reshape(visible // 128, 128), axes, moves).reshape(visible)
    owners = owners.reshape(rows, CLASSES).T.reshape(visible)

    outgoing, send_slot = call(
        functools.partial(pack_kernel, visible, capacity),
        (jax.ShapeDtypeStruct((slots, width), bf16), jax.ShapeDtypeStruct((1, count), jnp.int32)),
        (IN_HBM, IN_VMEM),
        "pack",
        dest_table.reshape(1, count),
        tiles,
        in_specs=[IN_VMEM, IN_HBM],
        scratch=[
            pltpu.VMEM((count, width), bf16),
            pltpu.VMEM((slots, width), bf16),
            COPIES,
            COPIES((slots // math.gcd(slots, 256),)),
        ],
    )
    arrived = lax.all_to_all(
        outgoing.reshape(devices, capacity, width), axes, split_axis=0, concat_axis=0, tiled=True
    ).reshape(slots, width)

    source = owners // count
    same = source[:, None] == source[None, :]
    earlier = owners[None, :] < owners[:, None]
    placed = jnp.sum((same & earlier).astype(jnp.int32), axis=1)
    slot = source * capacity + placed

    weights = (w_qkv, w_qkv[:, 2 * width :].T)
    blocks = []
    for i, part in enumerate(parts):
        first, last, dealt = part
        heads, units = len(dealt[0][0]), len(dealt[0][1])
        shape = jax.ShapeDtypeStruct((members, heads * visible + units // 2 * rows, 2 * HDIM), bf16)
        size = (last - first) * HDIM
        scratch = [
            pltpu.VMEM((2, width, size), bf16),
            pltpu.VMEM((size, width), bf16),
            pltpu.VMEM(shape.shape, bf16),
            pltpu.VMEM((visible, size), bf16),
            pltpu.VMEM((visible, size), bf16),
            pltpu.VMEM((size, visible), bf16),
            COPIES((members,)),
        ]
        if i == 0:
            student, normed, send = call(
                functools.partial(first_kernel, part),
                (jax.ShapeDtypeStruct((visible, width), bf16),) * 2 + (shape,),
                (IN_HBM,) * 3,
                "project_first",
                slot[:, None],
                arrived,
                gain_attn[None, :],
                *weights,
                in_specs=[IN_VMEM] * 3 + [IN_HBM] * 2,
                scratch=scratch + [pltpu.VMEM((visible, width), bf16)] * 2 + [COPIES((5,))],
            )
        else:
            send = call(
                functools.partial(next_kernel, part),
                shape,
                IN_HBM,
                "project_next",
                normed,
                *weights,
                in_specs=[IN_VMEM] + [IN_HBM] * 2,
                scratch=scratch + [COPIES((3,))],
            )
        if blocks:
            blocks[-1], send = lax.optimization_barrier((blocks[-1], send))
        blocks.append(lax.all_to_all(send, inside, split_axis=0, concat_axis=0, tiled=True))

    mixed = []
    for (_, _, part), block in zip(parts, blocks):
        heads, units = len(part[0][0]), len(part[0][1])
        table = jnp.array([list(zip(*units)) for _, units in part], jnp.int32)[lax.axis_index(inside)]
        depth = SEG + (members * visible // SEG - 1) * SEG // CLASSES
        across = SEG // CLASSES
        result = pl.pallas_call(
            functools.partial(attend_kernel, visible, heads),
            out_shape=jax.ShapeDtypeStruct((members, units // 2 * rows, 2 * HDIM), bf16),
            grid_spec=pltpu.PrefetchScalarGridSpec(
                num_scalar_prefetch=2,
                grid=(1,),
                in_specs=[IN_VMEM],
                out_specs=pl.BlockSpec((members, units // 2 * rows, 2 * HDIM), lambda i, *_: (0, 0, 0)),
                scratch_shapes=[
                    pltpu.VMEM((2, depth, across), jnp.float32),
                    pltpu.VMEM((2, 8, across), jnp.float32),
                ],
            ),
            compiler_params=pltpu.CompilerParams(vmem_limit_bytes=VMEM),
            name="attend",
        )(table[0], table[1], block)
        mixed.append(lax.all_to_all(result, inside, split_axis=0, concat_axis=0, tiled=True))

    answers = call(
        functools.partial(finish_kernel, parts),
        jax.ShapeDtypeStruct((slots, width), bf16),
        IN_HBM,
        "finish",
        slot[None, :],
        *mixed,
        student,
        gain_out[None, :],
        w_out,
        in_specs=[IN_VMEM] * (1 + len(parts)) + [IN_HBM, IN_VMEM, IN_HBM],
        scratch=[
            pltpu.VMEM((visible, width), bf16),
            pltpu.VMEM((visible, width), bf16),
            pltpu.VMEM((width, width), bf16),
            pltpu.VMEM((slots, width), bf16),
            COPIES((2,)),
            COPIES((slots // math.gcd(slots, 256),)),
        ],
    )
    back = lax.all_to_all(
        answers.reshape(devices, capacity, width), axes, split_axis=0, concat_axis=0, tiled=True
    ).reshape(slots, width)
    shape = jax.ShapeDtypeStruct((count, width), bf16)
    return call(
        unpack_kernel,
        shape,
        IN_HBM,
        "unpack",
        send_slot.reshape(count, 1),
        back,
        scratch=[pltpu.VMEM((count, width), bf16), COPIES((count // math.gcd(count, 256),))],
    )


def solution(mesh):
    n_seq, n_slide = mesh.shape["seq"], mesh.shape["slide"]
    split = Mesh(
        mesh.devices.reshape(n_slide, n_seq // n_slide, n_slide), ("group", "high", "low")
    )
    every = ("group", "high", "low")
    in_specs = (P(every, None), P(every), P("low", ("group", "high")), P(), P(), P(), P())
    return jax.shard_map(
        on_device, mesh=split, in_specs=in_specs, out_specs=P(every, None), check_vma=False
    )
```

```python
import functools
import itertools
import math

import jax
import jax.numpy as jnp
from jax import lax
from jax.experimental import pallas as pl
from jax.experimental.pallas import tpu as pltpu
from jax.sharding import Mesh
from jax.sharding import PartitionSpec as P

HEADS = 12
HDIM = 64
SEG = 2048
CLASSES = 8
EPS = 1e-05
VMEM = 24 << 20


def layer_norm(inputs, gain):
    average = jnp.mean(inputs, axis=-1, keepdims=True)
    centred = inputs - average
    spread = jnp.mean(centred * centred, axis=-1, keepdims=True)
    return centred * lax.rsqrt(spread + EPS) * gain


def one_hot(left, right):
    return jnp.where(left == right, 1.0, 0.0).astype(jnp.bfloat16)


def dot(left, right):
    return jnp.dot(left, right, preferred_element_type=jnp.float32)


def parts_of(members, segments):
    full = HEADS // members
    every = [(0, segment) for segment in range(segments)]
    parts = [
        (i * members, (i + 1) * members, [([i * members + member], every) for member in range(members)])
        for i in range(full)
    ]
    first = full * members
    owned = (HEADS - first) * segments // members
    if owned:
        dealt = []
        for member in range(members):
            units = [divmod(first * segments + member * owned + i, segments) for i in range(owned)]
            dealt.append((sorted({head for head, _ in units}), units))
        width = max(len(heads) for heads, _ in dealt)
        part = []
        for heads, units in dealt:
            units = [(heads.index(head), segment) for head, segment in units]
            part.append((heads + heads[-1:] * (width - len(heads)), units))
        parts.append((first, HEADS, part))
    return parts


def place_pair(left, left_odd, right, right_odd):
    left = swap(left) if left_odd else left
    right = right if right_odd else swap(right)
    lanes = lax.broadcasted_iota(jnp.int32, left.shape, 1)
    return jnp.where(lanes < HDIM, left, right)


def swap(tile):
    return jnp.concatenate([tile[:, HDIM:], tile[:, :HDIM]], axis=1)


def dot_nt(left, right):
    return lax.dot_general(left, right, (((1,), (1,)), ((), ())), preferred_element_type=jnp.float32)


def pack_kernel(visible, capacity, dest_ref, tiles_hbm, out_hbm, slot_ref, tiles_ref, out_ref, sem, sems):
    fetch = pltpu.make_async_copy(tiles_hbm, tiles_ref, sem)
    fetch.start()
    slots, _ = out_ref.shape
    count = dest_ref.shape[1]
    devices = slots // capacity
    target = jnp.right_shift(dest_ref[...], visible.bit_length() - 1)
    lanes = 128
    before = one_hot_lt(lanes)
    offset = jnp.zeros((devices, 1), jnp.float32)
    pieces = []
    for start in range(0, count, lanes):
        here = target[:, start : start + lanes]
        device = lax.broadcasted_iota(jnp.int32, (devices, lanes), 0)
        chosen = jnp.where(device == here, 1.0, 0.0)
        rank = dot(chosen.astype(jnp.bfloat16), before) + offset
        placed = jnp.sum(chosen * rank, axis=0, keepdims=True).astype(jnp.int32)
        pieces.append(jnp.where(here >= 0, here * capacity + placed, -1))
        offset = offset + jnp.sum(chosen, axis=1, keepdims=True)
    slot = jnp.concatenate(pieces, axis=1)
    slot_ref[...] = slot
    fetch.wait()
    step = math.gcd(slots, 256)
    copies = []
    for start in range(0, slots, step):
        wanted = lax.broadcasted_iota(jnp.int32, (step, count), 0) + start
        rows = dot(one_hot(wanted, slot), tiles_ref[...])
        out_ref[start : start + step, :] = rows.astype(jnp.bfloat16)
        copies.append(write(out_ref, out_hbm, start, step, sems))
    for copy in copies:
        copy.wait()


def write(source, target, start, step, sems):
    at = pl.ds(start, step)
    copy = pltpu.make_async_copy(source.at[at], target.at[at], sems.at[start // step])
    copy.start()
    return copy


def one_hot_lt(size):
    row = lax.broadcasted_iota(jnp.int32, (size, size), 0)
    column = lax.broadcasted_iota(jnp.int32, (size, size), 1)
    return jnp.where(row < column, 1.0, 0.0).astype(jnp.bfloat16)


def project_part(part, segment, normed, extra, w_ref, wvt_ref, send_hbm, send_ref, q_ref, k_ref, vt_ref, sems):
    first, last, members = part
    visible, width = normed.shape
    rows, middle = visible // CLASSES, visible // 2
    wide = 2 * HDIM
    q_ref[...] = (dot(normed, w_ref[0]) * HDIM ** (-0.5)).astype(jnp.bfloat16)
    k_ref[...] = dot(normed, w_ref[1]).astype(jnp.bfloat16)
    vt_ref[...] = dot_nt(wvt_ref[...], normed).astype(jnp.bfloat16)

    def queries_of(head, cls):
        at = (head - first) // 2 * wide
        pair = [q_ref[(cls + i) * rows : (cls + i + 1) * rows, at : at + wide] for i in range(2)]
        return place_pair(pair[0], head % 2, pair[1], head % 2)

    for head in range(first, last):
        at, odd = (head - first) // 2 * wide, head % 2
        keys = place_pair(k_ref[:middle, at : at + wide], odd, k_ref[middle:, at : at + wide], odd)
        values = vt_ref[(head - first) * HDIM : (head - first + 1) * HDIM, :]
        for member, (heads, _) in enumerate(members):
            for place in [place for place, one in enumerate(heads) if one == head]:
                base = place * visible
                send_ref[member, base : base + middle, :] = keys
                for i in range(visible // wide):
                    top = base + middle + i * HDIM
                    send_ref[member, top : top + HDIM, :] = values[:, i * wide : (i + 1) * wide]
    copies = []
    for member, (heads, units) in enumerate(members):
        base = len(heads) * visible
        for i in range(CLASSES // 2):
            tile = queries_of(heads[0], 2 * i)
            for place, head in enumerate(heads[1:], 1):
                mine = functools.reduce(
                    jnp.logical_or, [segment[0] == one for at, one in units if at == place], False
                )
                if head != heads[0]:
                    tile = jnp.where(mine, queries_of(head, 2 * i), tile)
            send_ref[member, base + i * rows : base + (i + 1) * rows, :] = tile
        if extra is not None:
            send_ref[member, base + middle :, :] = extra
        copies.append(write(send_ref, send_hbm, member, 1, sems))
    return copies


def fetch_weights(part, w_hbm, wvt_hbm, w_ref, wvt_ref, sems):
    width = w_hbm.shape[0]
    at, size = part[0] * HDIM, (part[1] - part[0]) * HDIM
    copies = [
        pltpu.make_async_copy(w_hbm.at[:, pl.ds(i * width + at, size)], w_ref.at[i], sems.at[i])
        for i in range(2)
    ]
    copies.append(pltpu.make_async_copy(wvt_hbm.at[pl.ds(at, size)], wvt_ref, sems.at[2]))
    for copy in copies:
        copy.start()
    return copies


def first_kernel(part, segment, slot_ref, extra_ref, arrived_ref, gain_ref, w_hbm, wvt_hbm, normed_hbm, send_hbm,
                 w_ref, wvt_ref, send_ref, q_ref, k_ref, vt_ref, sems, normed_ref, more):
    weights = fetch_weights(part, w_hbm, wvt_hbm, w_ref, wvt_ref, more)
    visible, slots = normed_ref.shape[0], arrived_ref.shape[0]
    chosen = one_hot(lax.broadcasted_iota(jnp.int32, (visible, slots), 1), slot_ref[...])
    rows = dot(chosen, arrived_ref[...])
    normed = layer_norm(rows, gain_ref[...]).astype(jnp.bfloat16)
    normed_ref[...] = normed
    copies = [pltpu.make_async_copy(normed_ref, normed_hbm, more.at[3])]
    for copy in copies:
        copy.start()
    for copy in weights:
        copy.wait()
    copies += project_part(
        part, segment, normed, extra_ref[...], w_ref, wvt_ref, send_hbm, send_ref, q_ref, k_ref, vt_ref, sems
    )
    for copy in copies:
        copy.wait()


def next_kernel(part, segment, normed_ref, w_hbm, wvt_hbm, send_hbm, w_ref, wvt_ref, send_ref, q_ref, k_ref, vt_ref, sems, more):
    for copy in fetch_weights(part, w_hbm, wvt_hbm, w_ref, wvt_ref, more):
        copy.wait()
    copies = project_part(
        part, segment, normed_ref[...], None, w_ref, wvt_ref, send_hbm, send_ref, q_ref, k_ref, vt_ref, sems
    )
    for copy in copies:
        copy.wait()


def attend_kernel(visible, heads, place_ref, segment_ref, block_ref, out_ref, score_ref, peak_ref):
    members = block_ref.shape[0]
    rows, middle = visible // CLASSES, visible // 2
    group = SEG // visible
    segments = members // group
    wide = 2 * HDIM
    size = group * rows
    pairs = CLASSES // 2
    turns = out_ref.shape[0] // group * pairs
    low = lax.broadcasted_iota(jnp.int32, (size, wide), 1) < HDIM

    def tile_of(turn, half):
        unit, step = turn // pairs, turn % pairs
        base = pl.multiple_of(place_ref[unit] * visible, visible)
        return step, segment_ref[unit], 2 * step + half, base

    def member_of(segment, i, apart):
        return lax.rem(segment + apart, segments) * group + i

    def blocks_of(segment):
        near = [(member_of(segment, i, 0), side) for i in range(group) for side in range(2)]
        return near + [(apart, None) for apart in range(1, segments)]

    def score_steps(turn, half):
        step, segment, cls, base = tile_of(turn, half)
        top = pl.multiple_of(heads * visible + step * rows, rows)
        queries = jnp.concatenate(
            [block_ref[member_of(segment, i, 0), pl.ds(top, rows), :] for i in range(group)], axis=0
        )
        turned = swap(queries)
        none = jnp.zeros_like(queries)
        left = jnp.where(low, turned if half else queries, none)
        right = jnp.where(low, none, queries if half else turned)
        far = jnp.where(cls >= CLASSES // 2, right, left)
        peak = None
        for j, (member, side) in enumerate(blocks_of(segment)):
            if side is None:
                at = pl.multiple_of(base + jnp.bitwise_and(cls, CLASSES // 2 - 1) * rows, rows)
                keys = [block_ref[member_of(segment, i, member), pl.ds(at, rows), :] for i in range(group)]
                score = dot_nt(jnp.concatenate(keys, axis=0), far)
            else:
                score = dot_nt(block_ref[member, pl.ds(base, middle), :], right if side else left)
            score_ref[half, j * size : (j + 1) * size, :] = score
            highest = jnp.max(score.reshape(size // 8, 8, size), axis=0)
            peak = highest if peak is None else jnp.maximum(peak, highest)
            yield
        peak_ref[half] = jnp.broadcast_to(jnp.max(peak, axis=0, keepdims=True), peak.shape)
        yield

    def weight_steps(turn, half, results):
        step, segment, cls, base = tile_of(turn, half)
        peak = peak_ref[half]
        odd = jnp.bitwise_and(cls, 1) == 1
        mixed = jnp.zeros((HDIM + 16, size), jnp.float32)
        for j, (member, side) in enumerate(blocks_of(segment)):
            values = []
            if side is None:
                at = pl.multiple_of(base + middle + jnp.right_shift(cls, 1) * HDIM, HDIM)
                for i in range(group):
                    tile = block_ref[member_of(segment, i, member), pl.ds(at, HDIM), :]
                    values.append(jnp.where(odd, swap(tile), tile)[:, :HDIM])
                shifted = [peak] * group
            else:
                count = visible // wide // 2
                for i in range(count):
                    at = pl.multiple_of(base + middle + (side * count + i) * HDIM, HDIM)
                    values.append(block_ref[member, pl.ds(at, HDIM), :])
                shifted = []
                for other in range(side * 4, side * 4 + 4):
                    apart = jnp.bitwise_and(other - cls, CLASSES - 1)
                    offset = jnp.where(jnp.bitwise_and(apart, 1) == 0, math.log(2.0), 0.0)
                    offset = jnp.where(apart == 4, math.log(3.0), offset)
                    shifted.append(peak - jnp.where(apart == 0, math.log(4.0), offset))
            weights = []
            for i, one in enumerate(shifted):
                at = j * size + i * rows
                score = score_ref[half, at : at + rows, :].reshape(rows // 8, 8, size)
                weights.append(jnp.exp(score - one[None]).reshape(rows, size).astype(jnp.bfloat16))
            values = jnp.concatenate(values, axis=1)
            values = jnp.concatenate([values, jnp.ones((16, size), jnp.bfloat16)], axis=0)
            mixed += dot(values, jnp.concatenate(weights, axis=0))
            yield
        results.append(mixed[:HDIM] / mixed[HDIM : HDIM + 1])
        yield

    def run(*streams):
        for _ in itertools.zip_longest(*streams):
            pass

    def body(turn, carry):
        results = []
        run(weight_steps(turn, 0, results), score_steps(turn, 1))
        after = jnp.minimum(turn + 1, turns - 1)
        run(weight_steps(turn, 1, results), score_steps(after, 0))
        unit, step = turn // pairs, turn % pairs
        for half, result in enumerate(results):
            twice = jnp.concatenate([result, result], axis=0).T.astype(jnp.bfloat16)
            at = pl.multiple_of((2 * step + half) * rows, rows)
            for i in range(group):
                out_ref[unit * group + i, pl.ds(at, rows), :] = twice[i * rows : (i + 1) * rows, :]
        return carry

    run(score_steps(0, 0))
    lax.fori_loop(0, turns, body, 0)


def spread_kernel(heads, capacity, segment_ref, block_ref, *refs):
    mixed_refs, (out_hbm, out_ref, sem) = refs[:-3], refs[-3:]
    visible = mixed_refs[0].shape[1]
    members = block_ref.shape[0]
    devices = out_ref.shape[0]
    group = SEG // visible
    slots = devices * capacity
    lines = visible // 128
    top = heads * visible + visible // 2
    units = [(ref, i) for ref in mixed_refs for i in range(ref.shape[0] // group)]
    step = math.gcd(slots, 256)
    low = lax.broadcasted_iota(jnp.int32, (step, 2 * HDIM), 1) < HDIM
    slot_of = {}

    def slot_row(u, i):
        if (u, i) not in slot_of:
            info = block_ref[segment_ref[u] * group + i, top : top + 16, :].astype(jnp.float32)
            place = (info[:lines] * capacity + info[lines : 2 * lines]).astype(jnp.int32)
            slot_of[u, i] = jnp.concatenate([place[j : j + 1] for j in range(lines)], axis=1)
        return slot_of[u, i]

    def spread(u, i, start):
        wanted = lax.broadcasted_iota(jnp.int32, (step, visible), 0) + start
        ref, unit = units[u]
        return dot(one_hot(wanted, slot_row(u, i)), ref[unit * group + i])

    for start in range(0, slots, step):
        owners = slice(start // capacity, (start + step) // capacity)
        for u in range(0, len(units), 2):
            base = u // 2 * group * capacity
            if u + 1 < len(units):
                pairs = [((u, i), (u + 1, i)) for i in range(group)]
            else:
                pairs = [((u, i), (u, i + group // 2)) for i in range(group // 2)]
            for i, (left, right) in enumerate(pairs):
                both = jnp.where(low, spread(*left, start), spread(*right, start)).astype(jnp.bfloat16)
                both = both.reshape(step // capacity, capacity, 2 * HDIM)
                out_ref[owners, base + i * capacity : base + (i + 1) * capacity, :] = both
    copy = pltpu.make_async_copy(out_ref, out_hbm, sem)
    copy.start()
    copy.wait()


def finish_kernel(parts, capacity, slot_ref, back_ref, rows_hbm, gain_ref, w_hbm, out_hbm,
                  attended_ref, rows_ref, w_ref, answer_ref, out_ref, more, sems):
    fetches = [
        pltpu.make_async_copy(w_hbm, w_ref, more.at[0]),
        pltpu.make_async_copy(rows_hbm, rows_ref, more.at[1]),
    ]
    for copy in fetches:
        copy.start()
    slots, count = attended_ref.shape[0], out_ref.shape[0]
    members = len(parts[0][2])
    groups = back_ref.shape[0] // members
    segments = 1 + max(segment for _, _, part in parts for _, units in part for _, segment in units)
    group = members // segments
    total = sum(len(part[0][1]) for _, _, part in parts)
    where = {}
    for member in range(members):
        u = 0
        for _, _, part in parts:
            heads, units = part[member]
            for place, segment in units:
                where[heads[place], segment] = member, u
                u += 1

    def piece(which, head, source):
        member, u = where[head, source // group]
        i, odd = source % group, u % 2
        if u + 1 == total and total % 2:
            i, odd = i % (group // 2), i // (group // 2)
        at = u // 2 * group * capacity + i * capacity
        return back_ref[which * members + member, at : at + capacity, :], odd

    for which in range(groups):
        for source in range(members):
            at = (which * members + source) * capacity
            for head in range(0, HEADS, 2):
                pair = piece(which, head, source) + piece(which, head + 1, source)
                attended_ref[at : at + capacity, head * HDIM : (head + 2) * HDIM] = place_pair(*pair)
    for copy in fetches:
        copy.wait()
    step = math.gcd(slots, 256)
    for start in range(0, slots, step):
        at = slice(start, start + step)
        hidden = rows_ref[at, :].astype(jnp.float32) + dot(attended_ref[at, :], w_ref[...])
        answer_ref[at, :] = layer_norm(hidden, gain_ref[...]).astype(jnp.bfloat16)
    step = math.gcd(count, 256)
    copies = []
    for start in range(0, count, step):
        here = lax.broadcasted_iota(jnp.int32, (step, slots), 1)
        chosen = one_hot(slot_ref[start : start + step, :], here)
        out_ref[start : start + step, :] = dot(chosen, answer_ref[...]).astype(jnp.bfloat16)
        copies.append(write(out_ref, out_hbm, start, step, sems))
    for copy in copies:
        copy.wait()


IN_VMEM = pl.BlockSpec(memory_space=pltpu.VMEM)
IN_HBM = pl.BlockSpec(memory_space=pltpu.HBM)
IN_SMEM = pl.BlockSpec(memory_space=pltpu.SMEM)
COPIES = pltpu.SemaphoreType.DMA


def call(kernel, outs, out_specs, name, *operands, in_specs=None, scratch=()):
    in_specs = in_specs or [IN_VMEM] * len(operands)
    operands = [
        pltpu.with_memory_space_constraint(operand, pltpu.HBM) if spec is IN_HBM else operand
        for operand, spec in zip(operands, in_specs)
    ]
    outs = jax.tree.map(
        lambda out, spec: pltpu.HBM(out.shape, out.dtype) if spec is IN_HBM else out, outs, out_specs
    )
    return pl.pallas_call(
        kernel,
        out_shape=outs,
        in_specs=in_specs,
        out_specs=out_specs,
        scratch_shapes=list(scratch),
        compiler_params=pltpu.CompilerParams(vmem_limit_bytes=VMEM),
        name=name,
    )(*operands)


def on_device(tiles, dest_table, owner_row, w_qkv, w_out, gain_attn, gain_out):
    groups = lax.axis_size("group")
    axes = ("group", "high", "low")
    inside = ("high", "low")
    members = lax.axis_size(inside)
    devices = groups * members
    count, width = tiles.shape
    visible = owner_row.shape[1]
    capacity = 2 * visible // devices
    slots = devices * capacity
    rows = visible // CLASSES
    segments = members * visible // SEG
    group = members // segments
    parts = parts_of(members, segments)
    bf16 = jnp.bfloat16

    moves = [(s * groups + g, g * members + s) for g in range(groups) for s in range(members)]
    owners = lax.ppermute(owner_row.reshape(visible // 128, 128), axes, moves).reshape(visible)
    owners = owners.reshape(rows, CLASSES).T.reshape(visible)

    outgoing, send_slot = call(
        functools.partial(pack_kernel, visible, capacity),
        (jax.ShapeDtypeStruct((slots, width), bf16), jax.ShapeDtypeStruct((1, count), jnp.int32)),
        (IN_HBM, IN_VMEM),
        "pack",
        dest_table.reshape(1, count),
        tiles,
        in_specs=[IN_VMEM, IN_HBM],
        scratch=[
            pltpu.VMEM((count, width), bf16),
            pltpu.VMEM((slots, width), bf16),
            COPIES,
            COPIES((slots // math.gcd(slots, 256),)),
        ],
    )
    arrived = lax.all_to_all(
        outgoing.reshape(devices, capacity, width), axes, split_axis=0, concat_axis=0, tiled=True
    ).reshape(slots, width)

    source = owners // count
    same = source[:, None] == source[None, :]
    earlier = owners[None, :] < owners[:, None]
    placed = jnp.sum((same & earlier).astype(jnp.int32), axis=1)
    slot = source * capacity + placed
    lines = visible // 128
    extra = jnp.concatenate([source.reshape(lines, 128), placed.reshape(lines, 128)])
    extra = jnp.pad(extra, ((0, 16 - 2 * lines), (0, 0))).astype(bf16)
    member = lax.axis_index(inside)
    tables = [
        jnp.array([list(zip(*units)) for _, units in part], jnp.int32)[member] for _, _, part in parts
    ]
    places = [table[0] for table in tables]
    sought = [table[1] for table in tables]
    every = jnp.concatenate(sought)
    slot, extra, places, sought, every = lax.optimization_barrier((slot, extra, places, sought, every))

    weights = (w_qkv, w_qkv[:, 2 * width :].T)
    mine = [member // group]
    blocks = []
    for i, part in enumerate(parts):
        first, last, dealt = part
        heads = len(dealt[0][0])
        depth = heads * visible + visible // 2 + (16 if i == 0 else 0)
        shape = jax.ShapeDtypeStruct((members, depth, 2 * HDIM), bf16)
        size = (last - first) * HDIM
        scratch = [
            pltpu.VMEM((2, width, size), bf16),
            pltpu.VMEM((size, width), bf16),
            pltpu.VMEM(shape.shape, bf16),
            pltpu.VMEM((visible, size), bf16),
            pltpu.VMEM((visible, size), bf16),
            pltpu.VMEM((size, visible), bf16),
            COPIES((members,)),
        ]
        segment = jnp.array(mine, jnp.int32)
        if i == 0:
            normed, send = call(
                functools.partial(first_kernel, part),
                (jax.ShapeDtypeStruct((visible, width), bf16), shape),
                (IN_HBM,) * 2,
                "project_first",
                segment,
                slot[:, None],
                extra,
                arrived,
                gain_attn[None, :],
                *weights,
                in_specs=[IN_SMEM] + [IN_VMEM] * 4 + [IN_HBM] * 2,
                scratch=scratch + [pltpu.VMEM((visible, width), bf16), COPIES((4,))],
            )
        else:
            send = call(
                functools.partial(next_kernel, part),
                shape,
                IN_HBM,
                "project_next",
                segment,
                normed,
                *weights,
                in_specs=[IN_SMEM, IN_VMEM] + [IN_HBM] * 2,
                scratch=scratch + [COPIES((3,))],
            )
        if blocks:
            blocks[-1], send = lax.optimization_barrier((blocks[-1], send))
        blocks.append(lax.all_to_all(send, inside, split_axis=0, concat_axis=0, tiled=True))

    mixed = []
    for (_, _, part), block, place, segment in zip(parts, blocks, places, sought):
        heads, units = len(part[0][0]), len(part[0][1])
        depth = SEG + (segments - 1) * SEG // CLASSES
        result = call(
            functools.partial(attend_kernel, visible, heads),
            jax.ShapeDtypeStruct((units * group, visible, 2 * HDIM), bf16),
            IN_VMEM,
            "attend",
            place,
            segment,
            block,
            in_specs=[IN_SMEM, IN_SMEM, IN_VMEM],
            scratch=[
                pltpu.VMEM((2, depth, SEG // CLASSES), jnp.float32),
                pltpu.VMEM((2, 8, SEG // CLASSES), jnp.float32),
            ],
        )
        mixed.append(result)

    heads = len(parts[0][2][0][0])
    shape = jax.ShapeDtypeStruct((devices, every.shape[0] * group * capacity // 2, 2 * HDIM), bf16)
    answers = call(
        functools.partial(spread_kernel, heads, capacity),
        shape,
        IN_HBM,
        "spread",
        every,
        blocks[0],
        *mixed,
        in_specs=[IN_SMEM] + [IN_VMEM] * (1 + len(mixed)),
        scratch=[pltpu.VMEM(shape.shape, bf16), COPIES],
    )
    back = lax.all_to_all(answers, axes, split_axis=0, concat_axis=0, tiled=True)
    return call(
        functools.partial(finish_kernel, parts, capacity),
        jax.ShapeDtypeStruct((count, width), bf16),
        IN_HBM,
        "finish",
        send_slot.reshape(count, 1),
        back,
        outgoing,
        gain_out[None, :],
        w_out,
        in_specs=[IN_VMEM, IN_VMEM, IN_HBM, IN_VMEM, IN_HBM],
        scratch=[
            pltpu.VMEM((slots, width), bf16),
            pltpu.VMEM((slots, width), bf16),
            pltpu.VMEM((width, width), bf16),
            pltpu.VMEM((slots, width), bf16),
            pltpu.VMEM((count, width), bf16),
            COPIES((2,)),
            COPIES((count // math.gcd(count, 256),)),
        ],
    )


def solution(mesh):
    n_seq, n_slide = mesh.shape["seq"], mesh.shape["slide"]
    split = Mesh(
        mesh.devices.reshape(n_slide, n_seq // n_slide, n_slide), ("group", "high", "low")
    )
    every = ("group", "high", "low")
    in_specs = (P(every, None), P(every), P("low", ("group", "high")), P(), P(), P(), P())
    return jax.shard_map(
        on_device, mesh=split, in_specs=in_specs, out_specs=P(every, None), check_vma=False
    )
```

```python
import functools
import itertools
import math

import jax
import jax.numpy as jnp
from jax import lax
from jax.experimental import pallas as pl
from jax.experimental.pallas import tpu as pltpu
from jax.sharding import Mesh
from jax.sharding import PartitionSpec as P

HEADS = 12
HDIM = 64
SEG = 2048
CLASSES = 8
EPS = 1e-05
VMEM = 24 << 20


def layer_norm(inputs, gain):
    average = jnp.mean(inputs, axis=-1, keepdims=True)
    centred = inputs - average
    spread = jnp.mean(centred * centred, axis=-1, keepdims=True)
    return centred * lax.rsqrt(spread + EPS) * gain


def one_hot(left, right):
    return jnp.where(left == right, 1.0, 0.0).astype(jnp.bfloat16)


def dot(left, right):
    return jnp.dot(left, right, preferred_element_type=jnp.float32)


def parts_of(members, segments):
    full = HEADS // members
    every = [(0, segment) for segment in range(segments)]
    parts = [
        (i * members, (i + 1) * members, [([i * members + member], every) for member in range(members)])
        for i in range(full)
    ]
    first = full * members
    owned = (HEADS - first) * segments // members
    if owned:
        dealt = []
        for member in range(members):
            units = [divmod(first * segments + member * owned + i, segments) for i in range(owned)]
            dealt.append((sorted({head for head, _ in units}), units))
        width = max(len(heads) for heads, _ in dealt)
        part = []
        for heads, units in dealt:
            units = [(heads.index(head), segment) for head, segment in units]
            part.append((heads + heads[-1:] * (width - len(heads)), units))
        parts.append((first, HEADS, part))
    return parts


def shares(part):
    held = [heads for heads, _ in part[2]]
    return len(held[0]) == 1 and len(held) % 2 == 0 and held[::2] == held[1::2]


def depth_of(part, visible):
    depth = len(part[2][0][0]) * visible + visible // 2
    return depth // 2 if shares(part) else depth


def place_pair(left, left_odd, right, right_odd):
    left = swap(left) if left_odd else left
    right = right if right_odd else swap(right)
    lanes = lax.broadcasted_iota(jnp.int32, left.shape, 1)
    return jnp.where(lanes < HDIM, left, right)


def swap(tile):
    return jnp.concatenate([tile[:, HDIM:], tile[:, :HDIM]], axis=1)


def column_of(row):
    pieces = [row[:, at : at + 128].astype(jnp.float32) for at in range(0, row.shape[1], 128)]
    pieces = [jnp.broadcast_to(piece, (8, 128)).T[:, :1] for piece in pieces]
    return jnp.concatenate(pieces, axis=0).astype(jnp.int32)


def member_index():
    return lax.axis_index("high") * lax.axis_size("low") + lax.axis_index("low")


def dealt_unit(segments, first, owned, i):
    start = member_index() * owned
    segment = lax.rem(start + i, segments)
    return lax.div(start + i, segments) - lax.div(start, segments), segment


def dot_nt(left, right):
    return lax.dot_general(left, right, (((1,), (1,)), ((), ())), preferred_element_type=jnp.float32)


def pack_kernel(visible, capacity, dest_ref, tiles_hbm, out_hbm, slot_ref, tiles_ref, out_ref, sem, sems):
    fetch = pltpu.make_async_copy(tiles_hbm, tiles_ref, sem)
    fetch.start()
    slots, _ = out_ref.shape
    count = dest_ref.shape[1]
    devices = slots // capacity
    target = jnp.right_shift(dest_ref[...], visible.bit_length() - 1)
    lanes = 128
    before = one_hot_lt(lanes)
    offset = jnp.zeros((devices, 1), jnp.float32)
    pieces = []
    for start in range(0, count, lanes):
        here = target[:, start : start + lanes]
        device = lax.broadcasted_iota(jnp.int32, (devices, lanes), 0)
        chosen = jnp.where(device == here, 1.0, 0.0)
        rank = dot(chosen.astype(jnp.bfloat16), before) + offset
        placed = jnp.sum(chosen * rank, axis=0, keepdims=True).astype(jnp.int32)
        pieces.append(jnp.where(here >= 0, here * capacity + placed, -1))
        offset = offset + jnp.sum(chosen, axis=1, keepdims=True)
    slot = jnp.concatenate(pieces, axis=1)
    slot_ref[...] = slot
    fetch.wait()
    step = math.gcd(slots, 256)
    copies = []
    for start in range(0, slots, step):
        wanted = lax.broadcasted_iota(jnp.int32, (step, count), 0) + start
        rows = dot(one_hot(wanted, slot), tiles_ref[...])
        out_ref[start : start + step, :] = rows.astype(jnp.bfloat16)
        copies.append(write(out_ref, out_hbm, start, step, sems))
    for copy in copies:
        copy.wait()


def write(source, target, start, step, sems):
    at = pl.ds(start, step)
    copy = pltpu.make_async_copy(source.at[at], target.at[at], sems.at[start // step])
    copy.start()
    return copy


def one_hot_lt(size):
    row = lax.broadcasted_iota(jnp.int32, (size, size), 0)
    column = lax.broadcasted_iota(jnp.int32, (size, size), 1)
    return jnp.where(row < column, 1.0, 0.0).astype(jnp.bfloat16)


def project_part(part, normed, extra, w_ref, wvt_ref, send_hbm, send_ref, q_ref, k_ref, vt_ref, sems):
    first, last, members = part
    visible, width = normed.shape
    rows, middle = visible // CLASSES, visible // 2
    wide = 2 * HDIM
    q_ref[...] = (dot(normed, w_ref[0]) * HDIM ** (-0.5)).astype(jnp.bfloat16)
    k_ref[...] = dot(normed, w_ref[1]).astype(jnp.bfloat16)
    vt_ref[...] = dot_nt(wvt_ref[...], normed).astype(jnp.bfloat16)

    def queries_of(head, cls):
        at = (head - first) // 2 * wide
        pair = [q_ref[(cls + i) * rows : (cls + i + 1) * rows, at : at + wide] for i in range(2)]
        return place_pair(pair[0], head % 2, pair[1], head % 2)

    for head in range(first, last):
        at, odd = (head - first) // 2 * wide, head % 2
        keys = place_pair(k_ref[:middle, at : at + wide], odd, k_ref[middle:, at : at + wide], odd)
        values = vt_ref[(head - first) * HDIM : (head - first + 1) * HDIM, :]
        for member, (heads, _) in enumerate(members):
            for place in [place for place, one in enumerate(heads) if one == head]:
                base = place * visible
                if not shares(part) or member % 2 == 0:
                    send_ref[member, base : base + middle, :] = keys
                if not shares(part) or member % 2 == 1:
                    base += 0 if shares(part) else middle
                    for i in range(visible // wide):
                        top = base + i * HDIM
                        send_ref[member, top : top + HDIM, :] = values[:, i * wide : (i + 1) * wide]
    copies = []
    for member, (heads, units) in enumerate(members):
        base, steps = len(heads) * visible, range(CLASSES // 2)
        if shares(part):
            steps = steps[member % 2 * CLASSES // 4 : (member % 2 + 1) * CLASSES // 4]
            base = middle - steps[0] * rows
        for i in steps:
            tile = queries_of(heads[0], 2 * i)
            for place, head in enumerate(heads[1:], 1):
                segment = lax.div(member_index(), SEG // visible)
                mine = functools.reduce(
                    jnp.logical_or, [segment == one for at, one in units if at == place], False
                )
                if head != heads[0]:
                    tile = jnp.where(mine, queries_of(head, 2 * i), tile)
            send_ref[member, base + i * rows : base + (i + 1) * rows, :] = tile
        if extra is not None:
            send_ref[member, depth_of(part, visible) :, :] = extra
        copies.append(write(send_ref, send_hbm, member, 1, sems))
    return copies


def fetch_weights(part, w_hbm, wvt_hbm, w_ref, wvt_ref, sems):
    width = w_hbm.shape[0]
    at, size = part[0] * HDIM, (part[1] - part[0]) * HDIM
    copies = [
        pltpu.make_async_copy(w_hbm.at[:, pl.ds(i * width + at, size)], w_ref.at[i], sems.at[i])
        for i in range(2)
    ]
    copies.append(pltpu.make_async_copy(wvt_hbm.at[pl.ds(at, size)], wvt_ref, sems.at[2]))
    for copy in copies:
        copy.start()
    return copies


def first_kernel(part, slot_ref, extra_ref, arrived_ref, gain_ref, w_hbm, wvt_hbm, normed_hbm, send_hbm,
                 w_ref, wvt_ref, send_ref, q_ref, k_ref, vt_ref, sems, normed_ref, more):
    weights = fetch_weights(part, w_hbm, wvt_hbm, w_ref, wvt_ref, more)
    visible, slots = normed_ref.shape[0], arrived_ref.shape[0]
    chosen = one_hot(lax.broadcasted_iota(jnp.int32, (visible, slots), 1), column_of(slot_ref[...]))
    rows = dot(chosen, arrived_ref[...])
    normed = layer_norm(rows, gain_ref[...]).astype(jnp.bfloat16)
    normed_ref[...] = normed
    copies = [pltpu.make_async_copy(normed_ref, normed_hbm, more.at[3])]
    for copy in copies:
        copy.start()
    for copy in weights:
        copy.wait()
    copies += project_part(
        part, normed, extra_ref[...], w_ref, wvt_ref, send_hbm, send_ref, q_ref, k_ref, vt_ref, sems
    )
    for copy in copies:
        copy.wait()


def next_kernel(part, normed_ref, w_hbm, wvt_hbm, send_hbm, w_ref, wvt_ref, send_ref, q_ref, k_ref, vt_ref, sems, more):
    for copy in fetch_weights(part, w_hbm, wvt_hbm, w_ref, wvt_ref, more):
        copy.wait()
    copies = project_part(
        part, normed_ref[...], None, w_ref, wvt_ref, send_hbm, send_ref, q_ref, k_ref, vt_ref, sems
    )
    for copy in copies:
        copy.wait()


def attend_kernel(visible, part, whole, staged, *refs):
    first, heads = part[0], len(part[2][0][0])
    block_ref, *refs = refs
    if shares(part):
        other_ref, *refs = refs
    result_ref, *refs = refs
    full_ref, own_ref = block_ref, block_ref
    if shares(part):
        *refs, full_ref = refs
    *infos, score_ref, peak_ref = refs[:-2] if staged else refs
    out_ref, sems = refs[-2:] if staged else (result_ref, None)
    for info_ref in infos:
        info_ref[...] = own_ref[:, depth_of(part, visible) :, :]
    if shares(part):
        odd_member = lax.rem(member_index(), 2)
        half, quarter = visible // 2, visible // 4
        for odd, (even_ref, odd_ref) in enumerate(((own_ref, other_ref), (other_ref, own_ref))):

            @pl.when(odd_member == odd)
            def _():
                full_ref[:, :half, :] = even_ref[:, :half, :]
                full_ref[:, half:visible, :] = odd_ref[:, :half, :]
                full_ref[:, visible : visible + quarter, :] = even_ref[:, half : half + quarter, :]
                full_ref[:, visible + quarter :, :] = odd_ref[:, half : half + quarter, :]

    block_ref = full_ref
    members = block_ref.shape[0]
    rows, middle = visible // CLASSES, visible // 2
    group = SEG // visible
    segments = members // group
    wide = 2 * HDIM
    size = group * rows
    pairs = CLASSES // 2
    turns = out_ref.shape[0] // group * pairs
    low = lax.broadcasted_iota(jnp.int32, (size, wide), 1) < HDIM

    def tile_of(turn, half):
        unit, step = turn // pairs, turn % pairs
        place, segment = (0, unit) if whole else dealt_unit(segments, first, turns // pairs, unit)
        return step, segment, 2 * step + half, pl.multiple_of(place * visible, visible)

    def member_of(segment, i, apart):
        return lax.rem(segment + apart, segments) * group + i

    def blocks_of(segment):
        near = [(member_of(segment, i, 0), side) for i in range(group) for side in range(2)]
        return near + [(apart, None) for apart in range(1, segments)]

    def score_steps(turn, half):
        step, segment, cls, base = tile_of(turn, half)
        top = pl.multiple_of(heads * visible + step * rows, rows)
        queries = jnp.concatenate(
            [block_ref[member_of(segment, i, 0), pl.ds(top, rows), :] for i in range(group)], axis=0
        )
        turned = swap(queries)
        none = jnp.zeros_like(queries)
        left = jnp.where(low, turned if half else queries, none)
        right = jnp.where(low, none, queries if half else turned)
        far = jnp.where(cls >= CLASSES // 2, right, left)
        peak = None
        for j, (member, side) in enumerate(blocks_of(segment)):
            if side is None:
                at = pl.multiple_of(base + jnp.bitwise_and(cls, CLASSES // 2 - 1) * rows, rows)
                keys = [block_ref[member_of(segment, i, member), pl.ds(at, rows), :] for i in range(group)]
                score = dot_nt(jnp.concatenate(keys, axis=0), far)
            else:
                score = dot_nt(block_ref[member, pl.ds(base, middle), :], right if side else left)
            score_ref[half, j * size : (j + 1) * size, :] = score
            highest = jnp.max(score.reshape(size // 8, 8, size), axis=0)
            peak = highest if peak is None else jnp.maximum(peak, highest)
            yield
        peak_ref[half] = jnp.broadcast_to(jnp.max(peak, axis=0, keepdims=True), peak.shape)
        yield

    def weight_steps(turn, half, results):
        step, segment, cls, base = tile_of(turn, half)
        peak = peak_ref[half]
        odd = jnp.bitwise_and(cls, 1) == 1
        mixed = jnp.zeros((HDIM + 16, size), jnp.float32)
        for j, (member, side) in enumerate(blocks_of(segment)):
            values = []
            if side is None:
                at = pl.multiple_of(base + middle + jnp.right_shift(cls, 1) * HDIM, HDIM)
                for i in range(group):
                    tile = block_ref[member_of(segment, i, member), pl.ds(at, HDIM), :]
                    values.append(jnp.where(odd, swap(tile), tile)[:, :HDIM])
                shifted = [peak] * group
            else:
                count = visible // wide // 2
                for i in range(count):
                    at = pl.multiple_of(base + middle + (side * count + i) * HDIM, HDIM)
                    values.append(block_ref[member, pl.ds(at, HDIM), :])
                shifted = []
                for other in range(side * 4, side * 4 + 4):
                    apart = jnp.bitwise_and(other - cls, CLASSES - 1)
                    offset = jnp.where(jnp.bitwise_and(apart, 1) == 0, math.log(2.0), 0.0)
                    offset = jnp.where(apart == 4, math.log(3.0), offset)
                    shifted.append(peak - jnp.where(apart == 0, math.log(4.0), offset))
            weights = []
            for i, one in enumerate(shifted):
                at = j * size + i * rows
                score = score_ref[half, at : at + rows, :].reshape(rows // 8, 8, size)
                weights.append(jnp.exp(score - one[None]).reshape(rows, size).astype(jnp.bfloat16))
            values = jnp.concatenate(values, axis=1)
            values = jnp.concatenate([values, jnp.ones((16, size), jnp.bfloat16)], axis=0)
            mixed += dot(values, jnp.concatenate(weights, axis=0))
            yield
        results.append(mixed[:HDIM] / mixed[HDIM : HDIM + 1])
        yield

    def run(*streams):
        for _ in itertools.zip_longest(*streams):
            pass

    def body(turn, carry):
        results = []
        run(weight_steps(turn, 0, results), score_steps(turn, 1))
        after = jnp.minimum(turn + 1, turns - 1)
        run(weight_steps(turn, 1, results), score_steps(after, 0))
        unit, step = turn // pairs, turn % pairs
        for half, result in enumerate(results):
            twice = jnp.concatenate([result, result], axis=0).T.astype(jnp.bfloat16)
            at = pl.multiple_of((2 * step + half) * rows, rows)
            for i in range(group):
                out_ref[unit * group + i, pl.ds(at, rows), :] = twice[i * rows : (i + 1) * rows, :]
        if staged:

            @pl.when(step == pairs - 1)
            def _():
                at = pl.ds(unit * group, group)
                pltpu.make_async_copy(out_ref.at[at], result_ref.at[at], sems.at[unit]).start()
        return carry

    run(score_steps(0, 0))
    lax.fori_loop(0, turns, body, 0)
    if staged:
        for unit in range(turns // pairs):
            at = pl.ds(unit * group, group)
            pltpu.make_async_copy(out_ref.at[at], result_ref.at[at], sems.at[unit]).wait()


def spread_kernel(capacity, fixed, info_ref, *refs):
    mixed_refs, (out_hbm, out_ref, sems) = refs[:-3], refs[-3:]
    visible = mixed_refs[0].shape[1]
    members = info_ref.shape[0]
    devices = out_ref.shape[0]
    group = SEG // visible
    segments = members // group
    slots = devices * capacity
    lines = visible // 128
    wide = 2 * HDIM
    units = [(ref, i) for ref in mixed_refs for i in range(ref.shape[0] // group)]
    step = math.gcd(slots, 256)
    low = lax.broadcasted_iota(jnp.int32, (step, wide), 1) < HDIM

    def slots_of(source):
        info = info_ref[source].astype(jnp.float32)
        place = (info[:lines] * capacity + info[lines : 2 * lines]).astype(jnp.int32)
        return jnp.concatenate([place[j : j + 1] for j in range(lines)], axis=1)

    def rows_of(u, i):
        ref, unit = units[u]
        return ref[unit * group + i]

    def segment_of(u):
        return dealt_unit(segments, 0, len(units) - fixed, u - fixed)[1]

    jobs = []
    if fixed:
        for segment in range(segments):
            for i in range(group):
                others = [u for u in range(len(units)) if u >= fixed]
                own = [u for u in range(fixed) if u % segments == segment]
                right = [rows_of(u, i) for u in own]
                right += [
                    jnp.where(segment_of(u) == segment, rows_of(u, i), jnp.zeros((visible, wide), jnp.bfloat16))
                    for u in others
                ]
                jobs.append((i, own + others, slots_of(segment * group + i), jnp.concatenate(right, axis=1)))
    else:
        for u in range(len(units)):
            for i in range(group):
                jobs.append((i, [u], slots_of(segment_of(u) * group + i), rows_of(u, i)))

    copies = []
    for start in range(0, slots, step):
        found = {}
        for i, names, place, right in jobs:
            wanted = lax.broadcasted_iota(jnp.int32, (step, visible), 0) + start
            result = dot(one_hot(wanted, place), right)
            for j, u in enumerate(names):
                piece = result[:, j * wide : (j + 1) * wide]
                found[u, i] = found[u, i] + piece if (u, i) in found else piece
        first, last = start // capacity, (start + step) // capacity
        for u in range(0, len(units), 2):
            base = u // 2 * group * capacity
            if u + 1 < len(units):
                pairs = [((u, i), (u + 1, i)) for i in range(group)]
            else:
                pairs = [((u, i), (u, i + group // 2)) for i in range(group // 2)]
            for i, (left, right) in enumerate(pairs):
                both = jnp.where(low, found[left], found[right]).astype(jnp.bfloat16)
                both = both.reshape(step // capacity, capacity, wide)
                out_ref[first:last, base + i * capacity : base + (i + 1) * capacity, :] = both
        copies.append(write(out_ref, out_hbm, first, last - first, sems))
    for copy in copies:
        copy.wait()


def finish_kernel(parts, capacity, slot_ref, back_ref, rows_hbm, gain_ref, w_hbm, out_hbm,
                  attended_ref, rows_ref, w_ref, answer_ref, out_ref, more, sems):
    fetches = [
        pltpu.make_async_copy(w_hbm, w_ref, more.at[0]),
        pltpu.make_async_copy(rows_hbm, rows_ref, more.at[1]),
    ]
    for copy in fetches:
        copy.start()
    slots, count = attended_ref.shape[0], out_ref.shape[0]
    members = len(parts[0][2])
    groups = back_ref.shape[0] // members
    segments = 1 + max(segment for _, _, part in parts for _, units in part for _, segment in units)
    group = members // segments
    total = sum(len(part[0][1]) for _, _, part in parts)
    where = {}
    for member in range(members):
        u = 0
        for _, _, part in parts:
            heads, units = part[member]
            for place, segment in units:
                where[heads[place], segment] = member, u
                u += 1

    def piece(which, head, source):
        member, u = where[head, source // group]
        i, odd = source % group, u % 2
        if u + 1 == total and total % 2:
            i, odd = i % (group // 2), i // (group // 2)
        at = u // 2 * group * capacity + i * capacity
        return back_ref[which * members + member, at : at + capacity, :], odd

    for which in range(groups):
        for source in range(members):
            at = (which * members + source) * capacity
            for head in range(0, HEADS, 2):
                pair = piece(which, head, source) + piece(which, head + 1, source)
                attended_ref[at : at + capacity, head * HDIM : (head + 2) * HDIM] = place_pair(*pair)
    for copy in fetches:
        copy.wait()
    step = math.gcd(slots, 256)
    for start in range(0, slots, step):
        at = slice(start, start + step)
        hidden = rows_ref[at, :].astype(jnp.float32) + dot(attended_ref[at, :], w_ref[...])
        answer_ref[at, :] = layer_norm(hidden, gain_ref[...]).astype(jnp.bfloat16)
    step = math.gcd(count, 256)
    copies = []
    for start in range(0, count, step):
        here = lax.broadcasted_iota(jnp.int32, (step, slots), 1)
        chosen = one_hot(column_of(slot_ref[:, start : start + step]), here)
        out_ref[start : start + step, :] = dot(chosen, answer_ref[...]).astype(jnp.bfloat16)
        copies.append(write(out_ref, out_hbm, start, step, sems))
    for copy in copies:
        copy.wait()


IN_VMEM = pl.BlockSpec(memory_space=pltpu.VMEM)
IN_HBM = pl.BlockSpec(memory_space=pltpu.HBM)
IN_SMEM = pl.BlockSpec(memory_space=pltpu.SMEM)
PINNED = pl.BlockSpec(memory_space=pltpu.VMEM)
SPACES = {id(IN_HBM): pltpu.HBM, id(PINNED): pltpu.VMEM}
COPIES = pltpu.SemaphoreType.DMA


def call(kernel, outs, out_specs, name, *operands, in_specs=None, scratch=()):
    in_specs = in_specs or [IN_VMEM] * len(operands)
    operands = [
        pltpu.with_memory_space_constraint(operand, SPACES[id(spec)]) if id(spec) in SPACES else operand
        for operand, spec in zip(operands, in_specs)
    ]
    outs = jax.tree.map(
        lambda out, spec: pltpu.HBM(out.shape, out.dtype) if spec is IN_HBM else out, outs, out_specs
    )
    return pl.pallas_call(
        kernel,
        out_shape=outs,
        in_specs=in_specs,
        out_specs=out_specs,
        scratch_shapes=[one for one in scratch if one is not None],
        compiler_params=pltpu.CompilerParams(vmem_limit_bytes=VMEM),
        name=name,
    )(*operands)


def on_device(tiles, dest_table, owner_row, w_qkv, w_out, gain_attn, gain_out):
    groups = lax.axis_size("group")
    axes = ("group", "high", "low")
    inside = ("high", "low")
    members = lax.axis_size(inside)
    devices = groups * members
    count, width = tiles.shape
    visible = owner_row.shape[1]
    capacity = 2 * visible // devices
    slots = devices * capacity
    rows = visible // CLASSES
    segments = members * visible // SEG
    group = members // segments
    parts = parts_of(members, segments)
    bf16 = jnp.bfloat16

    moves = [(s * groups + g, g * members + s) for g in range(groups) for s in range(members)]
    owners = lax.ppermute(owner_row.reshape(visible // 128, 128), axes, moves).reshape(visible)
    owners = owners.reshape(rows, CLASSES).T.reshape(visible)

    outgoing, send_slot = call(
        functools.partial(pack_kernel, visible, capacity),
        (jax.ShapeDtypeStruct((slots, width), bf16), jax.ShapeDtypeStruct((1, count), jnp.int32)),
        (IN_HBM, IN_VMEM),
        "pack",
        dest_table.reshape(1, count),
        tiles,
        in_specs=[IN_VMEM, IN_HBM],
        scratch=[
            pltpu.VMEM((count, width), bf16),
            pltpu.VMEM((slots, width), bf16),
            COPIES,
            COPIES((slots // math.gcd(slots, 256),)),
        ],
    )
    arrived = lax.all_to_all(
        outgoing.reshape(devices, capacity, width), axes, split_axis=0, concat_axis=0, tiled=True
    ).reshape(slots, width)

    source = owners // count
    same = source[:, None] == source[None, :]
    earlier = owners[None, :] < owners[:, None]
    placed = jnp.sum((same & earlier).astype(jnp.int32), axis=1)
    slot = source * capacity + placed
    lines = visible // 128
    extra = jnp.concatenate([source.reshape(lines, 128), placed.reshape(lines, 128)])
    extra = jnp.pad(extra, ((0, 16 - 2 * lines), (0, 0))).astype(bf16)
    weights = (w_qkv, w_qkv[:, 2 * width :].T)
    blocks = {}
    sequence = list(range(len(parts)))[::-1]
    for i in sequence:
        part = parts[i]
        first, last, dealt = part
        depth = depth_of(part, visible) + (16 if i == sequence[0] else 0)
        shape = jax.ShapeDtypeStruct((members, depth, 2 * HDIM), bf16)
        size = (last - first) * HDIM
        scratch = [
            pltpu.VMEM((2, width, size), bf16),
            pltpu.VMEM((size, width), bf16),
            pltpu.VMEM(shape.shape, bf16),
            pltpu.VMEM((visible, size), bf16),
            pltpu.VMEM((visible, size), bf16),
            pltpu.VMEM((size, visible), bf16),
            COPIES((members,)),
        ]
        if i == sequence[0]:
            normed, send = call(
                functools.partial(first_kernel, part),
                (jax.ShapeDtypeStruct((visible, width), bf16), shape),
                (IN_HBM,) * 2,
                "project_first",
                slot[None, :],
                extra,
                arrived,
                gain_attn[None, :],
                *weights,
                in_specs=[IN_VMEM] * 4 + [IN_HBM] * 2,
                scratch=scratch + [pltpu.VMEM((visible, width), bf16), COPIES((4,))],
            )
        else:
            send = call(
                functools.partial(next_kernel, part),
                shape,
                IN_HBM,
                "project_next",
                normed,
                *weights,
                in_specs=[IN_VMEM] + [IN_HBM] * 2,
                scratch=scratch + [COPIES((3,))],
            )
        if blocks:
            blocks[before], send = lax.optimization_barrier((blocks[before], send))
        blocks[i] = lax.all_to_all(send, inside, split_axis=0, concat_axis=0, tiled=True)
        before = i

    mixed, infos = {}, []
    for i in sequence:
        part = parts[i]
        units = len(part[2][0][1])
        depth = SEG + (segments - 1) * SEG // CLASSES
        outs = [jax.ShapeDtypeStruct((units * group, visible, 2 * HDIM), bf16)]
        staged = i != sequence[-1]
        if i == sequence[0]:
            outs.append(jax.ShapeDtypeStruct((members, 16, 2 * HDIM), bf16))
        operands = [blocks[i]]
        if shares(part):
            partners = [(member, member ^ 1) for member in range(members)]
            operands.append(lax.ppermute(blocks[i], inside, partners))
        mixed[i], *info = call(
            functools.partial(attend_kernel, visible, part, i < HEADS // members, staged),
            outs,
            [IN_HBM if staged else IN_VMEM] + [IN_VMEM] * (len(outs) - 1),
            "attend",
            *operands,
            scratch=[
                pltpu.VMEM((2, depth, SEG // CLASSES), jnp.float32),
                pltpu.VMEM((2, 8, SEG // CLASSES), jnp.float32),
                pltpu.VMEM(outs[0].shape, bf16) if staged else None,
                COPIES((units,)) if staged else None,
                pltpu.VMEM((members, visible + visible // 2, 2 * HDIM), bf16) if shares(part) else None,
            ],
        )
        infos += info
    mixed = [mixed[i] for i in range(len(parts))]

    fixed = HEADS // members * segments
    units_each = HEADS * segments // members
    shape = jax.ShapeDtypeStruct((devices, units_each * group * capacity // 2, 2 * HDIM), bf16)
    answers = call(
        functools.partial(spread_kernel, capacity, fixed),
        shape,
        IN_HBM,
        "spread",
        infos[0],
        *mixed,
        in_specs=[IN_VMEM] * (1 + len(mixed)),
        scratch=[pltpu.VMEM(shape.shape, bf16), COPIES((slots // math.gcd(slots, 256),))],
    )
    back = lax.all_to_all(answers, axes, split_axis=0, concat_axis=0, tiled=True)
    return call(
        functools.partial(finish_kernel, parts, capacity),
        jax.ShapeDtypeStruct((count, width), bf16),
        IN_HBM,
        "finish",
        send_slot,
        back,
        outgoing,
        gain_out[None, :],
        w_out,
        in_specs=[IN_VMEM, IN_VMEM, IN_HBM, IN_VMEM, IN_HBM],
        scratch=[
            pltpu.VMEM((slots, width), bf16),
            pltpu.VMEM((slots, width), bf16),
            pltpu.VMEM((width, width), bf16),
            pltpu.VMEM((slots, width), bf16),
            pltpu.VMEM((count, width), bf16),
            COPIES((2,)),
            COPIES((count // math.gcd(count, 256),)),
        ],
    )


def solution(mesh):
    n_seq, n_slide = mesh.shape["seq"], mesh.shape["slide"]
    split = Mesh(
        mesh.devices.reshape(n_slide, n_seq // n_slide, n_slide), ("group", "high", "low")
    )
    every = ("group", "high", "low")
    in_specs = (P(every, None), P(every), P("low", ("group", "high")), P(), P(), P(), P())
    return jax.shard_map(
        on_device, mesh=split, in_specs=in_specs, out_specs=P(every, None), check_vma=False
    )
```

```python
import functools
import itertools
import math

import jax
import jax.numpy as jnp
from jax import lax
from jax.experimental import pallas as pl
from jax.experimental.pallas import tpu as pltpu
from jax.sharding import Mesh
from jax.sharding import PartitionSpec as P

HEADS = 12
HDIM = 64
SEG = 2048
CLASSES = 8
EPS = 1e-05
VMEM = 24 << 20


def layer_norm(inputs, gain):
    average = jnp.mean(inputs, axis=-1, keepdims=True)
    centred = inputs - average
    spread = jnp.mean(centred * centred, axis=-1, keepdims=True)
    return centred * lax.rsqrt(spread + EPS) * gain


def one_hot(left, right):
    return jnp.where(left == right, 1.0, 0.0).astype(jnp.bfloat16)


def dot(left, right):
    return jnp.dot(left, right, preferred_element_type=jnp.float32)


def parts_of(members, segments):
    full = HEADS // members
    every = [(0, segment) for segment in range(segments)]
    parts = [
        (i * members, (i + 1) * members, [([i * members + member], every) for member in range(members)])
        for i in range(full)
    ]
    first = full * members
    owned = (HEADS - first) * segments // members
    if owned:
        dealt = []
        for member in range(members):
            units = [divmod(first * segments + member * owned + i, segments) for i in range(owned)]
            dealt.append((sorted({head for head, _ in units}), units))
        width = max(len(heads) for heads, _ in dealt)
        part = []
        for heads, units in dealt:
            units = [(heads.index(head), segment) for head, segment in units]
            part.append((heads + heads[-1:] * (width - len(heads)), units))
        parts.append((first, HEADS, part))
    return parts


def shares(part):
    held = [heads for heads, _ in part[2]]
    return len(held[0]) == 1 and len(held) % 2 == 0 and held[::2] == held[1::2]


def depth_of(part, visible):
    depth = len(part[2][0][0]) * visible + visible // 2
    return depth // 2 if shares(part) else depth


def place_pair(left, left_odd, right, right_odd):
    left = swap(left) if left_odd else left
    right = right if right_odd else swap(right)
    lanes = lax.broadcasted_iota(jnp.int32, left.shape, 1)
    return jnp.where(lanes < HDIM, left, right)


def swap(tile):
    return jnp.concatenate([tile[:, HDIM:], tile[:, :HDIM]], axis=1)


def column_of(row):
    pieces = [row[:, at : at + 128].astype(jnp.float32) for at in range(0, row.shape[1], 128)]
    pieces = [jnp.broadcast_to(piece, (8, 128)).T[:, :1] for piece in pieces]
    return jnp.concatenate(pieces, axis=0).astype(jnp.int32)


def member_index():
    return lax.axis_index("high") * lax.axis_size("low") + lax.axis_index("low")


def dealt_unit(segments, first, owned, i):
    start = member_index() * owned
    segment = lax.rem(start + i, segments)
    return lax.div(start + i, segments) - lax.div(start, segments), segment


def dot_nt(left, right):
    return lax.dot_general(left, right, (((1,), (1,)), ((), ())), preferred_element_type=jnp.float32)


def pack_kernel(visible, capacity, dest_ref, tiles_hbm, out_hbm, slot_ref, tiles_ref, out_ref, sem, sems):
    fetch = pltpu.make_async_copy(tiles_hbm, tiles_ref, sem)
    fetch.start()
    slots, _ = out_ref.shape
    count = dest_ref.shape[0] * 128
    devices = slots // capacity
    target = jnp.right_shift(dest_ref[...], visible.bit_length() - 1)
    lanes = 128
    before = one_hot_lt(lanes)
    offset = jnp.zeros((devices, 1), jnp.float32)
    pieces = []
    for start in range(0, count, lanes):
        here = target[start // lanes : start // lanes + 1, :]
        device = lax.broadcasted_iota(jnp.int32, (devices, lanes), 0)
        chosen = jnp.where(device == here, 1.0, 0.0)
        rank = dot(chosen.astype(jnp.bfloat16), before) + offset
        placed = jnp.sum(chosen * rank, axis=0, keepdims=True).astype(jnp.int32)
        pieces.append(jnp.where(here >= 0, here * capacity + placed, -1))
        offset = offset + jnp.sum(chosen, axis=1, keepdims=True)
    slot = jnp.concatenate(pieces, axis=1)
    slot_ref[...] = slot
    fetch.wait()
    step = math.gcd(slots, 256)
    copies = []
    for start in range(0, slots, step):
        wanted = lax.broadcasted_iota(jnp.int32, (step, count), 0) + start
        rows = dot(one_hot(wanted, slot), tiles_ref[...])
        out_ref[start : start + step, :] = rows.astype(jnp.bfloat16)
        copies.append(write(out_ref, out_hbm, start, step, sems))
    for copy in copies:
        copy.wait()


def write(source, target, start, step, sems):
    at = pl.ds(start, step)
    copy = pltpu.make_async_copy(source.at[at], target.at[at], sems.at[start // step])
    copy.start()
    return copy


def one_hot_lt(size):
    row = lax.broadcasted_iota(jnp.int32, (size, size), 0)
    column = lax.broadcasted_iota(jnp.int32, (size, size), 1)
    return jnp.where(row < column, 1.0, 0.0).astype(jnp.bfloat16)


def project_part(part, normed, extra, w_ref, wvt_ref, send_hbm, send_ref, q_ref, k_ref, vt_ref, sems):
    first, last, members = part
    visible, width = normed.shape
    rows, middle = visible // CLASSES, visible // 2
    wide = 2 * HDIM
    q_ref[...] = (dot(normed, w_ref[0]) * HDIM ** (-0.5)).astype(jnp.bfloat16)
    k_ref[...] = dot(normed, w_ref[1]).astype(jnp.bfloat16)
    vt_ref[...] = dot_nt(wvt_ref[...], normed).astype(jnp.bfloat16)

    def queries_of(head, cls):
        at = (head - first) // 2 * wide
        pair = [q_ref[(cls + i) * rows : (cls + i + 1) * rows, at : at + wide] for i in range(2)]
        return place_pair(pair[0], head % 2, pair[1], head % 2)

    for head in range(first, last):
        at, odd = (head - first) // 2 * wide, head % 2
        keys = place_pair(k_ref[:middle, at : at + wide], odd, k_ref[middle:, at : at + wide], odd)
        values = vt_ref[(head - first) * HDIM : (head - first + 1) * HDIM, :]
        for member, (heads, _) in enumerate(members):
            for place in [place for place, one in enumerate(heads) if one == head]:
                base = place * visible
                if not shares(part) or member % 2 == 0:
                    send_ref[member, base : base + middle, :] = keys
                if not shares(part) or member % 2 == 1:
                    base += 0 if shares(part) else middle
                    for i in range(visible // wide):
                        top = base + i * HDIM
                        send_ref[member, top : top + HDIM, :] = values[:, i * wide : (i + 1) * wide]
    copies = []
    for member, (heads, units) in enumerate(members):
        base, steps = len(heads) * visible, range(CLASSES // 2)
        if shares(part):
            steps = steps[member % 2 * CLASSES // 4 : (member % 2 + 1) * CLASSES // 4]
            base = middle - steps[0] * rows
        for i in steps:
            tile = queries_of(heads[0], 2 * i)
            for place, head in enumerate(heads[1:], 1):
                segment = lax.div(member_index(), SEG // visible)
                mine = functools.reduce(
                    jnp.logical_or, [segment == one for at, one in units if at == place], False
                )
                if head != heads[0]:
                    tile = jnp.where(mine, queries_of(head, 2 * i), tile)
            send_ref[member, base + i * rows : base + (i + 1) * rows, :] = tile
        if extra is not None:
            send_ref[member, depth_of(part, visible) :, :] = extra
        copies.append(write(send_ref, send_hbm, member, 1, sems))
    return copies


def fetch_weights(part, w_hbm, wvt_hbm, w_ref, wvt_ref, sems):
    width = w_hbm.shape[0]
    at, size = part[0] * HDIM, (part[1] - part[0]) * HDIM
    copies = [
        pltpu.make_async_copy(w_hbm.at[:, pl.ds(i * width + at, size)], w_ref.at[i], sems.at[i])
        for i in range(2)
    ]
    copies.append(pltpu.make_async_copy(wvt_hbm.at[pl.ds(at, size)], wvt_ref, sems.at[2]))
    for copy in copies:
        copy.start()
    return copies


def first_kernel(part, slot_ref, extra_ref, arrived_ref, gain_ref, w_hbm, wvt_hbm, normed_hbm, send_hbm,
                 w_ref, wvt_ref, send_ref, q_ref, k_ref, vt_ref, sems, normed_ref, more):
    weights = fetch_weights(part, w_hbm, wvt_hbm, w_ref, wvt_ref, more)
    visible, slots = normed_ref.shape[0], arrived_ref.shape[0]
    chosen = one_hot(lax.broadcasted_iota(jnp.int32, (visible, slots), 1), column_of(slot_ref[...]))
    rows = dot(chosen, arrived_ref[...])
    normed = layer_norm(rows, gain_ref[...]).astype(jnp.bfloat16)
    normed_ref[...] = normed
    copies = [pltpu.make_async_copy(normed_ref, normed_hbm, more.at[3])]
    for copy in copies:
        copy.start()
    for copy in weights:
        copy.wait()
    copies += project_part(
        part, normed, extra_ref[...], w_ref, wvt_ref, send_hbm, send_ref, q_ref, k_ref, vt_ref, sems
    )
    for copy in copies:
        copy.wait()


def next_kernel(part, normed_ref, w_hbm, wvt_hbm, send_hbm, w_ref, wvt_ref, send_ref, q_ref, k_ref, vt_ref, sems, more):
    for copy in fetch_weights(part, w_hbm, wvt_hbm, w_ref, wvt_ref, more):
        copy.wait()
    copies = project_part(
        part, normed_ref[...], None, w_ref, wvt_ref, send_hbm, send_ref, q_ref, k_ref, vt_ref, sems
    )
    for copy in copies:
        copy.wait()


def attend_kernel(visible, part, whole, *refs):
    first, heads = part[0], len(part[2][0][0])
    block_ref, *refs = refs
    if shares(part):
        other_ref, *refs = refs
    out_ref, *refs = refs
    full_ref, own_ref = block_ref, block_ref
    if shares(part):
        *refs, full_ref = refs
    *infos, score_ref, peak_ref = refs
    for info_ref in infos:
        info_ref[...] = own_ref[:, depth_of(part, visible) :, :]
    if shares(part):
        odd_member = lax.rem(member_index(), 2)
        half, quarter = visible // 2, visible // 4
        for odd, (even_ref, odd_ref) in enumerate(((own_ref, other_ref), (other_ref, own_ref))):

            @pl.when(odd_member == odd)
            def _():
                full_ref[:, :half, :] = even_ref[:, :half, :]
                full_ref[:, half:visible, :] = odd_ref[:, :half, :]
                full_ref[:, visible : visible + quarter, :] = even_ref[:, half : half + quarter, :]
                full_ref[:, visible + quarter :, :] = odd_ref[:, half : half + quarter, :]

    block_ref = full_ref
    members = block_ref.shape[0]
    rows, middle = visible // CLASSES, visible // 2
    group = SEG // visible
    segments = members // group
    wide = 2 * HDIM
    size = group * rows
    pairs = CLASSES // 2
    turns = out_ref.shape[0] // group * pairs
    low = lax.broadcasted_iota(jnp.int32, (size, wide), 1) < HDIM

    def tile_of(turn, half):
        unit, step = turn // pairs, turn % pairs
        place, segment = (0, unit) if whole else dealt_unit(segments, first, turns // pairs, unit)
        return step, segment, 2 * step + half, pl.multiple_of(place * visible, visible)

    def member_of(segment, i, apart):
        return lax.rem(segment + apart, segments) * group + i

    def blocks_of(segment):
        near = [(member_of(segment, i, 0), side) for i in range(group) for side in range(2)]
        return near + [(apart, None) for apart in range(1, segments)]

    def score_steps(turn, half):
        step, segment, cls, base = tile_of(turn, half)
        top = pl.multiple_of(heads * visible + step * rows, rows)
        queries = jnp.concatenate(
            [block_ref[member_of(segment, i, 0), pl.ds(top, rows), :] for i in range(group)], axis=0
        )
        turned = swap(queries)
        none = jnp.zeros_like(queries)
        left = jnp.where(low, turned if half else queries, none)
        right = jnp.where(low, none, queries if half else turned)
        far = jnp.where(cls >= CLASSES // 2, right, left)
        peak = None
        for j, (member, side) in enumerate(blocks_of(segment)):
            if side is None:
                at = pl.multiple_of(base + jnp.bitwise_and(cls, CLASSES // 2 - 1) * rows, rows)
                keys = [block_ref[member_of(segment, i, member), pl.ds(at, rows), :] for i in range(group)]
                score = dot_nt(jnp.concatenate(keys, axis=0), far)
            else:
                score = dot_nt(block_ref[member, pl.ds(base, middle), :], right if side else left)
            score_ref[half, j * size : (j + 1) * size, :] = score
            highest = jnp.max(score.reshape(size // 8, 8, size), axis=0)
            peak = highest if peak is None else jnp.maximum(peak, highest)
            yield
        peak_ref[half] = jnp.broadcast_to(jnp.max(peak, axis=0, keepdims=True), peak.shape)
        yield

    def weight_steps(turn, half, results):
        step, segment, cls, base = tile_of(turn, half)
        peak = peak_ref[half]
        odd = jnp.bitwise_and(cls, 1) == 1
        mixed = jnp.zeros((HDIM + 16, size), jnp.float32)
        for j, (member, side) in enumerate(blocks_of(segment)):
            values = []
            if side is None:
                at = pl.multiple_of(base + middle + jnp.right_shift(cls, 1) * HDIM, HDIM)
                for i in range(group):
                    tile = block_ref[member_of(segment, i, member), pl.ds(at, HDIM), :]
                    values.append(jnp.where(odd, swap(tile), tile)[:, :HDIM])
                shifted = [peak] * group
            else:
                count = visible // wide // 2
                for i in range(count):
                    at = pl.multiple_of(base + middle + (side * count + i) * HDIM, HDIM)
                    values.append(block_ref[member, pl.ds(at, HDIM), :])
                shifted = []
                for other in range(side * 4, side * 4 + 4):
                    apart = jnp.bitwise_and(other - cls, CLASSES - 1)
                    offset = jnp.where(jnp.bitwise_and(apart, 1) == 0, math.log(2.0), 0.0)
                    offset = jnp.where(apart == 4, math.log(3.0), offset)
                    shifted.append(peak - jnp.where(apart == 0, math.log(4.0), offset))
            weights = []
            for i, one in enumerate(shifted):
                at = j * size + i * rows
                score = score_ref[half, at : at + rows, :].reshape(rows // 8, 8, size)
                weights.append(jnp.exp(score - one[None]).reshape(rows, size).astype(jnp.bfloat16))
            values = jnp.concatenate(values, axis=1)
            values = jnp.concatenate([values, jnp.ones((16, size), jnp.bfloat16)], axis=0)
            mixed += dot(values, jnp.concatenate(weights, axis=0))
            yield
        results.append(mixed[:HDIM] / mixed[HDIM : HDIM + 1])
        yield

    def run(*streams):
        for _ in itertools.zip_longest(*streams):
            pass

    def body(turn, carry):
        results = []
        run(weight_steps(turn, 0, results), score_steps(turn, 1))
        after = jnp.minimum(turn + 1, turns - 1)
        run(weight_steps(turn, 1, results), score_steps(after, 0))
        unit, step = turn // pairs, turn % pairs
        for half, result in enumerate(results):
            twice = jnp.concatenate([result, result], axis=0).T.astype(jnp.bfloat16)
            at = pl.multiple_of((2 * step + half) * rows, rows)
            for i in range(group):
                out_ref[unit * group + i, pl.ds(at, rows), :] = twice[i * rows : (i + 1) * rows, :]
        return carry

    run(score_steps(0, 0))
    lax.fori_loop(0, turns, body, 0)


def spread_kernel(capacity, first, whole, info_ref, mixed_ref, out_hbm, out_ref, sems):
    visible = mixed_ref.shape[1]
    members = info_ref.shape[0]
    devices = out_ref.shape[0]
    group = SEG // visible
    segments = members // group
    slots = devices * capacity
    lines = visible // 128
    wide = 2 * HDIM
    units = range(mixed_ref.shape[0] // group)
    step = math.gcd(slots, 256)
    low = lax.broadcasted_iota(jnp.int32, (step, wide), 1) < HDIM
    jobs = []
    for u in units:
        segment = u if whole else dealt_unit(segments, first, len(units), u)[1]
        for i in range(group):
            info = info_ref[segment * group + i].astype(jnp.float32)
            place = (info[:lines] * capacity + info[lines : 2 * lines]).astype(jnp.int32)
            place = jnp.concatenate([place[j : j + 1] for j in range(lines)], axis=1)
            jobs.append((u, i, place, mixed_ref[u * group + i]))

    copies = []
    for start in range(0, slots, step):
        found = {}
        for u, i, place, right in jobs:
            wanted = lax.broadcasted_iota(jnp.int32, (step, visible), 0) + start
            found[u, i] = dot(one_hot(wanted, place), right)
        at, last = start // capacity, (start + step) // capacity
        for u in range(0, len(units), 2):
            base = u // 2 * group * capacity
            if u + 1 < len(units):
                pairs = [((u, i), (u + 1, i)) for i in range(group)]
            else:
                pairs = [((u, i), (u, i + group // 2)) for i in range(group // 2)]
            for i, (left, right) in enumerate(pairs):
                both = jnp.where(low, found[left], found[right]).astype(jnp.bfloat16)
                both = both.reshape(step // capacity, capacity, wide)
                out_ref[at:last, base + i * capacity : base + (i + 1) * capacity, :] = both
        copies.append(write(out_ref, out_hbm, at, last - at, sems))
    for copy in copies:
        copy.wait()


def finish_kernel(parts, capacity, slot_ref, rows_hbm, gain_ref, w_hbm, *refs):
    back_refs, refs = refs[: len(parts)], refs[len(parts) :]
    out_hbm, attended_ref, rows_ref, w_ref, answer_ref, out_ref, more, sems = refs
    fetches = [
        pltpu.make_async_copy(w_hbm, w_ref, more.at[0]),
        pltpu.make_async_copy(rows_hbm, rows_ref, more.at[1]),
    ]
    for copy in fetches:
        copy.start()
    slots, count = attended_ref.shape[0], out_ref.shape[0]
    members = len(parts[0][2])
    groups = back_refs[0].shape[0] // members
    segments = 1 + max(segment for _, _, part in parts for _, units in part for _, segment in units)
    group = members // segments
    where = {}
    for back_ref, (_, _, part) in zip(back_refs, parts):
        for member, (heads, units) in enumerate(part):
            for u, (place, segment) in enumerate(units):
                alone = u + 1 == len(units) and u % 2 == 0
                where[heads[place], segment] = back_ref, member, u, alone

    def piece(which, head, source):
        back_ref, member, u, alone = where[head, source // group]
        i, odd = source % group, u % 2
        if alone:
            i, odd = i % (group // 2), i // (group // 2)
        at = u // 2 * group * capacity + i * capacity
        return back_ref[which * members + member, at : at + capacity, :], odd

    for which in range(groups):
        for source in range(members):
            at = (which * members + source) * capacity
            for head in range(0, HEADS, 2):
                pair = piece(which, head, source) + piece(which, head + 1, source)
                attended_ref[at : at + capacity, head * HDIM : (head + 2) * HDIM] = place_pair(*pair)
    for copy in fetches:
        copy.wait()
    step = math.gcd(slots, 256)
    for start in range(0, slots, step):
        at = slice(start, start + step)
        hidden = rows_ref[at, :].astype(jnp.float32) + dot(attended_ref[at, :], w_ref[...])
        answer_ref[at, :] = layer_norm(hidden, gain_ref[...]).astype(jnp.bfloat16)
    step = math.gcd(count, 256)
    copies = []
    for start in range(0, count, step):
        here = lax.broadcasted_iota(jnp.int32, (step, slots), 1)
        chosen = one_hot(column_of(slot_ref[:, start : start + step]), here)
        out_ref[start : start + step, :] = dot(chosen, answer_ref[...]).astype(jnp.bfloat16)
        copies.append(write(out_ref, out_hbm, start, step, sems))
    for copy in copies:
        copy.wait()


IN_VMEM = pl.BlockSpec(memory_space=pltpu.VMEM)
IN_HBM = pl.BlockSpec(memory_space=pltpu.HBM)
IN_SMEM = pl.BlockSpec(memory_space=pltpu.SMEM)
PINNED = pl.BlockSpec(memory_space=pltpu.VMEM)
SPACES = {id(IN_HBM): pltpu.HBM, id(PINNED): pltpu.VMEM}
COPIES = pltpu.SemaphoreType.DMA


def call(kernel, outs, out_specs, name, *operands, in_specs=None, scratch=()):
    in_specs = in_specs or [IN_VMEM] * len(operands)
    operands = [
        pltpu.with_memory_space_constraint(operand, SPACES[id(spec)]) if id(spec) in SPACES else operand
        for operand, spec in zip(operands, in_specs)
    ]
    outs = jax.tree.map(
        lambda out, spec: pltpu.HBM(out.shape, out.dtype) if spec is IN_HBM else out, outs, out_specs
    )
    return pl.pallas_call(
        kernel,
        out_shape=outs,
        in_specs=in_specs,
        out_specs=out_specs,
        scratch_shapes=[one for one in scratch if one is not None],
        compiler_params=pltpu.CompilerParams(vmem_limit_bytes=VMEM),
        name=name,
    )(*operands)


def on_device(tiles, dest_table, owner_row, w_qkv, w_out, gain_attn, gain_out):
    groups = lax.axis_size("group")
    axes = ("group", "high", "low")
    inside = ("high", "low")
    members = lax.axis_size(inside)
    devices = groups * members
    count, width = tiles.shape
    visible = owner_row.shape[1]
    capacity = 2 * visible // devices
    slots = devices * capacity
    rows = visible // CLASSES
    segments = members * visible // SEG
    group = members // segments
    parts = parts_of(members, segments)
    bf16 = jnp.bfloat16

    moves = [(s * groups + g, g * members + s) for g in range(groups) for s in range(members)]
    owners = lax.ppermute(owner_row.reshape(visible // 128, 128), axes, moves).reshape(visible)
    owners = owners.reshape(rows, CLASSES).T.reshape(visible)

    outgoing, send_slot = call(
        functools.partial(pack_kernel, visible, capacity),
        (jax.ShapeDtypeStruct((slots, width), bf16), jax.ShapeDtypeStruct((1, count), jnp.int32)),
        (IN_HBM, IN_VMEM),
        "pack",
        dest_table.reshape(count // 128, 128),
        tiles,
        in_specs=[IN_VMEM, IN_HBM],
        scratch=[
            pltpu.VMEM((count, width), bf16),
            pltpu.VMEM((slots, width), bf16),
            COPIES,
            COPIES((slots // math.gcd(slots, 256),)),
        ],
    )
    arrived = lax.all_to_all(
        outgoing.reshape(devices, capacity, width), axes, split_axis=0, concat_axis=0, tiled=True
    ).reshape(slots, width)

    source = owners // count
    same = source[:, None] == source[None, :]
    earlier = owners[None, :] < owners[:, None]
    placed = jnp.sum((same & earlier).astype(jnp.int32), axis=1)
    slot = source * capacity + placed
    lines = visible // 128
    extra = jnp.concatenate([source.reshape(lines, 128), placed.reshape(lines, 128)])
    extra = jnp.pad(extra, ((0, 16 - 2 * lines), (0, 0))).astype(bf16)
    weights = (w_qkv, w_qkv[:, 2 * width :].T)
    blocks = {}
    sequence = list(range(len(parts)))[::-1]
    for i in sequence:
        part = parts[i]
        first, last, dealt = part
        depth = depth_of(part, visible) + (16 if i == sequence[0] else 0)
        shape = jax.ShapeDtypeStruct((members, depth, 2 * HDIM), bf16)
        size = (last - first) * HDIM
        scratch = [
            pltpu.VMEM((2, width, size), bf16),
            pltpu.VMEM((size, width), bf16),
            pltpu.VMEM(shape.shape, bf16),
            pltpu.VMEM((visible, size), bf16),
            pltpu.VMEM((visible, size), bf16),
            pltpu.VMEM((size, visible), bf16),
            COPIES((members,)),
        ]
        if i == sequence[0]:
            normed, send = call(
                functools.partial(first_kernel, part),
                (jax.ShapeDtypeStruct((visible, width), bf16), shape),
                (IN_HBM,) * 2,
                "project_first",
                slot[None, :],
                extra,
                arrived,
                gain_attn[None, :],
                *weights,
                in_specs=[IN_VMEM] * 4 + [IN_HBM] * 2,
                scratch=scratch + [pltpu.VMEM((visible, width), bf16), COPIES((4,))],
            )
        else:
            send = call(
                functools.partial(next_kernel, part),
                shape,
                IN_HBM,
                "project_next",
                normed,
                *weights,
                in_specs=[IN_VMEM] + [IN_HBM] * 2,
                scratch=scratch + [COPIES((3,))],
            )
        if blocks:
            blocks[before], send = lax.optimization_barrier((blocks[before], send))
        blocks[i] = lax.all_to_all(send, inside, split_axis=0, concat_axis=0, tiled=True)
        before = i

    backs, infos = {}, []
    for i in sequence:
        part = parts[i]
        units = len(part[2][0][1])
        depth = SEG + (segments - 1) * SEG // CLASSES
        outs = [jax.ShapeDtypeStruct((units * group, visible, 2 * HDIM), bf16)]
        staged = i != sequence[-1]
        if i == sequence[0]:
            outs.append(jax.ShapeDtypeStruct((members, 16, 2 * HDIM), bf16))
        operands = [blocks[i]]
        if shares(part):
            partners = [(member, member ^ 1) for member in range(members)]
            operands.append(lax.ppermute(blocks[i], inside, partners))
        mixed, *info = call(
            functools.partial(attend_kernel, visible, part, i < HEADS // members),
            outs,
            [IN_VMEM] * len(outs),
            "attend",
            *operands,
            scratch=[
                pltpu.VMEM((2, depth, SEG // CLASSES), jnp.float32),
                pltpu.VMEM((2, 8, SEG // CLASSES), jnp.float32),
                pltpu.VMEM((members, visible + visible // 2, 2 * HDIM), bf16) if shares(part) else None,
            ],
        )
        infos += info
        shape = jax.ShapeDtypeStruct((devices, units * group * capacity // 2, 2 * HDIM), bf16)
        answers = call(
            functools.partial(spread_kernel, capacity, part[0], i < HEADS // members),
            shape,
            IN_HBM,
            "spread",
            infos[0],
            mixed,
            scratch=[pltpu.VMEM(shape.shape, bf16), COPIES((slots // math.gcd(slots, 256),))],
        )
        if staged:
            after = sequence[sequence.index(i) + 1]
            blocks[after], answers, infos[0] = lax.optimization_barrier((blocks[after], answers, infos[0]))
        backs[i] = lax.all_to_all(answers, axes, split_axis=0, concat_axis=0, tiled=True)
    backs = [backs[i] for i in range(len(parts))]

    return call(
        functools.partial(finish_kernel, parts, capacity),
        jax.ShapeDtypeStruct((count, width), bf16),
        IN_HBM,
        "finish",
        send_slot,
        outgoing,
        gain_out[None, :],
        w_out,
        *backs,
        in_specs=[IN_VMEM, IN_HBM, IN_VMEM, IN_HBM] + [IN_VMEM] * len(backs),
        scratch=[
            pltpu.VMEM((slots, width), bf16),
            pltpu.VMEM((slots, width), bf16),
            pltpu.VMEM((width, width), bf16),
            pltpu.VMEM((slots, width), bf16),
            pltpu.VMEM((count, width), bf16),
            COPIES((2,)),
            COPIES((count // math.gcd(count, 256),)),
        ],
    )


def solution(mesh):
    n_seq, n_slide = mesh.shape["seq"], mesh.shape["slide"]
    split = Mesh(
        mesh.devices.reshape(n_slide, n_seq // n_slide, n_slide), ("group", "high", "low")
    )
    every = ("group", "high", "low")
    in_specs = (P(every, None), P(every), P("low", ("group", "high")), P(), P(), P(), P())
    return jax.shard_map(
        on_device, mesh=split, in_specs=in_specs, out_specs=P(every, None), check_vma=False
    )
```

```python
import functools
import itertools
import math

import jax
import jax.numpy as jnp
from jax import lax
from jax.experimental import pallas as pl
from jax.experimental.pallas import tpu as pltpu
from jax.sharding import Mesh
from jax.sharding import PartitionSpec as P

HEADS = 12
HDIM = 64
SEG = 2048
CLASSES = 8
EPS = 1e-05
VMEM = 24 << 20


def layer_norm(inputs, gain):
    average = jnp.mean(inputs, axis=-1, keepdims=True)
    centred = inputs - average
    spread = jnp.mean(centred * centred, axis=-1, keepdims=True)
    return centred * lax.rsqrt(spread + EPS) * gain


def one_hot(left, right):
    return jnp.where(left == right, 1.0, 0.0).astype(jnp.bfloat16)


def dot(left, right):
    return jnp.dot(left, right, preferred_element_type=jnp.float32)


def parts_of(members, segments):
    full = HEADS // members
    every = [(0, segment) for segment in range(segments)]
    parts = [
        (i * members, (i + 1) * members, [([i * members + member], every) for member in range(members)])
        for i in range(full)
    ]
    first = full * members
    owned = (HEADS - first) * segments // members
    if owned:
        dealt = []
        for member in range(members):
            units = [divmod(first * segments + member * owned + i, segments) for i in range(owned)]
            dealt.append((sorted({head for head, _ in units}), units))
        width = max(len(heads) for heads, _ in dealt)
        part = []
        for heads, units in dealt:
            units = [(heads.index(head), segment) for head, segment in units]
            part.append((heads + heads[-1:] * (width - len(heads)), units))
        parts.append((first, HEADS, part))
    return parts


def shares(part):
    held = [heads for heads, _ in part[2]]
    return len(held[0]) == 1 and len(held) % 2 == 0 and held[::2] == held[1::2]


def depth_of(part, visible):
    depth = len(part[2][0][0]) * visible + visible // 2
    return depth // 2 if shares(part) else depth


def place_pair(left, left_odd, right, right_odd):
    left = swap(left) if left_odd else left
    right = right if right_odd else swap(right)
    lanes = lax.broadcasted_iota(jnp.int32, left.shape, 1)
    return jnp.where(lanes < HDIM, left, right)


def swap(tile):
    return jnp.concatenate([tile[:, HDIM:], tile[:, :HDIM]], axis=1)


def column_of(row):
    pieces = [row[:, at : at + 128].astype(jnp.float32) for at in range(0, row.shape[1], 128)]
    pieces = [jnp.broadcast_to(piece, (8, 128)).T[:, :1] for piece in pieces]
    return jnp.concatenate(pieces, axis=0).astype(jnp.int32)


def member_index():
    return lax.axis_index("high") * lax.axis_size("low") + lax.axis_index("low")


def dealt_unit(segments, first, owned, i):
    start = member_index() * owned
    segment = lax.rem(start + i, segments)
    return lax.div(start + i, segments) - lax.div(start, segments), segment


def dot_nt(left, right):
    return lax.dot_general(left, right, (((1,), (1,)), ((), ())), preferred_element_type=jnp.float32)


def pack_kernel(visible, capacity, dest_hbm, tiles_hbm, out_hbm, slot_ref, dest_ref, tiles_ref, out_ref, more, sems):
    width = tiles_ref.shape[1]
    spans = [(0, width // 3), (width // 3, width)]
    table = pltpu.make_async_copy(dest_hbm, dest_ref, more.at[0])
    fetches = [
        pltpu.make_async_copy(
            tiles_hbm.at[:, pl.ds(low, high - low)], tiles_ref.at[:, pl.ds(low, high - low)], more.at[1 + i]
        )
        for i, (low, high) in enumerate(spans)
    ]
    for copy in [table, *fetches]:
        copy.start()
    slots, _ = out_ref.shape
    count = dest_ref.shape[0] * 128
    devices = slots // capacity
    table.wait()
    target = jnp.right_shift(dest_ref[...], visible.bit_length() - 1)
    lanes = 128
    before = one_hot_lt(lanes)
    offset = jnp.zeros((devices, 1), jnp.float32)
    pieces = []
    for start in range(0, count, lanes):
        here = target[start // lanes : start // lanes + 1, :]
        device = lax.broadcasted_iota(jnp.int32, (devices, lanes), 0)
        chosen = jnp.where(device == here, 1.0, 0.0)
        rank = dot(chosen.astype(jnp.bfloat16), before) + offset
        placed = jnp.sum(chosen * rank, axis=0, keepdims=True).astype(jnp.int32)
        pieces.append(jnp.where(here >= 0, here * capacity + placed, -1))
        offset = offset + jnp.sum(chosen, axis=1, keepdims=True)
    slot = jnp.concatenate(pieces, axis=1)
    slot_ref[...] = slot
    step = math.gcd(slots, 256)
    copies = []
    for fetch, (low, high) in zip(fetches, spans):
        fetch.wait()
        for start in range(0, slots, step):
            wanted = lax.broadcasted_iota(jnp.int32, (step, count), 0) + start
            rows = dot(one_hot(wanted, slot), tiles_ref[:, low:high])
            out_ref[start : start + step, low:high] = rows.astype(jnp.bfloat16)
            if high == width:
                copies.append(write(out_ref, out_hbm, start, step, sems))
    for copy in copies:
        copy.wait()


def write(source, target, start, step, sems):
    at = pl.ds(start, step)
    copy = pltpu.make_async_copy(source.at[at], target.at[at], sems.at[start // step])
    copy.start()
    return copy


def one_hot_lt(size):
    row = lax.broadcasted_iota(jnp.int32, (size, size), 0)
    column = lax.broadcasted_iota(jnp.int32, (size, size), 1)
    return jnp.where(row < column, 1.0, 0.0).astype(jnp.bfloat16)


def project_part(part, normed, extra, w_ref, wvt_ref, send_hbm, send_ref, q_ref, k_ref, vt_ref, sems):
    first, last, members = part
    visible, width = normed.shape
    rows, middle = visible // CLASSES, visible // 2
    wide = 2 * HDIM
    q_ref[...] = (dot(normed, w_ref[0]) * HDIM ** (-0.5)).astype(jnp.bfloat16)
    k_ref[...] = dot(normed, w_ref[1]).astype(jnp.bfloat16)
    vt_ref[...] = dot_nt(wvt_ref[...], normed).astype(jnp.bfloat16)

    def queries_of(head, cls):
        at = (head - first) // 2 * wide
        pair = [q_ref[(cls + i) * rows : (cls + i + 1) * rows, at : at + wide] for i in range(2)]
        return place_pair(pair[0], head % 2, pair[1], head % 2)

    for head in range(first, last):
        at, odd = (head - first) // 2 * wide, head % 2
        keys = place_pair(k_ref[:middle, at : at + wide], odd, k_ref[middle:, at : at + wide], odd)
        values = vt_ref[(head - first) * HDIM : (head - first + 1) * HDIM, :]
        for member, (heads, _) in enumerate(members):
            for place in [place for place, one in enumerate(heads) if one == head]:
                base = place * visible
                if not shares(part) or member % 2 == 0:
                    send_ref[member, base : base + middle, :] = keys
                if not shares(part) or member % 2 == 1:
                    base += 0 if shares(part) else middle
                    for i in range(visible // wide):
                        top = base + i * HDIM
                        send_ref[member, top : top + HDIM, :] = values[:, i * wide : (i + 1) * wide]
    copies = []
    for member, (heads, units) in enumerate(members):
        base, steps = len(heads) * visible, range(CLASSES // 2)
        if shares(part):
            steps = steps[member % 2 * CLASSES // 4 : (member % 2 + 1) * CLASSES // 4]
            base = middle - steps[0] * rows
        for i in steps:
            tile = queries_of(heads[0], 2 * i)
            for place, head in enumerate(heads[1:], 1):
                segment = lax.div(member_index(), SEG // visible)
                mine = functools.reduce(
                    jnp.logical_or, [segment == one for at, one in units if at == place], False
                )
                if head != heads[0]:
                    tile = jnp.where(mine, queries_of(head, 2 * i), tile)
            send_ref[member, base + i * rows : base + (i + 1) * rows, :] = tile
        if extra is not None:
            send_ref[member, depth_of(part, visible) :, :] = extra
        copies.append(write(send_ref, send_hbm, member, 1, sems))
    return copies


def fetch_weights(part, w_hbm, wvt_hbm, w_ref, wvt_ref, sems):
    width = w_hbm.shape[0]
    at, size = part[0] * HDIM, (part[1] - part[0]) * HDIM
    copies = [
        pltpu.make_async_copy(w_hbm.at[:, pl.ds(i * width + at, size)], w_ref.at[i], sems.at[i])
        for i in range(2)
    ]
    copies.append(pltpu.make_async_copy(wvt_hbm.at[pl.ds(at, size)], wvt_ref, sems.at[2]))
    for copy in copies:
        copy.start()
    return copies


def first_kernel(part, slot_ref, extra_ref, arrived_ref, gain_ref, w_hbm, wvt_hbm, normed_hbm, send_hbm,
                 w_ref, wvt_ref, send_ref, q_ref, k_ref, vt_ref, sems, normed_ref, more):
    weights = fetch_weights(part, w_hbm, wvt_hbm, w_ref, wvt_ref, more)
    visible, slots = normed_ref.shape[0], arrived_ref.shape[0]
    chosen = one_hot(lax.broadcasted_iota(jnp.int32, (visible, slots), 1), column_of(slot_ref[...]))
    rows = dot(chosen, arrived_ref[...])
    normed = layer_norm(rows, gain_ref[...]).astype(jnp.bfloat16)
    normed_ref[...] = normed
    copies = [pltpu.make_async_copy(normed_ref, normed_hbm, more.at[3])]
    for copy in copies:
        copy.start()
    for copy in weights:
        copy.wait()
    copies += project_part(
        part, normed, extra_ref[...], w_ref, wvt_ref, send_hbm, send_ref, q_ref, k_ref, vt_ref, sems
    )
    for copy in copies:
        copy.wait()


def next_kernel(part, normed_ref, w_hbm, wvt_hbm, send_hbm, w_ref, wvt_ref, send_ref, q_ref, k_ref, vt_ref, sems, more):
    for copy in fetch_weights(part, w_hbm, wvt_hbm, w_ref, wvt_ref, more):
        copy.wait()
    copies = project_part(
        part, normed_ref[...], None, w_ref, wvt_ref, send_hbm, send_ref, q_ref, k_ref, vt_ref, sems
    )
    for copy in copies:
        copy.wait()


def attend_kernel(visible, part, whole, *refs):
    first, heads = part[0], len(part[2][0][0])
    block_ref, *refs = refs
    if shares(part):
        other_ref, *refs = refs
    out_ref, *refs = refs
    full_ref, own_ref = block_ref, block_ref
    if shares(part):
        *refs, full_ref = refs
    *infos, score_ref, peak_ref, mixed_ref = refs
    for info_ref in infos:
        info_ref[...] = own_ref[:, depth_of(part, visible) :, :]
    if shares(part):
        odd_member = lax.rem(member_index(), 2)
        half, quarter = visible // 2, visible // 4
        for odd, (even_ref, odd_ref) in enumerate(((own_ref, other_ref), (other_ref, own_ref))):

            @pl.when(odd_member == odd)
            def _():
                full_ref[:, :half, :] = even_ref[:, :half, :]
                full_ref[:, half:visible, :] = odd_ref[:, :half, :]
                full_ref[:, visible : visible + quarter, :] = even_ref[:, half : half + quarter, :]
                full_ref[:, visible + quarter :, :] = odd_ref[:, half : half + quarter, :]

    block_ref = full_ref
    members = block_ref.shape[0]
    rows, middle = visible // CLASSES, visible // 2
    group = SEG // visible
    segments = members // group
    wide = 2 * HDIM
    size = group * rows
    pairs = CLASSES // 2
    turns = out_ref.shape[0] // group * pairs
    low = lax.broadcasted_iota(jnp.int32, (size, wide), 1) < HDIM

    def tile_of(turn, half):
        unit, step = turn // pairs, turn % pairs
        place, segment = (0, unit) if whole else dealt_unit(segments, first, turns // pairs, unit)
        return step, segment, 2 * step + half, pl.multiple_of(place * visible, visible)

    def member_of(segment, i, apart):
        return lax.rem(segment + apart, segments) * group + i

    def blocks_of(segment):
        near = [(member_of(segment, i, 0), side) for i in range(group) for side in range(2)]
        return near + [(apart, None) for apart in range(1, segments)]

    def score_steps(turn, half):
        step, segment, cls, base = tile_of(turn, half)
        top = pl.multiple_of(heads * visible + step * rows, rows)
        queries = jnp.concatenate(
            [block_ref[member_of(segment, i, 0), pl.ds(top, rows), :] for i in range(group)], axis=0
        )
        turned = swap(queries)
        none = jnp.zeros_like(queries)
        left = jnp.where(low, turned if half else queries, none)
        right = jnp.where(low, none, queries if half else turned)
        far = jnp.where(cls >= CLASSES // 2, right, left)
        peak = None
        for j, (member, side) in enumerate(blocks_of(segment)):
            if side is None:
                at = pl.multiple_of(base + jnp.bitwise_and(cls, CLASSES // 2 - 1) * rows, rows)
                keys = [block_ref[member_of(segment, i, member), pl.ds(at, rows), :] for i in range(group)]
                score = dot_nt(jnp.concatenate(keys, axis=0), far)
            else:
                score = dot_nt(block_ref[member, pl.ds(base, middle), :], right if side else left)
            score_ref[half, j * size : (j + 1) * size, :] = score
            highest = jnp.max(score.reshape(size // 8, 8, size), axis=0)
            peak = highest if peak is None else jnp.maximum(peak, highest)
            yield
        peak_ref[half] = jnp.broadcast_to(jnp.max(peak, axis=0, keepdims=True), peak.shape)
        yield

    def weight_steps(turn, half):
        step, segment, cls, base = tile_of(turn, half)
        peak = peak_ref[half]
        odd = jnp.bitwise_and(cls, 1) == 1
        mixed = jnp.zeros((HDIM + 16, size), jnp.float32)
        for j, (member, side) in enumerate(blocks_of(segment)):
            values = []
            if side is None:
                at = pl.multiple_of(base + middle + jnp.right_shift(cls, 1) * HDIM, HDIM)
                for i in range(group):
                    tile = block_ref[member_of(segment, i, member), pl.ds(at, HDIM), :]
                    values.append(jnp.where(odd, swap(tile), tile)[:, :HDIM])
                shifted = [peak] * group
            else:
                count = visible // wide // 2
                for i in range(count):
                    at = pl.multiple_of(base + middle + (side * count + i) * HDIM, HDIM)
                    values.append(block_ref[member, pl.ds(at, HDIM), :])
                shifted = []
                for other in range(side * 4, side * 4 + 4):
                    apart = jnp.bitwise_and(other - cls, CLASSES - 1)
                    offset = jnp.where(jnp.bitwise_and(apart, 1) == 0, math.log(2.0), 0.0)
                    offset = jnp.where(apart == 4, math.log(3.0), offset)
                    shifted.append(peak - jnp.where(apart == 0, math.log(4.0), offset))
            weights = []
            for i, one in enumerate(shifted):
                at = j * size + i * rows
                score = score_ref[half, at : at + rows, :].reshape(rows // 8, 8, size)
                weights.append(jnp.exp(score - one[None]).reshape(rows, size).astype(jnp.bfloat16))
            values = jnp.concatenate(values, axis=1)
            values = jnp.concatenate([values, jnp.ones((16, size), jnp.bfloat16)], axis=0)
            mixed += dot(values, jnp.concatenate(weights, axis=0))
            yield
        mixed_ref[lax.rem(turn, 2), half] = mixed
        yield

    def finish_steps(turn):
        unit, step = turn // pairs, turn % pairs
        for half in range(2):
            result = mixed_ref[lax.rem(turn, 2), half, :HDIM] / mixed_ref[lax.rem(turn, 2), half, HDIM : HDIM + 1]
            twice = jnp.concatenate([result, result], axis=0).T.astype(jnp.bfloat16)
            at = pl.multiple_of((2 * step + half) * rows, rows)
            for i in range(group):
                out_ref[unit * group + i, pl.ds(at, rows), :] = twice[i * rows : (i + 1) * rows, :]
            yield

    def run(*streams):
        for _ in itertools.zip_longest(*streams):
            pass

    mixed_ref[...] = jnp.ones_like(mixed_ref)

    def body(turn, carry):
        run(weight_steps(turn, 0), score_steps(turn, 1), finish_steps(jnp.maximum(turn - 1, 0)))
        run(weight_steps(turn, 1), score_steps(jnp.minimum(turn + 1, turns - 1), 0))
        return carry

    run(score_steps(0, 0))
    lax.fori_loop(0, turns, body, 0)
    run(finish_steps(turns - 1))


def spread_kernel(capacity, first, whole, info_ref, mixed_ref, out_hbm, out_ref, sems):
    visible = mixed_ref.shape[1]
    members = info_ref.shape[0]
    devices = out_ref.shape[0]
    group = SEG // visible
    segments = members // group
    slots = devices * capacity
    lines = visible // 128
    wide = 2 * HDIM
    units = range(mixed_ref.shape[0] // group)
    step = math.gcd(slots, 256)
    low = lax.broadcasted_iota(jnp.int32, (step, wide), 1) < HDIM
    jobs = []
    for u in units:
        segment = u if whole else dealt_unit(segments, first, len(units), u)[1]
        for i in range(group):
            info = info_ref[segment * group + i].astype(jnp.float32)
            place = (info[:lines] * capacity + info[lines : 2 * lines]).astype(jnp.int32)
            place = jnp.concatenate([place[j : j + 1] for j in range(lines)], axis=1)
            jobs.append((u, i, place, mixed_ref[u * group + i]))

    copies = []
    for start in range(0, slots, step):
        found = {}
        for u, i, place, right in jobs:
            wanted = lax.broadcasted_iota(jnp.int32, (step, visible), 0) + start
            found[u, i] = dot(one_hot(wanted, place), right)
        at, last = start // capacity, (start + step) // capacity
        for u in range(0, len(units), 2):
            base = u // 2 * group * capacity
            if u + 1 < len(units):
                pairs = [((u, i), (u + 1, i)) for i in range(group)]
            else:
                pairs = [((u, i), (u, i + group // 2)) for i in range(group // 2)]
            for i, (left, right) in enumerate(pairs):
                both = jnp.where(low, found[left], found[right]).astype(jnp.bfloat16)
                both = both.reshape(step // capacity, capacity, wide)
                out_ref[at:last, base + i * capacity : base + (i + 1) * capacity, :] = both
        copies.append(write(out_ref, out_hbm, at, last - at, sems))
    for copy in copies:
        copy.wait()


def finish_kernel(parts, capacity, slot_ref, rows_hbm, gain_ref, w_hbm, *refs):
    back_refs, refs = refs[: len(parts)], refs[len(parts) :]
    out_hbm, attended_ref, rows_ref, w_ref, answer_ref, out_ref, more, sems = refs
    fetches = [
        pltpu.make_async_copy(w_hbm, w_ref, more.at[0]),
        pltpu.make_async_copy(rows_hbm, rows_ref, more.at[1]),
    ]
    for copy in fetches:
        copy.start()
    slots, count = attended_ref.shape[0], out_ref.shape[0]
    members = len(parts[0][2])
    groups = back_refs[0].shape[0] // members
    segments = 1 + max(segment for _, _, part in parts for _, units in part for _, segment in units)
    group = members // segments
    where = {}
    for back_ref, (_, _, part) in zip(back_refs, parts):
        for member, (heads, units) in enumerate(part):
            for u, (place, segment) in enumerate(units):
                alone = u + 1 == len(units) and u % 2 == 0
                where[heads[place], segment] = back_ref, member, u, alone

    def piece(which, head, source):
        back_ref, member, u, alone = where[head, source // group]
        i, odd = source % group, u % 2
        if alone:
            i, odd = i % (group // 2), i // (group // 2)
        at = u // 2 * group * capacity + i * capacity
        return back_ref[which * members + member, at : at + capacity, :], odd

    for which in range(groups):
        for source in range(members):
            at = (which * members + source) * capacity
            for head in range(0, HEADS, 2):
                pair = piece(which, head, source) + piece(which, head + 1, source)
                attended_ref[at : at + capacity, head * HDIM : (head + 2) * HDIM] = place_pair(*pair)
    for copy in fetches:
        copy.wait()
    step = math.gcd(slots, 256)
    for start in range(0, slots, step):
        at = slice(start, start + step)
        hidden = rows_ref[at, :].astype(jnp.float32) + dot(attended_ref[at, :], w_ref[...])
        answer_ref[at, :] = layer_norm(hidden, gain_ref[...]).astype(jnp.bfloat16)
    step = math.gcd(count, 256)
    copies = []
    for start in range(0, count, step):
        here = lax.broadcasted_iota(jnp.int32, (step, slots), 1)
        chosen = one_hot(column_of(slot_ref[:, start : start + step]), here)
        out_ref[start : start + step, :] = dot(chosen, answer_ref[...]).astype(jnp.bfloat16)
        copies.append(write(out_ref, out_hbm, start, step, sems))
    for copy in copies:
        copy.wait()


IN_VMEM = pl.BlockSpec(memory_space=pltpu.VMEM)
IN_HBM = pl.BlockSpec(memory_space=pltpu.HBM)
IN_SMEM = pl.BlockSpec(memory_space=pltpu.SMEM)
PINNED = pl.BlockSpec(memory_space=pltpu.VMEM)
SPACES = {id(IN_HBM): pltpu.HBM, id(PINNED): pltpu.VMEM}
COPIES = pltpu.SemaphoreType.DMA


def call(kernel, outs, out_specs, name, *operands, in_specs=None, scratch=()):
    in_specs = in_specs or [IN_VMEM] * len(operands)
    operands = [
        pltpu.with_memory_space_constraint(operand, SPACES[id(spec)]) if id(spec) in SPACES else operand
        for operand, spec in zip(operands, in_specs)
    ]
    outs = jax.tree.map(
        lambda out, spec: pltpu.HBM(out.shape, out.dtype) if spec is IN_HBM else out, outs, out_specs
    )
    return pl.pallas_call(
        kernel,
        out_shape=outs,
        in_specs=in_specs,
        out_specs=out_specs,
        scratch_shapes=[one for one in scratch if one is not None],
        compiler_params=pltpu.CompilerParams(vmem_limit_bytes=VMEM),
        name=name,
    )(*operands)


def on_device(tiles, dest_table, owner_row, w_qkv, w_out, gain_attn, gain_out):
    groups = lax.axis_size("group")
    axes = ("group", "high", "low")
    inside = ("high", "low")
    members = lax.axis_size(inside)
    devices = groups * members
    count, width = tiles.shape
    visible = owner_row.shape[1]
    capacity = 2 * visible // devices
    slots = devices * capacity
    rows = visible // CLASSES
    segments = members * visible // SEG
    group = members // segments
    parts = parts_of(members, segments)
    bf16 = jnp.bfloat16

    moves = [(s * groups + g, g * members + s) for g in range(groups) for s in range(members)]
    owners = lax.ppermute(owner_row.reshape(visible // 128, 128), axes, moves).reshape(visible)
    owners = owners.reshape(rows, CLASSES).T.reshape(visible)

    outgoing, send_slot = call(
        functools.partial(pack_kernel, visible, capacity),
        (jax.ShapeDtypeStruct((slots, width), bf16), jax.ShapeDtypeStruct((1, count), jnp.int32)),
        (IN_HBM, IN_VMEM),
        "pack",
        dest_table.reshape(count // 128, 128),
        tiles,
        in_specs=[IN_HBM, IN_HBM],
        scratch=[
            pltpu.VMEM((count // 128, 128), jnp.int32),
            pltpu.VMEM((count, width), bf16),
            pltpu.VMEM((slots, width), bf16),
            COPIES((3,)),
            COPIES((slots // math.gcd(slots, 256),)),
        ],
    )
    arrived = lax.all_to_all(
        outgoing.reshape(devices, capacity, width), axes, split_axis=0, concat_axis=0, tiled=True
    ).reshape(slots, width)

    source = owners // count
    same = source[:, None] == source[None, :]
    earlier = owners[None, :] < owners[:, None]
    placed = jnp.sum((same & earlier).astype(jnp.int32), axis=1)
    slot = source * capacity + placed
    lines = visible // 128
    extra = jnp.concatenate([source.reshape(lines, 128), placed.reshape(lines, 128)])
    extra = jnp.pad(extra, ((0, 16 - 2 * lines), (0, 0))).astype(bf16)
    weights = (w_qkv, w_qkv[:, 2 * width :].T)
    blocks = {}
    sequence = list(range(len(parts)))[::-1]
    for i in sequence:
        part = parts[i]
        first, last, dealt = part
        depth = depth_of(part, visible) + (16 if i == sequence[0] else 0)
        shape = jax.ShapeDtypeStruct((members, depth, 2 * HDIM), bf16)
        size = (last - first) * HDIM
        scratch = [
            pltpu.VMEM((2, width, size), bf16),
            pltpu.VMEM((size, width), bf16),
            pltpu.VMEM(shape.shape, bf16),
            pltpu.VMEM((visible, size), bf16),
            pltpu.VMEM((visible, size), bf16),
            pltpu.VMEM((size, visible), bf16),
            COPIES((members,)),
        ]
        if i == sequence[0]:
            normed, send = call(
                functools.partial(first_kernel, part),
                (jax.ShapeDtypeStruct((visible, width), bf16), shape),
                (IN_HBM,) * 2,
                "project_first",
                slot[None, :],
                extra,
                arrived,
                gain_attn[None, :],
                *weights,
                in_specs=[IN_VMEM] * 4 + [IN_HBM] * 2,
                scratch=scratch + [pltpu.VMEM((visible, width), bf16), COPIES((4,))],
            )
        else:
            send = call(
                functools.partial(next_kernel, part),
                shape,
                IN_HBM,
                "project_next",
                normed,
                *weights,
                in_specs=[IN_VMEM] + [IN_HBM] * 2,
                scratch=scratch + [COPIES((3,))],
            )
        if blocks:
            blocks[before], send = lax.optimization_barrier((blocks[before], send))
        blocks[i] = lax.all_to_all(send, inside, split_axis=0, concat_axis=0, tiled=True)
        before = i

    backs, infos = {}, []
    for i in sequence:
        part = parts[i]
        units = len(part[2][0][1])
        depth = SEG + (segments - 1) * SEG // CLASSES
        outs = [jax.ShapeDtypeStruct((units * group, visible, 2 * HDIM), bf16)]
        staged = i != sequence[-1]
        if i == sequence[0]:
            outs.append(jax.ShapeDtypeStruct((members, 16, 2 * HDIM), bf16))
        operands = [blocks[i]]
        if shares(part):
            partners = [(member, member ^ 1) for member in range(members)]
            operands.append(lax.ppermute(blocks[i], inside, partners))
        mixed, *info = call(
            functools.partial(attend_kernel, visible, part, i < HEADS // members),
            outs,
            [IN_VMEM] * len(outs),
            "attend",
            *operands,
            scratch=[
                pltpu.VMEM((2, depth, SEG // CLASSES), jnp.float32),
                pltpu.VMEM((2, 8, SEG // CLASSES), jnp.float32),
                pltpu.VMEM((2, 2, HDIM + 16, SEG // CLASSES), jnp.float32),
                pltpu.VMEM((members, visible + visible // 2, 2 * HDIM), bf16) if shares(part) else None,
            ],
        )
        infos += info
        shape = jax.ShapeDtypeStruct((devices, units * group * capacity // 2, 2 * HDIM), bf16)
        answers = call(
            functools.partial(spread_kernel, capacity, part[0], i < HEADS // members),
            shape,
            IN_HBM,
            "spread",
            infos[0],
            mixed,
            scratch=[pltpu.VMEM(shape.shape, bf16), COPIES((slots // math.gcd(slots, 256),))],
        )
        if staged:
            after = sequence[sequence.index(i) + 1]
            blocks[after], answers, infos[0] = lax.optimization_barrier((blocks[after], answers, infos[0]))
        backs[i] = lax.all_to_all(answers, axes, split_axis=0, concat_axis=0, tiled=True)
    backs = [backs[i] for i in range(len(parts))]

    return call(
        functools.partial(finish_kernel, parts, capacity),
        jax.ShapeDtypeStruct((count, width), bf16),
        IN_HBM,
        "finish",
        send_slot,
        outgoing,
        gain_out[None, :],
        w_out,
        *backs,
        in_specs=[IN_VMEM, IN_HBM, IN_VMEM, IN_HBM] + [IN_VMEM] * len(backs),
        scratch=[
            pltpu.VMEM((slots, width), bf16),
            pltpu.VMEM((slots, width), bf16),
            pltpu.VMEM((width, width), bf16),
            pltpu.VMEM((slots, width), bf16),
            pltpu.VMEM((count, width), bf16),
            COPIES((2,)),
            COPIES((count // math.gcd(count, 256),)),
        ],
    )


def solution(mesh):
    n_seq, n_slide = mesh.shape["seq"], mesh.shape["slide"]
    split = Mesh(
        mesh.devices.reshape(n_slide, n_seq // n_slide, n_slide), ("group", "high", "low")
    )
    every = ("group", "high", "low")
    in_specs = (P(every, None), P(every), P("low", ("group", "high")), P(), P(), P(), P())
    return jax.shard_map(
        on_device, mesh=split, in_specs=in_specs, out_specs=P(every, None), check_vma=False
    )
```

```python
import functools
import itertools
import math

import jax
import jax.numpy as jnp
from jax import lax
from jax.experimental import pallas as pl
from jax.experimental.pallas import tpu as pltpu
from jax.sharding import Mesh
from jax.sharding import PartitionSpec as P

HEADS = 12
HDIM = 64
SEG = 2048
CLASSES = 8
EPS = 1e-05
VMEM = 24 << 20


def layer_norm(inputs, gain):
    average = jnp.mean(inputs, axis=-1, keepdims=True)
    centred = inputs - average
    spread = jnp.mean(centred * centred, axis=-1, keepdims=True)
    return centred * lax.rsqrt(spread + EPS) * gain


def one_hot(left, right):
    return jnp.where(left == right, 1.0, 0.0).astype(jnp.bfloat16)


def dot(left, right):
    return jnp.dot(left, right, preferred_element_type=jnp.float32)


def parts_of(members, segments):
    full = HEADS // members
    every = [(0, segment) for segment in range(segments)]
    parts = [
        (i * members, (i + 1) * members, [([i * members + member], every) for member in range(members)])
        for i in range(full)
    ]
    first = full * members
    owned = (HEADS - first) * segments // members
    if owned:
        dealt = []
        for member in range(members):
            units = [divmod(first * segments + member * owned + i, segments) for i in range(owned)]
            dealt.append((sorted({head for head, _ in units}), units))
        width = max(len(heads) for heads, _ in dealt)
        part = []
        for heads, units in dealt:
            units = [(heads.index(head), segment) for head, segment in units]
            part.append((heads + heads[-1:] * (width - len(heads)), units))
        parts.append((first, HEADS, part))
    return parts


def shares(part):
    held = [heads for heads, _ in part[2]]
    return len(held[0]) == 1 and len(held) % 2 == 0 and held[::2] == held[1::2]


def depth_of(part, visible):
    depth = len(part[2][0][0]) * visible + visible // 2
    return depth // 2 if shares(part) else depth


def place_pair(left, left_odd, right, right_odd):
    left = swap(left) if left_odd else left
    right = right if right_odd else swap(right)
    lanes = lax.broadcasted_iota(jnp.int32, left.shape, 1)
    return jnp.where(lanes < HDIM, left, right)


def swap(tile):
    return jnp.concatenate([tile[:, HDIM:], tile[:, :HDIM]], axis=1)


def column_of(row):
    pieces = [row[:, at : at + 128].astype(jnp.float32) for at in range(0, row.shape[1], 128)]
    pieces = [jnp.broadcast_to(piece, (8, 128)).T[:, :1] for piece in pieces]
    return jnp.concatenate(pieces, axis=0).astype(jnp.int32)


def member_index():
    return lax.axis_index("high") * lax.axis_size("low") + lax.axis_index("low")


def dealt_unit(segments, first, owned, i):
    start = member_index() * owned
    segment = lax.rem(start + i, segments)
    return lax.div(start + i, segments) - lax.div(start, segments), segment


def dot_nt(left, right):
    return lax.dot_general(left, right, (((1,), (1,)), ((), ())), preferred_element_type=jnp.float32)


def pack_kernel(visible, capacity, dest_hbm, tiles_hbm, out_hbm, slot_ref, dest_ref, tiles_ref, out_ref, more, sems):
    width = tiles_ref.shape[1]
    spans = [(0, width // 3), (width // 3, width)]
    table = pltpu.make_async_copy(dest_hbm, dest_ref, more.at[0])
    fetches = [
        pltpu.make_async_copy(
            tiles_hbm.at[:, pl.ds(low, high - low)], tiles_ref.at[:, pl.ds(low, high - low)], more.at[1 + i]
        )
        for i, (low, high) in enumerate(spans)
    ]
    for copy in [table, *fetches]:
        copy.start()
    slots, _ = out_ref.shape
    count = dest_ref.shape[0] * 128
    devices = slots // capacity
    table.wait()
    target = jnp.right_shift(dest_ref[...], visible.bit_length() - 1)
    lanes = 128
    before = one_hot_lt(lanes)
    offset = jnp.zeros((devices, 1), jnp.float32)
    pieces = []
    for start in range(0, count, lanes):
        here = target[start // lanes : start // lanes + 1, :]
        device = lax.broadcasted_iota(jnp.int32, (devices, lanes), 0)
        chosen = jnp.where(device == here, 1.0, 0.0)
        rank = dot(chosen.astype(jnp.bfloat16), before) + offset
        placed = jnp.sum(chosen * rank, axis=0, keepdims=True).astype(jnp.int32)
        pieces.append(jnp.where(here >= 0, here * capacity + placed, -1))
        offset = offset + jnp.sum(chosen, axis=1, keepdims=True)
    slot = jnp.concatenate(pieces, axis=1)
    slot_ref[...] = slot
    step = math.gcd(slots, 256)
    copies = []
    for fetch, (low, high) in zip(fetches, spans):
        fetch.wait()
        for start in range(0, slots, step):
            wanted = lax.broadcasted_iota(jnp.int32, (step, count), 0) + start
            rows = dot(one_hot(wanted, slot), tiles_ref[:, low:high])
            out_ref[start : start + step, low:high] = rows.astype(jnp.bfloat16)
            if high == width:
                copies.append(write(out_ref, out_hbm, start, step, sems))
    for copy in copies:
        copy.wait()


def write(source, target, start, step, sems):
    at = pl.ds(start, step)
    copy = pltpu.make_async_copy(source.at[at], target.at[at], sems.at[start // step])
    copy.start()
    return copy


def one_hot_lt(size):
    row = lax.broadcasted_iota(jnp.int32, (size, size), 0)
    column = lax.broadcasted_iota(jnp.int32, (size, size), 1)
    return jnp.where(row < column, 1.0, 0.0).astype(jnp.bfloat16)


def project_part(part, normed, extra, w_ref, wvt_ref, send_hbm, send_ref, q_ref, k_ref, vt_ref, sems):
    first, last, members = part
    visible, width = normed.shape
    rows, middle = visible // CLASSES, visible // 2
    wide = 2 * HDIM
    q_ref[...] = (dot(normed, w_ref[0]) * HDIM ** (-0.5)).astype(jnp.bfloat16)
    k_ref[...] = dot(normed, w_ref[1]).astype(jnp.bfloat16)
    vt_ref[...] = dot_nt(wvt_ref[...], normed).astype(jnp.bfloat16)

    def queries_of(head, cls):
        at = (head - first) // 2 * wide
        pair = [q_ref[(cls + i) * rows : (cls + i + 1) * rows, at : at + wide] for i in range(2)]
        return place_pair(pair[0], head % 2, pair[1], head % 2)

    for head in range(first, last):
        at, odd = (head - first) // 2 * wide, head % 2
        keys = place_pair(k_ref[:middle, at : at + wide], odd, k_ref[middle:, at : at + wide], odd)
        values = vt_ref[(head - first) * HDIM : (head - first + 1) * HDIM, :]
        for member, (heads, _) in enumerate(members):
            for place in [place for place, one in enumerate(heads) if one == head]:
                base = place * visible
                if not shares(part) or member % 2 == 0:
                    send_ref[member, base : base + middle, :] = keys
                if not shares(part) or member % 2 == 1:
                    base += 0 if shares(part) else middle
                    for i in range(visible // wide):
                        top = base + i * HDIM
                        send_ref[member, top : top + HDIM, :] = values[:, i * wide : (i + 1) * wide]
    copies = []
    for member, (heads, units) in enumerate(members):
        base, steps = len(heads) * visible, range(CLASSES // 2)
        if shares(part):
            steps = steps[member % 2 * CLASSES // 4 : (member % 2 + 1) * CLASSES // 4]
            base = middle - steps[0] * rows
        for i in steps:
            tile = queries_of(heads[0], 2 * i)
            for place, head in enumerate(heads[1:], 1):
                segment = lax.div(member_index(), SEG // visible)
                mine = functools.reduce(
                    jnp.logical_or, [segment == one for at, one in units if at == place], False
                )
                if head != heads[0]:
                    tile = jnp.where(mine, queries_of(head, 2 * i), tile)
            send_ref[member, base + i * rows : base + (i + 1) * rows, :] = tile
        if extra is not None:
            send_ref[member, depth_of(part, visible) :, :] = extra
        copies.append(write(send_ref, send_hbm, member, 1, sems))
    return copies


def fetch_weights(part, w_hbm, wvt_hbm, w_ref, wvt_ref, sems):
    width = w_hbm.shape[0]
    at, size = part[0] * HDIM, (part[1] - part[0]) * HDIM
    copies = [
        pltpu.make_async_copy(w_hbm.at[:, pl.ds(i * width + at, size)], w_ref.at[i], sems.at[i])
        for i in range(2)
    ]
    copies.append(pltpu.make_async_copy(wvt_hbm.at[pl.ds(at, size)], wvt_ref, sems.at[2]))
    for copy in copies:
        copy.start()
    return copies


def first_kernel(part, slot_ref, extra_ref, arrived_ref, gain_ref, w_hbm, wvt_hbm, normed_hbm, send_hbm,
                 w_ref, wvt_ref, send_ref, q_ref, k_ref, vt_ref, sems, normed_ref, more):
    weights = fetch_weights(part, w_hbm, wvt_hbm, w_ref, wvt_ref, more)
    visible, slots = normed_ref.shape[0], arrived_ref.shape[0]
    chosen = one_hot(lax.broadcasted_iota(jnp.int32, (visible, slots), 1), column_of(slot_ref[...]))
    rows = dot(chosen, arrived_ref[...])
    normed = layer_norm(rows, gain_ref[...]).astype(jnp.bfloat16)
    normed_ref[...] = normed
    copies = [pltpu.make_async_copy(normed_ref, normed_hbm, more.at[3])]
    for copy in copies:
        copy.start()
    for copy in weights:
        copy.wait()
    copies += project_part(
        part, normed, extra_ref[...], w_ref, wvt_ref, send_hbm, send_ref, q_ref, k_ref, vt_ref, sems
    )
    for copy in copies:
        copy.wait()


def next_kernel(part, normed_ref, w_hbm, wvt_hbm, send_hbm, w_ref, wvt_ref, send_ref, q_ref, k_ref, vt_ref, sems, more):
    for copy in fetch_weights(part, w_hbm, wvt_hbm, w_ref, wvt_ref, more):
        copy.wait()
    copies = project_part(
        part, normed_ref[...], None, w_ref, wvt_ref, send_hbm, send_ref, q_ref, k_ref, vt_ref, sems
    )
    for copy in copies:
        copy.wait()


def attend_kernel(visible, part, whole, *refs):
    first, heads = part[0], len(part[2][0][0])
    block_ref, *refs = refs
    if shares(part):
        other_ref, *refs = refs
    out_ref, *refs = refs
    full_ref, own_ref = block_ref, block_ref
    if shares(part):
        *refs, full_ref = refs
    *infos, score_ref, peak_ref, mixed_ref = refs
    for info_ref in infos:
        info_ref[...] = own_ref[:, depth_of(part, visible) :, :]
    if shares(part):
        odd_member = lax.rem(member_index(), 2)
        half, quarter = visible // 2, visible // 4
        for odd, (even_ref, odd_ref) in enumerate(((own_ref, other_ref), (other_ref, own_ref))):

            @pl.when(odd_member == odd)
            def _():
                full_ref[:, :half, :] = even_ref[:, :half, :]
                full_ref[:, half:visible, :] = odd_ref[:, :half, :]
                full_ref[:, visible : visible + quarter, :] = even_ref[:, half : half + quarter, :]
                full_ref[:, visible + quarter :, :] = odd_ref[:, half : half + quarter, :]

    block_ref = full_ref
    members = block_ref.shape[0]
    rows, middle = visible // CLASSES, visible // 2
    group = SEG // visible
    segments = members // group
    wide = 2 * HDIM
    size = group * rows
    pairs = CLASSES // 2
    turns = out_ref.shape[0] // group * pairs
    low = lax.broadcasted_iota(jnp.int32, (size, wide), 1) < HDIM

    def tile_of(turn, half):
        unit, step = turn // pairs, turn % pairs
        place, segment = (0, unit) if whole else dealt_unit(segments, first, turns // pairs, unit)
        return step, segment, 2 * step + half, pl.multiple_of(place * visible, visible)

    def member_of(segment, i, apart):
        return lax.rem(segment + apart, segments) * group + i

    def blocks_of(segment):
        near = [(member_of(segment, i, 0), side) for i in range(group) for side in range(2)]
        return near + [(apart, None) for apart in range(1, segments)]

    def score_steps(turn, half):
        step, segment, cls, base = tile_of(turn, half)
        top = pl.multiple_of(heads * visible + step * rows, rows)
        queries = jnp.concatenate(
            [block_ref[member_of(segment, i, 0), pl.ds(top, rows), :] for i in range(group)], axis=0
        )
        turned = swap(queries)
        none = jnp.zeros_like(queries)
        left = jnp.where(low, turned if half else queries, none)
        right = jnp.where(low, none, queries if half else turned)
        far = jnp.where(cls >= CLASSES // 2, right, left)
        peak = None
        for j, (member, side) in enumerate(blocks_of(segment)):
            if side is None:
                at = pl.multiple_of(base + jnp.bitwise_and(cls, CLASSES // 2 - 1) * rows, rows)
                keys = [block_ref[member_of(segment, i, member), pl.ds(at, rows), :] for i in range(group)]
                score = dot_nt(jnp.concatenate(keys, axis=0), far)
            else:
                score = dot_nt(block_ref[member, pl.ds(base, middle), :], right if side else left)
            score_ref[half, j * size : (j + 1) * size, :] = score
            highest = jnp.max(score.reshape(size // 8, 8, size), axis=0)
            peak = highest if peak is None else jnp.maximum(peak, highest)
            yield
        peak_ref[half] = jnp.broadcast_to(jnp.max(peak, axis=0, keepdims=True), peak.shape)
        yield

    def weight_steps(turn, half):
        step, segment, cls, base = tile_of(turn, half)
        peak = peak_ref[half]
        odd = jnp.bitwise_and(cls, 1) == 1
        mixed = jnp.zeros((HDIM + 16, size), jnp.float32)
        for j, (member, side) in enumerate(blocks_of(segment)):
            values = []
            if side is None:
                at = pl.multiple_of(base + middle + jnp.right_shift(cls, 1) * HDIM, HDIM)
                for i in range(group):
                    tile = block_ref[member_of(segment, i, member), pl.ds(at, HDIM), :]
                    values.append(jnp.where(odd, swap(tile), tile)[:, :HDIM])
                shifted = [peak] * group
            else:
                count = visible // wide // 2
                for i in range(count):
                    at = pl.multiple_of(base + middle + (side * count + i) * HDIM, HDIM)
                    values.append(block_ref[member, pl.ds(at, HDIM), :])
                shifted = []
                for other in range(side * 4, side * 4 + 4):
                    apart = jnp.bitwise_and(other - cls, CLASSES - 1)
                    offset = jnp.where(jnp.bitwise_and(apart, 1) == 0, math.log(2.0), 0.0)
                    offset = jnp.where(apart == 4, math.log(3.0), offset)
                    shifted.append(peak - jnp.where(apart == 0, math.log(4.0), offset))
            weights = []
            for i, one in enumerate(shifted):
                at = j * size + i * rows
                score = score_ref[half, at : at + rows, :].reshape(rows // 8, 8, size)
                weights.append(jnp.exp(score - one[None]).reshape(rows, size).astype(jnp.bfloat16))
            values = jnp.concatenate(values, axis=1)
            values = jnp.concatenate([values, jnp.ones((16, size), jnp.bfloat16)], axis=0)
            mixed += dot(values, jnp.concatenate(weights, axis=0))
            yield
        mixed_ref[lax.rem(turn, 2), half] = mixed
        yield

    def finish_steps(turn):
        unit, step = turn // pairs, turn % pairs
        for half in range(2):
            result = mixed_ref[lax.rem(turn, 2), half, :HDIM] / mixed_ref[lax.rem(turn, 2), half, HDIM : HDIM + 1]
            twice = jnp.concatenate([result, result], axis=0).T.astype(jnp.bfloat16)
            at = pl.multiple_of((2 * step + half) * rows, rows)
            for i in range(group):
                out_ref[unit * group + i, pl.ds(at, rows), :] = twice[i * rows : (i + 1) * rows, :]
            yield

    def run(*streams):
        for _ in itertools.zip_longest(*streams):
            pass

    mixed_ref[...] = jnp.ones_like(mixed_ref)

    def body(turn, carry):
        run(weight_steps(turn, 0), score_steps(turn, 1), finish_steps(jnp.maximum(turn - 1, 0)))
        run(weight_steps(turn, 1), score_steps(jnp.minimum(turn + 1, turns - 1), 0))
        return carry

    run(score_steps(0, 0))
    lax.fori_loop(0, turns, body, 0)
    run(finish_steps(turns - 1))


def spread_kernel(capacity, first, whole, info_ref, mixed_ref, out_hbm, out_ref, sems):
    visible = mixed_ref.shape[1]
    members = info_ref.shape[0]
    devices = out_ref.shape[0]
    group = SEG // visible
    segments = members // group
    slots = devices * capacity
    lines = visible // 128
    wide = 2 * HDIM
    units = range(mixed_ref.shape[0] // group)
    step = math.gcd(slots, 256)
    low = lax.broadcasted_iota(jnp.int32, (step, wide), 1) < HDIM
    jobs = []
    for u in units:
        segment = u if whole else dealt_unit(segments, first, len(units), u)[1]
        for i in range(group):
            info = info_ref[segment * group + i].astype(jnp.float32)
            place = (info[:lines] * capacity + info[lines : 2 * lines]).astype(jnp.int32)
            place = jnp.concatenate([place[j : j + 1] for j in range(lines)], axis=1)
            jobs.append((u, i, place, mixed_ref[u * group + i]))

    copies = []
    for start in range(0, slots, step):
        found = {}
        for u, i, place, right in jobs:
            wanted = lax.broadcasted_iota(jnp.int32, (step, visible), 0) + start
            found[u, i] = dot(one_hot(wanted, place), right)
        at, last = start // capacity, (start + step) // capacity
        for u in range(0, len(units), 2):
            base = u // 2 * group * capacity
            if u + 1 < len(units):
                pairs = [((u, i), (u + 1, i)) for i in range(group)]
            else:
                pairs = [((u, i), (u, i + group // 2)) for i in range(group // 2)]
            for i, (left, right) in enumerate(pairs):
                both = jnp.where(low, found[left], found[right]).astype(jnp.bfloat16)
                both = both.reshape(step // capacity, capacity, wide)
                out_ref[at:last, base + i * capacity : base + (i + 1) * capacity, :] = both
        copies.append(write(out_ref, out_hbm, at, last - at, sems))
    for copy in copies:
        copy.wait()


def finish_kernel(parts, capacity, slot_ref, rows_hbm, gain_ref, w_ref, *refs):
    back_refs, refs = refs[: len(parts)], refs[len(parts) :]
    out_hbm, attended_ref, rows_ref, answer_ref, out_ref, more, sems = refs
    fetches = [
        pltpu.make_async_copy(rows_hbm, rows_ref, more.at[0]),
    ]
    for copy in fetches:
        copy.start()
    slots, count = attended_ref.shape[0], out_ref.shape[0]
    members = len(parts[0][2])
    groups = back_refs[0].shape[0] // members
    segments = 1 + max(segment for _, _, part in parts for _, units in part for _, segment in units)
    group = members // segments
    where = {}
    for back_ref, (_, _, part) in zip(back_refs, parts):
        for member, (heads, units) in enumerate(part):
            for u, (place, segment) in enumerate(units):
                alone = u + 1 == len(units) and u % 2 == 0
                where[heads[place], segment] = back_ref, member, u, alone

    def piece(which, head, source):
        back_ref, member, u, alone = where[head, source // group]
        i, odd = source % group, u % 2
        if alone:
            i, odd = i % (group // 2), i // (group // 2)
        at = u // 2 * group * capacity + i * capacity
        return back_ref[which * members + member, at : at + capacity, :], odd

    for which in range(groups):
        for source in range(members):
            at = (which * members + source) * capacity
            for head in range(0, HEADS, 2):
                pair = piece(which, head, source) + piece(which, head + 1, source)
                attended_ref[at : at + capacity, head * HDIM : (head + 2) * HDIM] = place_pair(*pair)
    for copy in fetches:
        copy.wait()
    step = math.gcd(slots, 256)
    for start in range(0, slots, step):
        at = slice(start, start + step)
        hidden = rows_ref[at, :].astype(jnp.float32) + dot(attended_ref[at, :], w_ref[...])
        answer_ref[at, :] = layer_norm(hidden, gain_ref[...]).astype(jnp.bfloat16)
    step = math.gcd(count, 256)
    copies = []
    for start in range(0, count, step):
        here = lax.broadcasted_iota(jnp.int32, (step, slots), 1)
        chosen = one_hot(column_of(slot_ref[:, start : start + step]), here)
        out_ref[start : start + step, :] = dot(chosen, answer_ref[...]).astype(jnp.bfloat16)
        copies.append(write(out_ref, out_hbm, start, step, sems))
    for copy in copies:
        copy.wait()


IN_VMEM = pl.BlockSpec(memory_space=pltpu.VMEM)
IN_HBM = pl.BlockSpec(memory_space=pltpu.HBM)
IN_SMEM = pl.BlockSpec(memory_space=pltpu.SMEM)
PINNED = pl.BlockSpec(memory_space=pltpu.VMEM)
SPACES = {id(IN_HBM): pltpu.HBM, id(PINNED): pltpu.VMEM}
COPIES = pltpu.SemaphoreType.DMA


def call(kernel, outs, out_specs, name, *operands, in_specs=None, scratch=()):
    in_specs = in_specs or [IN_VMEM] * len(operands)
    operands = [
        pltpu.with_memory_space_constraint(operand, SPACES[id(spec)]) if id(spec) in SPACES else operand
        for operand, spec in zip(operands, in_specs)
    ]
    outs = jax.tree.map(
        lambda out, spec: pltpu.HBM(out.shape, out.dtype) if spec is IN_HBM else out, outs, out_specs
    )
    return pl.pallas_call(
        kernel,
        out_shape=outs,
        in_specs=in_specs,
        out_specs=out_specs,
        scratch_shapes=[one for one in scratch if one is not None],
        compiler_params=pltpu.CompilerParams(vmem_limit_bytes=VMEM),
        name=name,
    )(*operands)


def on_device(tiles, dest_table, owner_row, w_qkv, w_out, gain_attn, gain_out):
    groups = lax.axis_size("group")
    axes = ("group", "high", "low")
    inside = ("high", "low")
    members = lax.axis_size(inside)
    devices = groups * members
    count, width = tiles.shape
    visible = owner_row.shape[1]
    capacity = 2 * visible // devices
    slots = devices * capacity
    rows = visible // CLASSES
    segments = members * visible // SEG
    group = members // segments
    parts = parts_of(members, segments)
    bf16 = jnp.bfloat16

    moves = [(s * groups + g, g * members + s) for g in range(groups) for s in range(members)]
    owners = lax.ppermute(owner_row.reshape(visible // 128, 128), axes, moves).reshape(visible)
    owners = owners.reshape(rows, CLASSES).T.reshape(visible)

    outgoing, send_slot = call(
        functools.partial(pack_kernel, visible, capacity),
        (jax.ShapeDtypeStruct((slots, width), bf16), jax.ShapeDtypeStruct((1, count), jnp.int32)),
        (IN_HBM, IN_VMEM),
        "pack",
        dest_table.reshape(count // 128, 128),
        tiles,
        in_specs=[IN_HBM, IN_HBM],
        scratch=[
            pltpu.VMEM((count // 128, 128), jnp.int32),
            pltpu.VMEM((count, width), bf16),
            pltpu.VMEM((slots, width), bf16),
            COPIES((3,)),
            COPIES((slots // math.gcd(slots, 256),)),
        ],
    )
    arrived = lax.all_to_all(
        outgoing.reshape(devices, capacity, width), axes, split_axis=0, concat_axis=0, tiled=True
    ).reshape(slots, width)

    source = owners // count
    same = source[:, None] == source[None, :]
    earlier = owners[None, :] < owners[:, None]
    placed = jnp.sum((same & earlier).astype(jnp.int32), axis=1)
    slot = source * capacity + placed
    lines = visible // 128
    extra = jnp.concatenate([source.reshape(lines, 128), placed.reshape(lines, 128)])
    extra = jnp.pad(extra, ((0, 16 - 2 * lines), (0, 0))).astype(bf16)
    weights = (w_qkv, w_qkv[:, 2 * width :].T)
    blocks = {}
    sequence = list(range(len(parts)))[::-1]
    for i in sequence:
        part = parts[i]
        first, last, dealt = part
        depth = depth_of(part, visible) + (16 if i == sequence[0] else 0)
        shape = jax.ShapeDtypeStruct((members, depth, 2 * HDIM), bf16)
        size = (last - first) * HDIM
        scratch = [
            pltpu.VMEM((2, width, size), bf16),
            pltpu.VMEM((size, width), bf16),
            pltpu.VMEM(shape.shape, bf16),
            pltpu.VMEM((visible, size), bf16),
            pltpu.VMEM((visible, size), bf16),
            pltpu.VMEM((size, visible), bf16),
            COPIES((members,)),
        ]
        if i == sequence[0]:
            normed, send = call(
                functools.partial(first_kernel, part),
                (jax.ShapeDtypeStruct((visible, width), bf16), shape),
                (IN_HBM,) * 2,
                "project_first",
                slot[None, :],
                extra,
                arrived,
                gain_attn[None, :],
                *weights,
                in_specs=[IN_VMEM] * 4 + [IN_HBM] * 2,
                scratch=scratch + [pltpu.VMEM((visible, width), bf16), COPIES((4,))],
            )
        else:
            send = call(
                functools.partial(next_kernel, part),
                shape,
                IN_HBM,
                "project_next",
                normed,
                *weights,
                in_specs=[IN_VMEM] + [IN_HBM] * 2,
                scratch=scratch + [COPIES((3,))],
            )
        if blocks:
            blocks[before], send = lax.optimization_barrier((blocks[before], send))
        blocks[i] = lax.all_to_all(send, inside, split_axis=0, concat_axis=0, tiled=True)
        before = i

    backs, infos = {}, []
    for i in sequence:
        part = parts[i]
        units = len(part[2][0][1])
        depth = SEG + (segments - 1) * SEG // CLASSES
        outs = [jax.ShapeDtypeStruct((units * group, visible, 2 * HDIM), bf16)]
        staged = i != sequence[-1]
        if i == sequence[0]:
            outs.append(jax.ShapeDtypeStruct((members, 16, 2 * HDIM), bf16))
        operands = [blocks[i]]
        if shares(part):
            partners = [(member, member ^ 1) for member in range(members)]
            operands.append(lax.ppermute(blocks[i], inside, partners))
        mixed, *info = call(
            functools.partial(attend_kernel, visible, part, i < HEADS // members),
            outs,
            [IN_VMEM] * len(outs),
            "attend",
            *operands,
            scratch=[
                pltpu.VMEM((2, depth, SEG // CLASSES), jnp.float32),
                pltpu.VMEM((2, 8, SEG // CLASSES), jnp.float32),
                pltpu.VMEM((2, 2, HDIM + 16, SEG // CLASSES), jnp.float32),
                pltpu.VMEM((members, visible + visible // 2, 2 * HDIM), bf16) if shares(part) else None,
            ],
        )
        infos += info
        shape = jax.ShapeDtypeStruct((devices, units * group * capacity // 2, 2 * HDIM), bf16)
        answers = call(
            functools.partial(spread_kernel, capacity, part[0], i < HEADS // members),
            shape,
            IN_HBM,
            "spread",
            infos[0],
            mixed,
            scratch=[pltpu.VMEM(shape.shape, bf16), COPIES((slots // math.gcd(slots, 256),))],
        )
        if staged:
            after = sequence[sequence.index(i) + 1]
            blocks[after], answers, infos[0] = lax.optimization_barrier((blocks[after], answers, infos[0]))
        backs[i] = lax.all_to_all(answers, axes, split_axis=0, concat_axis=0, tiled=True)
    backs = [backs[i] for i in range(len(parts))]

    return call(
        functools.partial(finish_kernel, parts, capacity),
        jax.ShapeDtypeStruct((count, width), bf16),
        IN_HBM,
        "finish",
        send_slot,
        outgoing,
        gain_out[None, :],
        w_out,
        *backs,
        in_specs=[IN_VMEM, IN_HBM, IN_VMEM, PINNED] + [IN_VMEM] * len(backs),
        scratch=[
            pltpu.VMEM((slots, width), bf16),
            pltpu.VMEM((slots, width), bf16),
            pltpu.VMEM((slots, width), bf16),
            pltpu.VMEM((count, width), bf16),
            COPIES((1,)),
            COPIES((count // math.gcd(count, 256),)),
        ],
    )


def solution(mesh):
    n_seq, n_slide = mesh.shape["seq"], mesh.shape["slide"]
    split = Mesh(
        mesh.devices.reshape(n_slide, n_seq // n_slide, n_slide), ("group", "high", "low")
    )
    every = ("group", "high", "low")
    in_specs = (P(every, None), P(every), P("low", ("group", "high")), P(), P(), P(), P())
    return jax.shard_map(
        on_device, mesh=split, in_specs=in_specs, out_specs=P(every, None), check_vma=False
    )
```
